32 devices in a mesh: section: 2 (over x), space: 16 (over z, y, core).
Axes of the slice: x: 2, y: 2, z: 4, core: 2. Of those that a mesh axis runs over, the one named last changes fastest.
Arguments:
- input_tiles: bfloat16 [16, 2, 4, 8, 8, 256], P('space'), may hold values from -6 to 6
- saved_tiles: bfloat16 [16, 2, 32, 4, 4, 128], P('space'), may hold values from -6 to 6
- out_grad_tiles: bfloat16 [16, 2, 64, 2, 2, 64], P('space'), may hold values from -1 to 1
- kernel_first: bfloat16 [32, 4, 3, 3, 3], replicated, may hold values from -0.625 to 0.625
- bias_first: float32 [32], replicated, may hold values from -3 to 3
- kernel_second: bfloat16 [64, 32, 3, 3, 3], replicated, may hold values from -0.21875 to 0.21875
- bias_second: float32 [64], replicated, may hold values from -3 to 3
Outputs:
- grad_kernel_first: float32 [32, 4, 3, 3, 3], replicated
- grad_bias_first: float32 [32], replicated
- grad_kernel_second: float32 [64, 32, 3, 3, 3], replicated
- grad_bias_second: float32 [64], replicated
The draws below stay inside these ranges and needn't reach their ends.
All inputs are finite; a program needn't handle non-finite values.
Results may differ from the reference program's by a relative error of at most 0.0031.
Values may be sent and summed in bfloat16 or wider, within the bound.
No kernel may reach another device: no remote copies, remote signals or barrier semaphores. Data moves between devices by JAX's collectives and lax.ppermute only.
A program may use at most 128 MiB of HBM per device.

```python
import jax
import jax.numpy as jnp
from jax import lax

C0 = 4
C1 = 32
C2 = 64
TILE = 8
XLEN = 256
MB = 2
GY = 8
TILES = 16
N_SPACE = 16


def level_of(stream_key, shape, split, smallest, largest):
    loudness = 1.0
    for axis_at, blocks in split:
        draws = jax.random.uniform(jax.random.fold_in(jax.random.fold_in(stream_key, 6), axis_at), (blocks,), jnp.float32, smallest / len(split), largest / len(split))
        loudness = loudness * jnp.repeat(jnp.exp(draws), shape[axis_at] // blocks).reshape((-1,) + (1,) * (len(shape) - 1 - axis_at))
    return loudness


def bell_draw(rng, shape, scale, most, split=(), held_as=jnp.bfloat16):
    entries = scale * jax.random.normal(rng, shape, jnp.float32)
    if split:
        entries = entries * level_of(rng, shape, split, -0.22, 0.18)
    return jnp.clip(entries, -most, most).astype(held_as)


def setup_inputs(seed: int = 0) -> dict:
    splits = jax.random.split(jax.random.key(seed), 8)
    input_tiles = bell_draw(splits[0], (TILES, MB, C0, TILE, TILE, XLEN), 1.0, 6.0, ((0, 16),))
    saved_tiles = bell_draw(splits[1], (TILES, MB, C1, TILE // 2, TILE // 2, XLEN // 2), 1.0, 6.0, ((0, 16),))
    out_grad_tiles = bell_draw(splits[2], (TILES, MB, C2, TILE // 4, TILE // 4, XLEN // 4), 0.15, 1.0, ((0, 16),))
    kernel_first = bell_draw(splits[3], (C1, C0, 3, 3, 3), (C0 * 27) ** -0.5, 0.625)
    bias_first = bell_draw(splits[4], (C1,), 0.5, 3.0, (), jnp.float32)
    kernel_second = bell_draw(splits[5], (C2, C1, 3, 3, 3), (C1 * 27) ** -0.5, 0.21875)
    bias_second = bell_draw(splits[6], (C2,), 0.5, 3.0, (), jnp.float32)
    return dict(input_tiles=input_tiles, saved_tiles=saved_tiles, out_grad_tiles=out_grad_tiles, kernel_first=kernel_first, bias_first=bias_first, kernel_second=kernel_second, bias_second=bias_second)


def to_volume(tiles):
    grid_z = N_SPACE // GY
    count, batch, channels, side_y, side_z, depth = tiles.shape
    volume = tiles.reshape(GY, grid_z, batch, channels, side_y, side_z, depth)
    volume = jnp.transpose(volume, (2, 3, 0, 4, 1, 5, 6))
    return volume.reshape(batch, channels, GY * side_y, grid_z * side_z, depth)

def pad_all(field):
    return jnp.pad(field, ((0, 0), (0, 0), (1, 1), (1, 1), (1, 1)))

def correlate(padded, kernel):
    return lax.conv_general_dilated(padded, kernel, (1, 1, 1), 'VALID', dimension_numbers=('NCDHW', 'OIDHW', 'NCDHW'), precision=lax.Precision.HIGHEST)

def kernel_grad(padded, grads):
    result = lax.conv_general_dilated(padded, grads, (1, 1, 1), 'VALID', dimension_numbers=('CNDHW', 'IODHW', 'NCDHW'), precision=lax.Precision.HIGHEST)
    return jnp.transpose(result, (1, 0, 2, 3, 4))

def flipped(kernel):
    return jnp.transpose(kernel[:, :, ::-1, ::-1, ::-1], (1, 0, 2, 3, 4))

def spread_up(grad):
    batch, channels, rows_y, rows_z, rows_x = grad.shape
    value = grad.astype(jnp.float32) * 0.125
    value = jnp.broadcast_to(value[:, :, :, None, :, None, :, None], (batch, channels, rows_y, 2, rows_z, 2, rows_x, 2))
    return value.reshape(batch, channels, 2 * rows_y, 2 * rows_z, 2 * rows_x)

def slope(pre):
    return jnp.where(pre > 0, 1.0, 0.3)

def reference(input_tiles, saved_tiles, out_grad_tiles, kernel_first, bias_first, kernel_second, bias_second):
    first_vol = to_volume(input_tiles)
    second_vol = to_volume(saved_tiles)
    cot_vol = to_volume(out_grad_tiles)
    kernel_one = kernel_first.astype(jnp.float32)
    kernel_two = kernel_second.astype(jnp.float32)

    def one_batch(items):
        first, second, cotan = items
        second_pad = pad_all(second[None].astype(jnp.float32))
        pre_two = correlate(second_pad, kernel_two) + bias_second[None, :, None, None, None]
        delta_two = (spread_up(cotan[None]) * slope(pre_two)).astype(jnp.bfloat16)
        delta_float = delta_two.astype(jnp.float32)
        grad_w_two = kernel_grad(second_pad, delta_float)
        grad_b_two = lax.optimization_barrier(jnp.sum(delta_float, axis=(0, 2, 3, 4)))
        back = correlate(pad_all(delta_float), flipped(kernel_two)).astype(jnp.bfloat16)
        first_pad = pad_all(first[None].astype(jnp.float32))
        pre_one = correlate(first_pad, kernel_one) + bias_first[None, :, None, None, None]
        delta_one = (spread_up(back) * slope(pre_one)).astype(jnp.bfloat16).astype(jnp.float32)
        grad_w_one = kernel_grad(first_pad, delta_one)
        grad_b_one = lax.optimization_barrier(jnp.sum(delta_one, axis=(0, 2, 3, 4)))
        return (grad_w_one, grad_b_one, grad_w_two, grad_b_two)
    per_batch = lax.map(one_batch, (first_vol, second_vol, cot_vol))
    return (lax.optimization_barrier(jnp.sum(per_batch[0], axis=0)), lax.optimization_barrier(jnp.sum(per_batch[1], axis=0)), lax.optimization_barrier(jnp.sum(per_batch[2], axis=0)), lax.optimization_barrier(jnp.sum(per_batch[3], axis=0)))
```

```python
import functools

import jax
import jax.numpy as jnp
import numpy as np
from jax import lax
from jax.experimental import pallas as pl
from jax.experimental.pallas import tpu as pltpu
from jax.sharding import PartitionSpec as P

GY = 8
BF = jnp.bfloat16
F32 = jnp.float32
LOW = np.float32(0.3) * np.float32(0.125)
SPAN = 48
ROWS = 512
VMEM = pl.BlockSpec(memory_space=pltpu.VMEM)


def pairs_of(count, stride, kind):
    size, cells = count
    out = []
    for i in range(size):
        p = (i // stride) % cells
        q = p ^ 1 if kind == 0 else (p + 1 if p % 2 else p - 1)
        if 0 <= q < cells:
            out.append((i, i + (q - p) * stride))
    return out


def first_tables():
    place = -np.ones((SPAN,), np.int64)
    chan = -np.ones((SPAN,), np.int64)
    for i in range(4):
        for z in range(8):
            place[i * 8 + z], chan[i * 8 + z] = z + 1, i
        place[32 + i], chan[32 + i] = 0, i
        place[36 + i], chan[36 + i] = 9, i
    pick = np.zeros((3, 112, 9 * SPAN), np.float32)
    fold = np.zeros((40, 9 * SPAN), np.float32)
    zext = np.full((9 * SPAN,), -100.0, np.float32)
    for a in range(3):
        for c in range(3):
            for r in range(SPAN):
                col = (a * 3 + c) * SPAN + r
                if chan[r] >= 0:
                    zext[col] = place[r]
                    fold[(a * 3 + c) * 4 + chan[r], col] = 1.0
                    for b in range(3):
                        pick[b, ((a * 3 + b) * 3 + c) * 4 + chan[r], col] = 1.0
    zrow = np.broadcast_to(zext[None, :], (8, 9 * SPAN)).copy()
    zcol = np.broadcast_to(zext[:, None], (9 * SPAN, 128)).copy()
    return pick, fold, zrow, zcol


def shifts(block):
    wide = block.astype(F32)
    size = wide.shape[1]
    lane = lax.broadcasted_iota(jnp.int32, wide.shape, 1)
    before = jnp.where(lane == 0, 0.0, pltpu.roll(wide, 1, 1)).astype(BF)
    after = jnp.where(lane == size - 1, 0.0, pltpu.roll(wide, size - 1, 1)).astype(BF)
    return before, block, after


def doubler(size):
    row = lax.broadcasted_iota(jnp.int32, (size, 2 * size), 0)
    col = lax.broadcasted_iota(jnp.int32, (size, 2 * size), 1)
    return jnp.where(lax.shift_right_logical(col, 1) == row, 1.0, 0.0).astype(BF)


def dot(a, b):
    return jnp.dot(a, b, preferred_element_type=F32)


def dot_nt(a, b):
    return lax.dot_general(a, b, (((1,), (1,)), ((), ())), preferred_element_type=F32)


def y_parity(grid_z):
    return lax.rem(lax.div(lax.axis_index("space"), grid_z), 2)


def z_parity(grid_z):
    return lax.rem(lax.rem(lax.axis_index("space"), grid_z), 2)


def y_pack(grid_z, x1_ref, g2_ref, x0_ref, a_ref, b_ref):
    mb = lax.axis_index("section")
    par = y_parity(grid_z)
    for ref, up in ((a_ref, 1 - par), (b_ref, par)):
        for p in range(2):
            for z in range(4):
                ref[(p * 4 + z) * 32 : (p * 4 + z + 1) * 32, :] = x1_ref[up * 2 + p, z]
        ref[256:320, :] = jnp.concatenate([g2_ref[up, 0], g2_ref[up, 1]], axis=1)
        for i in range(4):
            plane = x0_ref[0, mb, i, up * 7]
            ref[320 + i * 8 : 328 + i * 8, :] = plane[:, :128]
            ref[352 + i * 8 : 360 + i * 8, :] = plane[:, 128:]


def z_pack(grid_z, x1_ref, g2_ref, x0_ref, ra_ref, rb_ref, x1y_ref, g2y_ref, x0y_ref, *sends):
    mb = lax.axis_index("section")
    even = y_parity(grid_z) == 0
    ra = ra_ref[...]
    rb = rb_ref[...]
    low = jnp.where(even, rb, ra)
    high = jnp.where(even, ra, rb)
    for side, rim in ((0, low), (1, high)):
        for p in range(2):
            for z in range(4):
                x1y_ref[side * 6 + p, z] = rim[(p * 4 + z) * 32 : (p * 4 + z + 1) * 32]
        for z in range(2):
            g2y_ref[side * 3, z] = rim[256:320, z * 64 : z * 64 + 64]
        x0y_ref[:, side * 2304 : side * 2304 + 128] = rim[320:352]
        x0y_ref[:, side * 2304 + 128 : side * 2304 + 256] = rim[352:384]
    x1y_ref[2:6] = x1_ref[...]
    g2y_ref[1:3] = g2_ref[...]
    for i in range(4):
        for y in range(8):
            x0y_ref[i * 8 : i * 8 + 8, (1 + y) * 256 : (2 + y) * 256] = x0_ref[0, mb, i, y]
    zpar = z_parity(grid_z)
    for k in range(len(sends) // 3):
        sx1_ref, sg2_ref, sx0_ref = sends[3 * k : 3 * k + 3]
        up = 1 - zpar if k == 0 else zpar
        for y in range(8):
            for p in range(2):
                sx1_ref[y, p] = x1y_ref[y, up * 2 + p]
        for y in range(4):
            sg2_ref[y] = g2y_ref[y, up]
        row = lax.broadcasted_iota(jnp.int32, (16, 32), 0)
        col = lax.broadcasted_iota(jnp.int32, (16, 32), 1)
        take = jnp.where((col == row * 8 + up * 7) & (row < 4), 1.0, 0.0).astype(BF)
        sx0_ref[...] = dot(take, x0y_ref[...]).astype(BF)


def grads(grid_z, kinds, *refs):
    x1y_ref, g2y_ref, x0y_ref = refs[:3]
    got = refs[3 : 3 + 3 * kinds]
    w1_ref, b1_ref, w2_ref, b2_ref, pick_ref, fold_ref, zrow_ref, zcol_ref, out_ref = refs[
        3 + 3 * kinds : 12 + 3 * kinds
    ]
    xs, dz1, ds, x0s, dz0, up, wb0, w1f, w2d = refs[12 + 3 * kinds :]
    even = z_parity(grid_z) == 0

    def rims(which, index):
        one = got[which][index]
        two = got[3 + which][index] if kinds == 2 else jnp.zeros_like(one)
        return jnp.where(even, two, one), jnp.where(even, one, two)

    for y in range(8):
        rim = [rims(0, (y, p)) for p in range(2)]
        column = [rim[0][0], rim[1][0]] + [x1y_ref[y, z] for z in range(4)] + [rim[0][1], rim[1][1]]
        for z in range(8):
            for c, value in enumerate(shifts(column[z])):
                for a in range(3):
                    if 0 <= y - a < 6:
                        row = z * 288 + a * 96 + c * 32
                        xs[row : row + 32, (y - a) * 128 : (y - a + 1) * 128] = value

    w2 = w2_ref[...].astype(F32)
    w2 = jnp.concatenate(
        [w2[(a * 3 + b) * 96 : (a * 3 + b + 1) * 96] for b in range(3) for a in range(3)], axis=0
    )
    w2t = jnp.transpose(w2).astype(BF)
    for b in range(3):
        for a in range(3):
            for c in range(3):
                k = (2 - a) * 9 + (2 - b) * 3 + 2 - c
                at = (b * 9 + a * 3 + c) * 64
                w2d[:, at : at + 64] = w2_ref[k * 32 : k * 32 + 32]
    b2c = jnp.transpose(jnp.broadcast_to(b2_ref[...], (128, 64)))
    b1c = jnp.transpose(jnp.broadcast_to(b1_ref[...], (128, 32)))

    twice = doubler(64)
    coarse = []
    rim = [rims(1, (y,)) for y in range(4)]
    for z in range(4):
        plane = [
            rim[y][0] if z == 0 else rim[y][1] if z == 3 else g2y_ref[y, z - 1] for y in range(4)
        ]
        coarse.append(dot(jnp.concatenate(plane, axis=0), twice))
    for z in range(6):
        pre = dot(w2t, xs[z * 288 : z * 288 + 864, :])
        for y in range(6):
            at = (y + 1) // 2 * 64
            grad = coarse[(z + 1) // 2][at : at + 64]
            here = pre[:, y * 128 : y * 128 + 128] + b2c
            delta = (grad * jnp.where(here > 0, 0.125, LOW)).astype(BF)
            dz1[z * 64 : z * 64 + 64, y * 128 : y * 128 + 128] = delta
            for c, value in enumerate(shifts(delta)):
                for a in range(3):
                    if 0 <= y - a < 4:
                        row = z * 576 + a * 192 + c * 64
                        ds[row : row + 64, (y - a) * 128 : (y - a + 1) * 128] = value

    total = jnp.zeros((864, 64), F32)
    bias = jnp.zeros((8, 64), F32)
    ones = jnp.ones((8, 512), BF)
    for z in range(4):
        delta = dz1[(z + 1) * 64 : (z + 2) * 64, 128:640]
        total += dot_nt(xs[(z + 1) * 288 : (z + 1) * 288 + 864, 128:640], delta)
        bias += dot_nt(ones, delta)
    total = jnp.concatenate(
        [total[(b * 3 + a) * 96 : (b * 3 + a + 1) * 96] for a in range(3) for b in range(3)], axis=0
    )
    out_ref[:432, :64] = total[:432]
    out_ref[:432, 64:] = total[432:]
    out_ref[432:, :] = jnp.zeros((ROWS - 432, 128), F32)
    out_ref[472:480, :64] = bias

    back = [dot(w2d[...], ds[z * 576 : z * 576 + 1728, :]).astype(BF) for z in range(4)]
    stack = [back[z][:, y * 128 : y * 128 + 128] for y in range(4) for z in range(4)]
    up[...] = dot(jnp.concatenate(stack, axis=0), doubler(128))

    low, high = rims(2, Ellipsis)
    ones = jnp.where(lax.broadcasted_iota(jnp.int32, (8, 256), 0) == 0, 1.0, 0.0)
    for y in range(10):
        lanes = slice(y * 256, y * 256 + 256)
        block = jnp.concatenate(
            [
                x0y_ref[:, lanes].astype(F32),
                jnp.concatenate([low[:4, lanes].astype(F32), high[:4, lanes].astype(F32)], axis=0),
                ones,
            ],
            axis=0,
        ).astype(BF)
        for c, value in enumerate(shifts(block)):
            for a in range(3):
                if 0 <= y - a < 8:
                    row = (a * 3 + c) * SPAN
                    x0s[row : row + SPAN, (y - a) * 256 : (y - a + 1) * 256] = value

    w1f[108:112, :] = jnp.zeros((4, 32), F32)
    for k in range(27):
        w1f[k * 4 : k * 4 + 4, :] = w1_ref[k].astype(F32)
    w1t = jnp.transpose(w1f[...]).astype(BF)
    spread = [dot(w1t, pick_ref[b]) for b in range(3)]
    zrow = jnp.broadcast_to(zrow_ref[0:1, :], (32, 9 * SPAN))
    for z in range(8):
        value = jnp.zeros((32, 9 * SPAN), F32)
        for b in range(3):
            value = jnp.where(zrow == z + b, spread[b], value)
        wb0[z * 32 : z * 32 + 32, :] = value.astype(BF)

    b1w = jnp.concatenate([b1c, b1c], axis=1)
    for y in range(8):
        lanes = slice(y * 256, y * 256 + 256)
        pre = dot(wb0[...], x0s[:, lanes])
        for z in range(8):
            at = (y // 2) * 128 + (z // 2) * 32
            here = pre[z * 32 : z * 32 + 32] + b1w
            delta = up[at : at + 32, :] * jnp.where(here > 0, 0.125, LOW)
            dz0[z * 32 : z * 32 + 32, lanes] = delta.astype(BF)

    full = dot_nt(x0s[...], dz0[...])
    zcol = jnp.concatenate([zcol_ref[...], zcol_ref[...]], axis=1)
    zlane = lax.shift_right_logical(lax.broadcasted_iota(jnp.int32, full.shape, 1), 5).astype(F32)
    fold = fold_ref[...]
    for b in range(3):
        part = jnp.where(zcol == zlane + b, full, 0.0)
        part = lax.dot_general(
            fold,
            part,
            (((1,), (0,)), ((), ())),
            precision=lax.Precision.HIGHEST,
            preferred_element_type=F32,
        )
        part = sum(part[:, z * 32 : z * 32 + 32] for z in range(8))
        out_ref[432:472, b * 32 : b * 32 + 32] = part
    line = full[4 * SPAN + 40 : 4 * SPAN + 48]
    line = sum(line[:, z * 32 : z * 32 + 32] for z in range(8))
    out_ref[472:480, 64:96] = line


def unpack(sum_ref, g1_ref, b1_ref, g2_ref, b2_ref):
    g2_ref[:432, :] = sum_ref[:432, :64].astype(F32)
    g2_ref[432:, :] = sum_ref[:432, 64:].astype(F32)
    rest = sum_ref[432:480, :].astype(F32)
    for a in range(3):
        for b in range(3):
            for c in range(3):
                row = (a * 3 + c) * 4
                g1_ref[a * 9 + b * 3 + c] = rest[row : row + 4, b * 32 : b * 32 + 32]
    b2_ref[...] = rest[40:41, :64]
    b1_ref[...] = rest[40:41, 64:96]


def call(kernel, out, inputs, scratch=(), name=None):
    return pl.pallas_call(
        kernel,
        out_shape=out,
        in_specs=[VMEM] * len(inputs),
        out_specs=jax.tree.map(lambda _: VMEM, out),
        scratch_shapes=list(scratch),
        name=name,
    )(*inputs)


def shaped(*shape, dtype=BF):
    return jax.ShapeDtypeStruct(shape, dtype)


def on_device(grid_z, tables, x0, x1, g2, kernel_one, bias_one, kernel_two, bias_two):
    size = lax.axis_size("space")
    section = lax.axis_index("section")
    x1 = jnp.transpose(lax.dynamic_index_in_dim(x1[0], section, 0, False), (1, 2, 0, 3))
    g2 = jnp.transpose(lax.dynamic_index_in_dim(g2[0], section, 0, False), (1, 2, 0, 3))

    send = call(
        functools.partial(y_pack, grid_z), (shaped(384, 128),) * 2, (x1, g2, x0), name="y_pack"
    )
    got = [
        lax.ppermute(v, "space", pairs_of((size, GY), grid_z, k)) for k, v in enumerate(send)
    ]
    kinds = 1 if grid_z == 2 else 2
    sends = (shaped(8, 2, 32, 128), shaped(4, 64, 64), shaped(16, 2560)) * kinds
    wide = call(
        functools.partial(z_pack, grid_z),
        (shaped(8, 4, 32, 128), shaped(4, 2, 64, 64), shaped(32, 2560)) + sends,
        (x1, g2, x0, *got),
        name="z_pack",
    )
    rims = [
        lax.ppermute(v, "space", pairs_of((size, grid_z), 1, k // 3))
        for k, v in enumerate(wide[3:])
    ]
    w1 = jnp.transpose(kernel_one, (2, 3, 4, 1, 0)).reshape(27, 4, 32)
    w2 = jnp.transpose(kernel_two, (2, 3, 4, 1, 0)).reshape(864, 64)
    inputs = (*wide[:3], *rims, w1, bias_one[None], w2, bias_two[None], *tables)
    packed = call(
        functools.partial(grads, grid_z, kinds),
        shaped(ROWS, 128, dtype=F32),
        inputs,
        scratch=(
            pltpu.VMEM((2304, 768), BF),
            pltpu.VMEM((384, 768), BF),
            pltpu.VMEM((3456, 512), BF),
            pltpu.VMEM((9 * SPAN, 2048), BF),
            pltpu.VMEM((256, 2048), BF),
            pltpu.VMEM((512, 256), F32),
            pltpu.VMEM((256, 9 * SPAN), BF),
            pltpu.VMEM((112, 32), F32),
            pltpu.VMEM((32, 1728), BF),
        ),
        name="grads",
    )
    axes = ("section", "space")
    count = lax.axis_size(axes)
    parts = lax.all_to_all(packed, axes, 0, 0, tiled=True)
    mine = jnp.sum(parts.reshape(count, ROWS // count, 128), axis=0).astype(BF)
    mine = jnp.broadcast_to(mine[None], (count, ROWS // count, 128)).reshape(ROWS, 128)
    total = lax.all_to_all(mine, axes, 0, 0, tiled=True)
    g1, b1, g2, b2 = call(
        unpack,
        (
            shaped(27, 4, 32, dtype=F32),
            shaped(1, 32, dtype=F32),
            shaped(864, 64, dtype=F32),
            shaped(1, 64, dtype=F32),
        ),
        (total,),
        name="unpack",
    )
    g1 = jnp.transpose(g1.reshape(3, 3, 3, 4, 32), (4, 3, 0, 1, 2))
    g2 = jnp.transpose(g2.reshape(3, 3, 3, 32, 64), (4, 3, 0, 1, 2))
    return g1, b1[0], g2, b2[0]


def solution(mesh):
    pick, fold, zrow, zcol = first_tables()
    tables = (jnp.asarray(pick, BF), jnp.asarray(fold), jnp.asarray(zrow), jnp.asarray(zcol))
    grid_z = mesh.shape["space"] // GY
    placed = (P("space"),) * 3 + (P(),) * 4

    return jax.shard_map(
        functools.partial(on_device, grid_z, tables),
        mesh=mesh,
        in_specs=placed,
        out_specs=(P(),) * 4,
        check_vma=False,
    )
```

```python
import functools

import jax
import jax.numpy as jnp
import numpy as np
from jax import lax
from jax.experimental import pallas as pl
from jax.experimental.pallas import tpu as pltpu
from jax.sharding import PartitionSpec as P

GY = 8
BF = jnp.bfloat16
F32 = jnp.float32
LOW = np.float32(0.3) * np.float32(0.125)
SPAN = 48
ROWS = 512
VMEM = pl.BlockSpec(memory_space=pltpu.VMEM)


def pairs_of(count, stride, kind):
    size, cells = count
    out = []
    for i in range(size):
        p = (i // stride) % cells
        q = p ^ 1 if kind == 0 else (p + 1 if p % 2 else p - 1)
        if 0 <= q < cells:
            out.append((i, i + (q - p) * stride))
    return out


def first_tables():
    place = -np.ones((SPAN,), np.int64)
    chan = -np.ones((SPAN,), np.int64)
    for i in range(4):
        for z in range(8):
            place[i * 8 + z], chan[i * 8 + z] = z + 1, i
        place[32 + i], chan[32 + i] = 0, i
        place[36 + i], chan[36 + i] = 9, i
    pick = np.zeros((3, 112, 9 * SPAN), np.float32)
    fold = np.zeros((40, 9 * SPAN), np.float32)
    zext = np.full((9 * SPAN,), -100.0, np.float32)
    for a in range(3):
        for c in range(3):
            for r in range(SPAN):
                col = (a * 3 + c) * SPAN + r
                if chan[r] >= 0:
                    zext[col] = place[r]
                    fold[(a * 3 + c) * 4 + chan[r], col] = 1.0
                    for b in range(3):
                        pick[b, ((a * 3 + b) * 3 + c) * 4 + chan[r], col] = 1.0
    zrow = np.broadcast_to(zext[None, :], (8, 9 * SPAN)).copy()
    zcol = np.broadcast_to(zext[:, None], (9 * SPAN, 128)).copy()
    return pick, fold, zrow, zcol


def shifts(block):
    wide = block.astype(F32)
    size = wide.shape[1]
    lane = lax.broadcasted_iota(jnp.int32, wide.shape, 1)
    before = jnp.where(lane == 0, 0.0, pltpu.roll(wide, 1, 1)).astype(BF)
    after = jnp.where(lane == size - 1, 0.0, pltpu.roll(wide, size - 1, 1)).astype(BF)
    return before, block, after


def doubler(size):
    row = lax.broadcasted_iota(jnp.int32, (size, 2 * size), 0)
    col = lax.broadcasted_iota(jnp.int32, (size, 2 * size), 1)
    return jnp.where(lax.shift_right_logical(col, 1) == row, 1.0, 0.0).astype(BF)


def dot(a, b):
    return jnp.dot(a, b, preferred_element_type=F32)


def dot_nt(a, b):
    return lax.dot_general(a, b, (((1,), (1,)), ((), ())), preferred_element_type=F32)


def y_parity(grid_z):
    return lax.rem(lax.div(lax.axis_index("space"), grid_z), 2)


def z_parity(grid_z):
    return lax.rem(lax.rem(lax.axis_index("space"), grid_z), 2)


def y_pack(grid_z, x1_ref, g2_ref, x0_ref, a_ref, b_ref):
    mb = lax.axis_index("section")
    par = y_parity(grid_z)
    for ref, up in ((a_ref, 1 - par), (b_ref, par)):
        for p in range(2):
            for z in range(4):
                ref[(p * 4 + z) * 32 : (p * 4 + z + 1) * 32, :] = x1_ref[up * 2 + p, z]
        ref[256:320, :] = jnp.concatenate([g2_ref[up, 0], g2_ref[up, 1]], axis=1)
        for i in range(4):
            plane = x0_ref[0, mb, i, up * 7]
            ref[320 + i * 8 : 328 + i * 8, :] = plane[:, :128]
            ref[352 + i * 8 : 360 + i * 8, :] = plane[:, 128:]


def z_pack(grid_z, x1_ref, g2_ref, x0_ref, ra_ref, rb_ref, x1y_ref, g2y_ref, x0y_ref, *sends):
    mb = lax.axis_index("section")
    even = y_parity(grid_z) == 0
    ra = ra_ref[...]
    rb = rb_ref[...]
    low = jnp.where(even, rb, ra)
    high = jnp.where(even, ra, rb)
    for side, rim in ((0, low), (1, high)):
        for p in range(2):
            for z in range(4):
                x1y_ref[side * 6 + p, z] = rim[(p * 4 + z) * 32 : (p * 4 + z + 1) * 32]
        for z in range(2):
            g2y_ref[side * 3, z] = rim[256:320, z * 64 : z * 64 + 64]
        x0y_ref[:, side * 2304 : side * 2304 + 128] = rim[320:352]
        x0y_ref[:, side * 2304 + 128 : side * 2304 + 256] = rim[352:384]
    x1y_ref[2:6] = x1_ref[...]
    g2y_ref[1:3] = g2_ref[...]
    for i in range(4):
        for y in range(8):
            x0y_ref[i * 8 : i * 8 + 8, (1 + y) * 256 : (2 + y) * 256] = x0_ref[0, mb, i, y]
    zpar = z_parity(grid_z)
    for k in range(len(sends) // 3):
        sx1_ref, sg2_ref, sx0_ref = sends[3 * k : 3 * k + 3]
        up = 1 - zpar if k == 0 else zpar
        for y in range(8):
            for p in range(2):
                sx1_ref[y, p] = x1y_ref[y, up * 2 + p]
        for y in range(4):
            sg2_ref[y] = g2y_ref[y, up]
        row = lax.broadcasted_iota(jnp.int32, (16, 32), 0)
        col = lax.broadcasted_iota(jnp.int32, (16, 32), 1)
        take = jnp.where((col == row * 8 + up * 7) & (row < 4), 1.0, 0.0).astype(BF)
        sx0_ref[...] = dot(take, x0y_ref[...]).astype(BF)


def grads(grid_z, kinds, *refs):
    x1y_ref, g2y_ref, x0y_ref = refs[:3]
    got = refs[3 : 3 + 3 * kinds]
    w1_ref, b1_ref, w2_ref, b2_ref, pick_ref, fold_ref, zrow_ref, zcol_ref, out_ref = refs[
        3 + 3 * kinds : 12 + 3 * kinds
    ]
    xs, dz1, ds, x0s, dz0, up, wb0, w1f, w2d = refs[12 + 3 * kinds :]
    even = z_parity(grid_z) == 0

    def rims(which, index):
        one = got[which][index]
        two = got[3 + which][index] if kinds == 2 else jnp.zeros_like(one)
        return jnp.where(even, two, one), jnp.where(even, one, two)

    for y in range(8):
        rim = [rims(0, (y, p)) for p in range(2)]
        column = [rim[0][0], rim[1][0]] + [x1y_ref[y, z] for z in range(4)] + [rim[0][1], rim[1][1]]
        for z in range(8):
            for c, value in enumerate(shifts(column[z])):
                for a in range(3):
                    if 0 <= y - a < 6:
                        row = z * 288 + a * 96 + c * 32
                        xs[row : row + 32, (y - a) * 128 : (y - a + 1) * 128] = value

    w2 = w2_ref[...].astype(F32)
    w2 = jnp.concatenate(
        [w2[(a * 3 + b) * 96 : (a * 3 + b + 1) * 96] for b in range(3) for a in range(3)], axis=0
    )
    w2t = jnp.transpose(w2).astype(BF)
    for b in range(3):
        for a in range(3):
            for c in range(3):
                k = (2 - a) * 9 + (2 - b) * 3 + 2 - c
                at = (b * 9 + a * 3 + c) * 64
                w2d[:, at : at + 64] = w2_ref[k * 32 : k * 32 + 32]
    b2c = jnp.transpose(jnp.broadcast_to(b2_ref[...], (128, 64)))
    b1c = jnp.transpose(jnp.broadcast_to(b1_ref[...], (128, 32)))

    twice = doubler(64)
    coarse = []
    rim = [rims(1, (y,)) for y in range(4)]
    for z in range(4):
        plane = [
            rim[y][0] if z == 0 else rim[y][1] if z == 3 else g2y_ref[y, z - 1] for y in range(4)
        ]
        coarse.append(dot(jnp.concatenate(plane, axis=0), twice))
    for z in range(6):
        pre = dot(w2t, xs[z * 288 : z * 288 + 864, :])
        for y in range(6):
            at = (y + 1) // 2 * 64
            grad = coarse[(z + 1) // 2][at : at + 64]
            here = pre[:, y * 128 : y * 128 + 128] + b2c
            delta = (grad * jnp.where(here > 0, 0.125, LOW)).astype(BF)
            dz1[z * 64 : z * 64 + 64, y * 128 : y * 128 + 128] = delta
            for c, value in enumerate(shifts(delta)):
                for a in range(3):
                    if 0 <= y - a < 4:
                        row = z * 576 + a * 192 + c * 64
                        ds[row : row + 64, (y - a) * 128 : (y - a + 1) * 128] = value

    total = jnp.zeros((864, 64), F32)
    bias = jnp.zeros((8, 64), F32)
    ones = jnp.ones((8, 512), BF)
    for z in range(4):
        delta = dz1[(z + 1) * 64 : (z + 2) * 64, 128:640]
        total += dot_nt(xs[(z + 1) * 288 : (z + 1) * 288 + 864, 128:640], delta)
        bias += dot_nt(ones, delta)
    total = jnp.concatenate(
        [total[(b * 3 + a) * 96 : (b * 3 + a + 1) * 96] for a in range(3) for b in range(3)], axis=0
    )
    out_ref[:432, :64] = total[:432]
    out_ref[:432, 64:] = total[432:]
    out_ref[432:, :] = jnp.zeros((ROWS - 432, 128), F32)
    out_ref[472:480, :64] = bias

    back = [dot(w2d[...], ds[z * 576 : z * 576 + 1728, :]).astype(BF) for z in range(4)]
    stack = [back[z][:, y * 128 : y * 128 + 128] for y in range(4) for z in range(4)]
    up[...] = dot(jnp.concatenate(stack, axis=0), doubler(128))

    low, high = rims(2, Ellipsis)
    ones = jnp.where(lax.broadcasted_iota(jnp.int32, (8, 256), 0) == 0, 1.0, 0.0)
    for y in range(10):
        lanes = slice(y * 256, y * 256 + 256)
        block = jnp.concatenate(
            [
                x0y_ref[:, lanes].astype(F32),
                jnp.concatenate([low[:4, lanes].astype(F32), high[:4, lanes].astype(F32)], axis=0),
                ones,
            ],
            axis=0,
        ).astype(BF)
        for c, value in enumerate(shifts(block)):
            for a in range(3):
                if 0 <= y - a < 8:
                    row = (a * 3 + c) * SPAN
                    x0s[row : row + SPAN, (y - a) * 256 : (y - a + 1) * 256] = value

    w1f[108:112, :] = jnp.zeros((4, 32), F32)
    for k in range(27):
        w1f[k * 4 : k * 4 + 4, :] = w1_ref[k].astype(F32)
    w1t = jnp.transpose(w1f[...]).astype(BF)
    spread = [dot(w1t, pick_ref[b]) for b in range(3)]
    zrow = jnp.broadcast_to(zrow_ref[0:1, :], (32, 9 * SPAN))
    for z in range(8):
        value = jnp.zeros((32, 9 * SPAN), F32)
        for b in range(3):
            value = jnp.where(zrow == z + b, spread[b], value)
        wb0[z * 32 : z * 32 + 32, :] = value.astype(BF)

    b1w = jnp.concatenate([b1c, b1c], axis=1)
    for y in range(8):
        lanes = slice(y * 256, y * 256 + 256)
        pre = dot(wb0[...], x0s[:, lanes])
        for z in range(8):
            at = (y // 2) * 128 + (z // 2) * 32
            here = pre[z * 32 : z * 32 + 32] + b1w
            delta = up[at : at + 32, :] * jnp.where(here > 0, 0.125, LOW)
            dz0[z * 32 : z * 32 + 32, lanes] = delta.astype(BF)

    full = dot_nt(x0s[...], dz0[...])
    zcol = jnp.concatenate([zcol_ref[...], zcol_ref[...]], axis=1)
    zlane = lax.shift_right_logical(lax.broadcasted_iota(jnp.int32, full.shape, 1), 5).astype(F32)
    fold = fold_ref[...]
    for b in range(3):
        part = jnp.where(zcol == zlane + b, full, 0.0)
        part = lax.dot_general(
            fold,
            part,
            (((1,), (0,)), ((), ())),
            precision=lax.Precision.HIGHEST,
            preferred_element_type=F32,
        )
        part = sum(part[:, z * 32 : z * 32 + 32] for z in range(8))
        out_ref[432:472, b * 32 : b * 32 + 32] = part
    line = full[4 * SPAN + 40 : 4 * SPAN + 48]
    line = sum(line[:, z * 32 : z * 32 + 32] for z in range(8))
    out_ref[472:480, 64:96] = line


def unpack(sum_ref, g1_ref, b1_ref, g2_ref, b2_ref):
    g2_ref[:432, :] = sum_ref[:432, :64].astype(F32)
    g2_ref[432:, :] = sum_ref[:432, 64:].astype(F32)
    rest = sum_ref[432:480, :].astype(F32)
    for a in range(3):
        for b in range(3):
            for c in range(3):
                row = (a * 3 + c) * 4
                g1_ref[a * 9 + b * 3 + c] = rest[row : row + 4, b * 32 : b * 32 + 32]
    b2_ref[...] = rest[40:41, :64]
    b1_ref[...] = rest[40:41, 64:96]


def call(kernel, out, inputs, scratch=(), name=None, room=8):
    return pl.pallas_call(
        kernel,
        out_shape=out,
        in_specs=[VMEM] * len(inputs),
        out_specs=jax.tree.map(lambda _: VMEM, out),
        scratch_shapes=list(scratch),
        compiler_params=pltpu.CompilerParams(vmem_limit_bytes=room << 20),
        name=name,
    )(*inputs)


def shaped(*shape, dtype=BF):
    return jax.ShapeDtypeStruct(shape, dtype)


def on_device(grid_z, tables, x0, x1, g2, kernel_one, bias_one, kernel_two, bias_two):
    size = lax.axis_size("space")
    section = lax.axis_index("section")
    x1 = jnp.transpose(lax.dynamic_index_in_dim(x1[0], section, 0, False), (1, 2, 0, 3))
    g2 = jnp.transpose(lax.dynamic_index_in_dim(g2[0], section, 0, False), (1, 2, 0, 3))

    send = call(
        functools.partial(y_pack, grid_z), (shaped(384, 128),) * 2, (x1, g2, x0), name="y_pack"
    )
    got = [
        lax.ppermute(v, "space", pairs_of((size, GY), grid_z, k)) for k, v in enumerate(send)
    ]
    kinds = 1 if grid_z == 2 else 2
    sends = (shaped(8, 2, 32, 128), shaped(4, 64, 64), shaped(16, 2560)) * kinds
    wide = call(
        functools.partial(z_pack, grid_z),
        (shaped(8, 4, 32, 128), shaped(4, 2, 64, 64), shaped(32, 2560)) + sends,
        (x1, g2, x0, *got),
        name="z_pack",
    )
    rims = [
        lax.ppermute(v, "space", pairs_of((size, grid_z), 1, k // 3))
        for k, v in enumerate(wide[3:])
    ]
    w1 = jnp.transpose(kernel_one, (2, 3, 4, 1, 0)).reshape(27, 4, 32)
    w2 = jnp.transpose(kernel_two, (2, 3, 4, 1, 0)).reshape(864, 64)
    inputs = (*wide[:3], *rims, w1, bias_one[None], w2, bias_two[None], *tables)
    packed = call(
        functools.partial(grads, grid_z, kinds),
        shaped(ROWS, 128, dtype=F32),
        inputs,
        scratch=(
            pltpu.VMEM((2304, 768), BF),
            pltpu.VMEM((384, 768), BF),
            pltpu.VMEM((3456, 512), BF),
            pltpu.VMEM((9 * SPAN, 2048), BF),
            pltpu.VMEM((256, 2048), BF),
            pltpu.VMEM((512, 256), F32),
            pltpu.VMEM((256, 9 * SPAN), BF),
            pltpu.VMEM((112, 32), F32),
            pltpu.VMEM((32, 1728), BF),
        ),
        name="grads",
        room=24,
    )
    axes = ("section", "space")
    count = lax.axis_size(axes)
    parts = lax.all_to_all(packed, axes, 0, 0, tiled=True)
    mine = jnp.sum(parts.reshape(count, ROWS // count, 128), axis=0).astype(BF)
    mine = jnp.broadcast_to(mine[None], (count, ROWS // count, 128)).reshape(ROWS, 128)
    total = lax.all_to_all(mine, axes, 0, 0, tiled=True)
    g1, b1, g2, b2 = call(
        unpack,
        (
            shaped(27, 4, 32, dtype=F32),
            shaped(1, 32, dtype=F32),
            shaped(864, 64, dtype=F32),
            shaped(1, 64, dtype=F32),
        ),
        (total,),
        name="unpack",
    )
    g1 = jnp.transpose(g1.reshape(3, 3, 3, 4, 32), (4, 3, 0, 1, 2))
    g2 = jnp.transpose(g2.reshape(3, 3, 3, 32, 64), (4, 3, 0, 1, 2))
    return g1, b1[0], g2, b2[0]


def solution(mesh):
    pick, fold, zrow, zcol = first_tables()
    tables = (jnp.asarray(pick, BF), jnp.asarray(fold), jnp.asarray(zrow), jnp.asarray(zcol))
    grid_z = mesh.shape["space"] // GY
    placed = (P("space"),) * 3 + (P(),) * 4

    return jax.shard_map(
        functools.partial(on_device, grid_z, tables),
        mesh=mesh,
        in_specs=placed,
        out_specs=(P(),) * 4,
        check_vma=False,
    )
```

```python
import functools

import jax
import jax.numpy as jnp
import numpy as np
from jax import lax
from jax.experimental import pallas as pl
from jax.experimental.pallas import tpu as pltpu
from jax.sharding import PartitionSpec as P

GY = 8
BF = jnp.bfloat16
F32 = jnp.float32
LOW = np.float32(0.3) * np.float32(0.125)
SPAN = 48
VMEM = pl.BlockSpec(memory_space=pltpu.VMEM)


def pairs_of(count, stride, kind):
    size, cells = count
    out = []
    for i in range(size):
        p = (i // stride) % cells
        q = p ^ 1 if kind == 0 else (p + 1 if p % 2 else p - 1)
        if 0 <= q < cells:
            out.append((i, i + (q - p) * stride))
    return out


def place_of(flat):
    block = lax.shift_right_logical(flat * 1366, 16)
    r = flat - block * SPAN
    chan = jnp.where(r < 32, lax.shift_right_logical(r, 3), r & 3)
    plane = jnp.where(r < 32, (r & 7) + 1, jnp.where(r < 36, 0, jnp.where(r < 40, 9, -100)))
    return block, chan, plane


def shifts(block):
    wide = block.astype(F32)
    size = wide.shape[1]
    lane = lax.broadcasted_iota(jnp.int32, wide.shape, 1)
    before = jnp.where(lane == 0, 0.0, pltpu.roll(wide, 1, 1)).astype(BF)
    after = jnp.where(lane == size - 1, 0.0, pltpu.roll(wide, size - 1, 1)).astype(BF)
    return before, block, after


def doubler(size):
    row = lax.broadcasted_iota(jnp.int32, (size, 2 * size), 0)
    col = lax.broadcasted_iota(jnp.int32, (size, 2 * size), 1)
    return jnp.where(lax.shift_right_logical(col, 1) == row, 1.0, 0.0).astype(BF)


def dot(a, b):
    return jnp.dot(a, b, preferred_element_type=F32)


def dot_nt(a, b):
    return lax.dot_general(a, b, (((1,), (1,)), ((), ())), preferred_element_type=F32)


def y_parity(grid_z):
    return lax.rem(lax.div(lax.axis_index("space"), grid_z), 2)


def z_parity(grid_z):
    return lax.rem(lax.rem(lax.axis_index("space"), grid_z), 2)


def y_pack(grid_z, x1_ref, g2_ref, x0_ref, a_ref, b_ref):
    par = y_parity(grid_z)
    for ref, up in ((a_ref, 1 - par), (b_ref, par)):
        for p in range(2):
            for z in range(4):
                ref[(p * 4 + z) * 32 : (p * 4 + z + 1) * 32, :] = x1_ref[up * 2 + p, z]
        ref[256:320, :] = jnp.concatenate([g2_ref[up, 0], g2_ref[up, 1]], axis=1)
        for i in range(4):
            plane = x0_ref[i, up * 7]
            ref[320 + i * 8 : 328 + i * 8, :] = plane[:, :128]
            ref[352 + i * 8 : 360 + i * 8, :] = plane[:, 128:]


def fetch(*refs):
    mb = lax.axis_index("section")
    sources, targets, sems = refs[:7], refs[7:14], refs[14]
    copies = [
        pltpu.make_async_copy(source.at[0, mb] if k < 3 else source, target, sems.at[k])
        for k, (source, target) in enumerate(zip(sources, targets))
    ]
    for copy in copies:
        copy.start()
    for copy in copies:
        copy.wait()


def z_pack(grid_z, ready_ref, x1_ref, g2_ref, x0_ref, ra_ref, rb_ref, x1r_ref, g2y_ref, x0r_ref, *sends):
    even = y_parity(grid_z) == 0
    ra = ra_ref[...]
    rb = rb_ref[...]
    low = jnp.where(even, rb, ra)
    high = jnp.where(even, ra, rb)
    for side, rim in ((0, low), (1, high)):
        for p in range(2):
            for z in range(4):
                x1r_ref[side * 2 + p, z] = rim[(p * 4 + z) * 32 : (p * 4 + z + 1) * 32]
        for z in range(2):
            g2y_ref[side * 3, z] = rim[256:320, z * 64 : z * 64 + 64]
        x0r_ref[side, :, :128] = rim[320:352]
        x0r_ref[side, :, 128:] = rim[352:384]
    g2y_ref[1:3] = g2_ref[...]
    zpar = z_parity(grid_z)
    for k in range(len(sends) // 3):
        sx1_ref, sg2_ref, sx0_ref = sends[3 * k : 3 * k + 3]
        up = 1 - zpar if k == 0 else zpar
        for y in range(8):
            for p in range(2):
                if 2 <= y < 6:
                    sx1_ref[y, p] = x1_ref[y - 2, up * 2 + p]
                else:
                    sx1_ref[y, p] = x1r_ref[y if y < 2 else y - 4, up * 2 + p]
        for y in range(4):
            sg2_ref[y] = g2y_ref[y, up]
        row = lax.broadcasted_iota(jnp.int32, (16, 32), 0)
        col = lax.broadcasted_iota(jnp.int32, (16, 32), 1)
        take = jnp.where((col == row * 8 + up * 7) & (row < 4), 1.0, 0.0).astype(BF)
        for y in range(10):
            if 1 <= y < 9:
                block = jnp.concatenate([x0_ref[i, y - 1] for i in range(4)], axis=0)
            else:
                block = x0r_ref[0 if y == 0 else 1]
            sx0_ref[:, y * 256 : y * 256 + 256] = dot(take, block).astype(BF)


def put_second(xs, y, z, block):
    for c, value in enumerate(shifts(block)):
        row = z * 96 + c * 32
        xs[row : row + 32, y * 128 : y * 128 + 128] = value


def put_first(x0s, y, start, block):
    for c, value in enumerate(shifts(block)):
        for a in range(3):
            if 0 <= y - a < 8:
                row = (a * 3 + c) * SPAN + start
                x0s[row : row + block.shape[0], (y - a) * 256 : (y - a + 1) * 256] = value


def prep(
    x1_ref, x0_ref, w1_ref, b1_ref, w2_ref, b2_ref,
    xs, x0s, wb2, wd, wb0, b1_out, b2_out, fold, zcol, w1f,
):
    for y in range(4):
        for z in range(4):
            put_second(xs, y + 2, z + 2, x1_ref[y, z])
    for y in range(8):
        block = jnp.concatenate([x0_ref[i, y] for i in range(4)], axis=0)
        put_first(x0s, y + 1, 0, block)
    wb2[...] = jnp.zeros_like(wb2)
    wd[...] = jnp.zeros_like(wd)
    for a in range(3):
        w2t = jnp.transpose(w2_ref[a * 288 : a * 288 + 288, :].astype(F32)).astype(BF)
        for z in range(6):
            wb2[a, z * 64 : z * 64 + 64, z * 96 : z * 96 + 288] = w2t
        for b in range(3):
            for c in range(3):
                k = (2 - a) * 9 + (2 - b) * 3 + 2 - c
                value = w2_ref[k * 32 : k * 32 + 32]
                for z in range(4):
                    at = (z + b) * 192 + c * 64
                    wd[a, z * 32 : z * 32 + 32, at : at + 64] = value
    b2_out[...] = jnp.transpose(jnp.broadcast_to(b2_ref[...], (128, 64)))
    b1_out[...] = jnp.transpose(jnp.broadcast_to(b1_ref[...], (128, 32)))
    block, chan, plane = place_of(lax.broadcasted_iota(jnp.int32, fold.shape, 1))
    row = lax.broadcasted_iota(jnp.int32, fold.shape, 0)
    fold[...] = jnp.where((row == block * 4 + chan) & (plane >= 0), 1.0, 0.0)
    zcol[...] = place_of(lax.broadcasted_iota(jnp.int32, zcol.shape, 0))[2].astype(F32)
    w1f[108:112, :] = jnp.zeros((4, 32), F32)
    for k in range(27):
        w1f[k * 4 : k * 4 + 4, :] = w1_ref[k].astype(F32)
    w1t = jnp.transpose(w1f[...]).astype(BF)
    block, chan, plane = place_of(lax.broadcasted_iota(jnp.int32, (112, 9 * SPAN), 1))
    row = lax.broadcasted_iota(jnp.int32, (112, 9 * SPAN), 0)
    third = lax.shift_right_logical(block * 11, 5)
    home = jnp.where(plane >= 0, third * 24 + block * 4 + chan, -100)
    spread = [dot(w1t, jnp.where(row == home + b * 12, 1.0, 0.0).astype(BF)) for b in range(3)]
    zrow = place_of(lax.broadcasted_iota(jnp.int32, (32, 9 * SPAN), 1))[2]
    for z in range(8):
        value = jnp.zeros((32, 9 * SPAN), F32)
        for b in range(3):
            value = jnp.where(zrow == z + b, spread[b], value)
        wb0[z * 32 : z * 32 + 32, :] = value.astype(BF)


def rims_in(xs_in, x0s_in, x1r_ref, x0r_ref, xs, x0s):
    for k, y in enumerate((0, 1, 6, 7)):
        for z in range(4):
            put_second(xs, y, z + 2, x1r_ref[k, z])
    for k, y in enumerate((0, 9)):
        put_first(x0s, y, 0, x0r_ref[k])


def rims_of(grid_z, kinds, got):
    even = z_parity(grid_z) == 0

    def rims(ref, index):
        one = got[ref][index]
        two = got[len(got) // 2 + ref][index] if kinds == 2 else jnp.zeros_like(one)
        return jnp.where(even, two, one), jnp.where(even, one, two)

    return rims


def second_grads(grid_z, kinds, *refs):
    xs_in, wb2, b2_ref, g2y_ref = refs[:4]
    rims = rims_of(grid_z, kinds, refs[4 : 4 + 3 * kinds])
    xs, ds, keep_ref, send_ref, bias_ref, dz1 = refs[4 + 3 * kinds :]

    for y in range(8):
        for p in range(2):
            low, high = rims(0, (y, p))
            put_second(xs, y, p, low)
            put_second(xs, y, 6 + p, high)

    twice = doubler(64)
    coarse = []
    rim = [rims(1, (y,)) for y in range(4)]
    for z in range(4):
        plane = [
            rim[y][0] if z == 0 else rim[y][1] if z == 3 else g2y_ref[y, z - 1] for y in range(4)
        ]
        coarse.append(dot(jnp.concatenate(plane, axis=0), twice))
    b2c = b2_ref[...]
    for half in range(3):
        pre = dot(wb2[0], xs[:, half * 256 : half * 256 + 256])
        pre += dot(wb2[1], xs[:, half * 256 + 128 : half * 256 + 384])
        pre += dot(wb2[2], xs[:, half * 256 + 256 : half * 256 + 512])
        for y in (2 * half, 2 * half + 1):
            at = (y + 1) // 2 * 64
            for z in range(6):
                grad = coarse[(z + 1) // 2][at : at + 64]
                here = pre[z * 64 : z * 64 + 64, (y % 2) * 128 : (y % 2) * 128 + 128] + b2c
                delta = (grad * jnp.where(here > 0, 0.125, LOW)).astype(BF)
                dz1[z * 64 : z * 64 + 64, y * 128 : y * 128 + 128] = delta
                for c, value in enumerate(shifts(delta)):
                    row = z * 192 + c * 64
                    ds[row : row + 64, y * 128 : y * 128 + 128] = value

    own = dz1[64:320, 128:640]
    line = dot_nt(jnp.ones((8, 512), BF), own)
    bias_ref[...] = sum(line[:, z * 64 : z * 64 + 64] for z in range(4))
    parts = []
    for a in range(3):
        full = dot_nt(xs[96:672, (a + 1) * 128 : (a + 5) * 128], own)
        parts.append(sum(full[z * 96 : z * 96 + 288, z * 64 : z * 64 + 64] for z in range(4)))
    even = z_parity(grid_z) == 0
    low = (parts[0][:216], jnp.concatenate([parts[0][216:], parts[1][:144]], axis=0))
    high = (jnp.concatenate([parts[1][144:], parts[2][:72]], axis=0), parts[2][72:])
    for k in range(2):
        keep_ref[:216, k * 64 : k * 64 + 64] = jnp.where(even, low[k], high[k])
        send_ref[:, k * 64 : k * 64 + 64] = jnp.where(even, high[k], low[k])


def first_grads(grid_z, kinds, *refs):
    x0s_in, ds, wd, wb0, b1_ref, fold_ref, zcol_ref = refs[:7]
    rims = rims_of(grid_z, kinds, refs[7 : 7 + kinds])
    x0s, out_ref, line_ref, dz0, up = refs[7 + kinds :]

    back = dot(wd[0], ds[:, :512])
    back += dot(wd[1], ds[:, 128:640])
    back += dot(wd[2], ds[:, 256:768])
    back = back.astype(BF)
    stack = [back[:, y * 128 : y * 128 + 128] for y in range(4)]
    up[...] = dot(jnp.concatenate(stack, axis=0), doubler(128))

    low, high = rims(0, Ellipsis)
    ones = jnp.where(lax.broadcasted_iota(jnp.int32, (8, 256), 0) == 0, 1.0, 0.0)
    for y in range(10):
        lanes = slice(y * 256, y * 256 + 256)
        pair = jnp.concatenate([low[:4, lanes].astype(F32), high[:4, lanes].astype(F32)], axis=0)
        put_first(x0s, y, 32, jnp.concatenate([pair, ones], axis=0).astype(BF))

    b1w = jnp.concatenate([b1_ref[...], b1_ref[...]], axis=1)
    for y in range(8):
        lanes = slice(y * 256, y * 256 + 256)
        pre = dot(wb0[...], x0s[:, lanes])
        for z in range(8):
            at = (y // 2) * 128 + (z // 2) * 32
            here = pre[z * 32 : z * 32 + 32] + b1w
            delta = up[at : at + 32, :] * jnp.where(here > 0, 0.125, LOW)
            dz0[z * 32 : z * 32 + 32, lanes] = delta.astype(BF)

    full = dot_nt(x0s[...], dz0[...])
    zcol = zcol_ref[...]
    lane = lax.broadcasted_iota(jnp.int32, zcol.shape, 1)
    zlane = lax.shift_right_logical(lane, 5).astype(F32)
    every = []
    for b in range(3):
        part = jnp.where(zcol == zlane + b, full[:, :128], 0.0)
        part += jnp.where(zcol == zlane + (b + 4), full[:, 128:], 0.0)
        part += pltpu.roll(part, 64, 1)
        every.append(part + pltpu.roll(part, 32, 1))
    part = jnp.where(lane < 32, every[0], jnp.where(lane < 64, every[1], every[2]))
    part = lax.dot_general(
        fold_ref[...],
        part,
        (((1,), (0,)), ((), ())),
        precision=lax.Precision.HIGHEST,
        preferred_element_type=F32,
    )
    out_ref[...] = part
    line = full[4 * SPAN + 40 : 4 * SPAN + 48]
    line_ref[...] = sum(line[:, z * 32 : z * 32 + 32] for z in range(8))


def pack_grads(count, deep, keep_ref, got_ref, bias_two_ref, part_ref, bias_one_ref, out_ref, flat):
    flat[...] = jnp.zeros_like(flat)
    flat[:216, :] = keep_ref[...] + got_ref[...]
    at = (deep - 1) * count
    flat[at : at + 27, :96] = part_ref[:27, :96]
    for b in range(3):
        flat[at + b * 9 : at + b * 9 + 9, 96:] = part_ref[27:36, b * 32 : b * 32 + 32]
    flat[at + 27 : at + 28, :64] = bias_two_ref[:1, :]
    flat[at + 27 : at + 28, 64:96] = bias_one_ref[:1, :]
    for k in range(deep):
        out_ref[:, k, :] = flat[k * count : (k + 1) * count, :]


def sum_parts(count, deep, parts_ref, out_ref):
    sums = [parts_ref[0], parts_ref[1]]
    for k in range(1, count // 2):
        sums[0] += parts_ref[2 * k]
        sums[1] += parts_ref[2 * k + 1]
    row = lax.broadcasted_iota(jnp.int32, (deep, 128), 0)
    sums[0] += jnp.where(row == deep - 1, sums[1], 0.0)
    for k in range(count):
        out_ref[k, 0] = sums[0].astype(BF)
        out_ref[k, 1] = sums[1].astype(BF)


def unpack(count, deep, sum_ref, g1_ref, b1_ref, g2_ref, b2_ref, flat):
    for half in range(2):
        for k in range(deep - 1):
            flat[k * count : (k + 1) * count, :] = sum_ref[:, half, k, :].astype(F32)
        g2_ref[half * 432 : half * 432 + 216, :] = flat[:216, :64]
        g2_ref[half * 432 + 216 : half * 432 + 432, :] = flat[:216, 64:]
    flat[:count, :] = sum_ref[:, 0, deep - 1, :].astype(F32)
    for a in range(3):
        for b in range(3):
            for c in range(3):
                row = (a * 3 + c) * 4
                for i in range(4):
                    r = row + i
                    if r < 27:
                        value = flat[r : r + 1, b * 32 : b * 32 + 32]
                    else:
                        value = flat[b * 9 + r - 27 : b * 9 + r - 26, 96:]
                    g1_ref[a * 9 + b * 3 + c, i : i + 1] = value
    b2_ref[...] = flat[27:28, :64]
    b1_ref[...] = flat[27:28, 64:96]


def call(kernel, out, inputs, scratch=(), name=None, room=8, specs=None, alias=None):
    return pl.pallas_call(
        kernel,
        out_shape=out,
        in_specs=specs or [VMEM] * len(inputs),
        out_specs=jax.tree.map(lambda _: VMEM, out),
        scratch_shapes=list(scratch),
        input_output_aliases=alias or {},
        name=name,
        compiler_params=pltpu.CompilerParams(vmem_limit_bytes=room << 20),
    )(*inputs)


def shaped(*shape, dtype=BF):
    return jax.ShapeDtypeStruct(shape, dtype)


def on_device(grid_z, x0, x1, g2, kernel_one, bias_one, kernel_two, bias_two):
    size = lax.axis_size("space")
    w1 = jnp.transpose(kernel_one, (2, 3, 4, 1, 0)).reshape(27, 4, 32)
    w2 = jnp.transpose(kernel_two, (2, 3, 4, 1, 0)).reshape(864, 64)
    inputs = (x0, x1, g2, w1, bias_one[None], w2, bias_two[None])
    x0, x1, g2, w1, b1, w2, b2 = call(
        fetch,
        (
            shaped(4, 8, 8, 256),
            shaped(32, 4, 4, 128),
            shaped(64, 2, 2, 64),
            shaped(27, 4, 32),
            shaped(1, 32, dtype=F32),
            shaped(864, 64),
            shaped(1, 64, dtype=F32),
        ),
        tuple(pltpu.with_memory_space_constraint(v, pltpu.HBM) for v in inputs),
        scratch=(pltpu.SemaphoreType.DMA((7,)),),
        specs=[pl.BlockSpec(memory_space=pltpu.HBM)] * 7,
        name="fetch",
    )
    x1 = jnp.transpose(x1, (1, 2, 0, 3))
    g2 = jnp.transpose(g2, (1, 2, 0, 3))

    send = call(
        functools.partial(y_pack, grid_z), (shaped(384, 128),) * 2, (x1, g2, x0), name="y_pack"
    )
    got = [lax.ppermute(v, "space", pairs_of((size, GY), grid_z, k)) for k, v in enumerate(send)]
    xs, x0s, wb2, wd, wb0, b1, b2, fold, zcol = call(
        prep,
        (
            shaped(768, 1024),
            shaped(9 * SPAN, 2048),
            shaped(3, 384, 768),
            shaped(3, 128, 1152),
            shaped(256, 9 * SPAN),
            shaped(32, 128, dtype=F32),
            shaped(64, 128, dtype=F32),
            shaped(40, 9 * SPAN, dtype=F32),
            shaped(9 * SPAN, 128, dtype=F32),
        ),
        (x1, x0, w1, b1, w2, b2),
        scratch=(pltpu.VMEM((112, 32), F32),),
        name="prep",
    )
    kinds = 1 if grid_z == 2 else 2
    sends = (shaped(8, 2, 32, 128), shaped(4, 64, 64), shaped(16, 2560)) * kinds
    wide = call(
        functools.partial(z_pack, grid_z),
        (shaped(4, 4, 32, 128), shaped(4, 2, 64, 64), shaped(2, 32, 256)) + sends,
        (b1, x1, g2, x0, *got),
        name="z_pack",
    )
    rims = [
        lax.ppermute(v, "space", pairs_of((size, grid_z), 1, k // 3))
        for k, v in enumerate(wide[3:])
    ]
    xs, x0s = call(
        rims_in,
        (shaped(768, 1024), shaped(9 * SPAN, 2048)),
        (xs, x0s, wide[0], wide[2]),
        alias={0: 0, 1: 1},
        name="rims_in",
    )
    xs, ds, keep, swap, line_two = call(
        functools.partial(second_grads, grid_z, kinds),
        (
            shaped(768, 1024),
            shaped(1152, 768),
            shaped(216, 128, dtype=F32),
            shaped(216, 128, dtype=F32),
            shaped(8, 64, dtype=F32),
        ),
        (xs, wb2, b2, wide[1], *rims),
        scratch=(pltpu.VMEM((384, 768), BF),),
        alias={0: 0},
        name="second_grads",
    )
    swap = lax.ppermute(swap, "space", [(k, k ^ 1) for k in range(size)])
    x0s, part_one, line_one = call(
        functools.partial(first_grads, grid_z, kinds),
        (shaped(9 * SPAN, 2048), shaped(40, 128, dtype=F32), shaped(8, 32, dtype=F32)),
        (x0s, ds, wd, wb0, b1, fold, zcol, *rims[2::3]),
        scratch=(pltpu.VMEM((256, 2048), BF), pltpu.VMEM((512, 256), F32)),
        alias={0: 0},
        name="first_grads",
    )
    axes = ("section", "space")
    count = lax.axis_size(axes)
    deep = -(-216 // count) + 1
    shape = shaped(count, deep, 128, dtype=F32)
    lines = (pltpu.VMEM((deep * count, 128), F32),)
    packed = call(
        functools.partial(pack_grads, count, deep),
        shape,
        (keep, swap, line_two, part_one, line_one),
        scratch=lines,
        name="pack_grads",
    )
    parts = lax.all_to_all(packed, axes, 0, 0, tiled=True)
    mine = call(
        functools.partial(sum_parts, count, deep),
        shaped(count, 2, deep, 128),
        (parts,),
        name="sum_parts",
    )
    total = lax.all_to_all(mine, axes, 0, 0, tiled=True)
    g1, b1, g2, b2 = call(
        functools.partial(unpack, count, deep),
        (
            shaped(27, 4, 32, dtype=F32),
            shaped(1, 32, dtype=F32),
            shaped(864, 64, dtype=F32),
            shaped(1, 64, dtype=F32),
        ),
        (total,),
        scratch=lines,
        name="unpack",
    )
    g1 = jnp.transpose(g1.reshape(3, 3, 3, 4, 32), (4, 3, 0, 1, 2))
    g2 = jnp.transpose(g2.reshape(3, 3, 3, 32, 64), (4, 3, 0, 1, 2))
    return g1, b1[0], g2, b2[0]


def solution(mesh):
    grid_z = mesh.shape["space"] // GY
    placed = (P("space"),) * 3 + (P(),) * 4

    return jax.shard_map(
        functools.partial(on_device, grid_z),
        mesh=mesh,
        in_specs=placed,
        out_specs=(P(),) * 4,
        check_vma=False,
    )
```

```python
import functools

import jax
import jax.numpy as jnp
import numpy as np
from jax import lax
from jax.experimental import pallas as pl
from jax.experimental.pallas import tpu as pltpu
from jax.sharding import PartitionSpec as P

GY = 8
BF = jnp.bfloat16
F32 = jnp.float32
LOW = np.float32(0.3) * np.float32(0.125)
SPAN = 48
VMEM = pl.BlockSpec(memory_space=pltpu.VMEM)


def pairs_of(count, stride, kind):
    size, cells = count
    out = []
    for i in range(size):
        p = (i // stride) % cells
        q = p ^ 1 if kind == 0 else (p + 1 if p % 2 else p - 1)
        if 0 <= q < cells:
            out.append((i, i + (q - p) * stride))
    return out


def place_of(flat):
    block = lax.shift_right_logical(flat * 1366, 16)
    r = flat - block * SPAN
    chan = jnp.where(r < 32, lax.shift_right_logical(r, 3), r & 3)
    plane = jnp.where(r < 32, (r & 7) + 1, jnp.where(r < 36, 0, jnp.where(r < 40, 9, -100)))
    return block, chan, plane


def shifts(block):
    wide = block.astype(F32)
    size = wide.shape[1]
    lane = lax.broadcasted_iota(jnp.int32, wide.shape, 1)
    before = jnp.where(lane == 0, 0.0, pltpu.roll(wide, 1, 1)).astype(BF)
    after = jnp.where(lane == size - 1, 0.0, pltpu.roll(wide, size - 1, 1)).astype(BF)
    return before, block, after


def doubler(size):
    row = lax.broadcasted_iota(jnp.int32, (size, 2 * size), 0)
    col = lax.broadcasted_iota(jnp.int32, (size, 2 * size), 1)
    return jnp.where(lax.shift_right_logical(col, 1) == row, 1.0, 0.0).astype(BF)


def dot(a, b):
    return jnp.dot(a, b, preferred_element_type=F32)


def dot_nt(a, b):
    return lax.dot_general(a, b, (((1,), (1,)), ((), ())), preferred_element_type=F32)


def y_parity(grid_z):
    return lax.rem(lax.div(lax.axis_index("space"), grid_z), 2)


def z_parity(grid_z):
    return lax.rem(lax.rem(lax.axis_index("space"), grid_z), 2)


def y_pack(grid_z, x1_ref, g2_ref, x0_ref, a_ref, b_ref):
    par = y_parity(grid_z)
    for ref, up in ((a_ref, 1 - par), (b_ref, par)):
        for p in range(2):
            for z in range(4):
                ref[(p * 4 + z) * 32 : (p * 4 + z + 1) * 32, :] = x1_ref[up * 2 + p, z]
        ref[256:320, :] = jnp.concatenate([g2_ref[up, 0], g2_ref[up, 1]], axis=1)
        for i in range(4):
            plane = x0_ref[i, up * 7]
            ref[320 + i * 8 : 328 + i * 8, :] = plane[:, :128]
            ref[352 + i * 8 : 360 + i * 8, :] = plane[:, 128:]


def fetch(*refs):
    mb = lax.axis_index("section")
    sources, targets, sems = refs[:7], refs[7:14], refs[14]
    copies = [
        pltpu.make_async_copy(source.at[0, mb] if k < 3 else source, target, sems.at[k])
        for k, (source, target) in enumerate(zip(sources, targets))
    ]
    for copy in copies:
        copy.start()
    for copy in copies:
        copy.wait()


def z_pack(grid_z, ready_ref, x1_ref, g2_ref, x0_ref, ra_ref, rb_ref, x1r_ref, g2y_ref, x0r_ref, *sends):
    even = y_parity(grid_z) == 0
    ra = ra_ref[...]
    rb = rb_ref[...]
    low = jnp.where(even, rb, ra)
    high = jnp.where(even, ra, rb)
    for side, rim in ((0, low), (1, high)):
        for p in range(2):
            for z in range(4):
                x1r_ref[side * 2 + p, z] = rim[(p * 4 + z) * 32 : (p * 4 + z + 1) * 32]
        for z in range(2):
            g2y_ref[side * 3, z] = rim[256:320, z * 64 : z * 64 + 64]
        x0r_ref[side, :, :128] = rim[320:352]
        x0r_ref[side, :, 128:] = rim[352:384]
    g2y_ref[1:3] = g2_ref[...]
    zpar = z_parity(grid_z)
    for k, send_ref in enumerate(sends):
        up = 1 - zpar if k == 0 else zpar
        for y in range(8):
            for p in range(2):
                if 2 <= y < 6:
                    plane = x1_ref[y - 2, up * 2 + p]
                else:
                    plane = x1r_ref[y if y < 2 else y - 4, up * 2 + p]
                send_ref[(y * 2 + p) * 32 : (y * 2 + p + 1) * 32, :] = plane
        for y in range(0, 4, 2):
            pair = jnp.concatenate([g2y_ref[y, up], g2y_ref[y + 1, up]], axis=1)
            send_ref[512 + y * 32 : 576 + y * 32, :] = pair
        row = lax.broadcasted_iota(jnp.int32, (16, 32), 0)
        col = lax.broadcasted_iota(jnp.int32, (16, 32), 1)
        take = jnp.where((col == row * 8 + up * 7) & (row < 4), 1.0, 0.0).astype(BF)
        for y in range(10):
            if 1 <= y < 9:
                block = jnp.concatenate([x0_ref[i, y - 1] for i in range(4)], axis=0)
            else:
                block = x0r_ref[0 if y == 0 else 1]
            plane = dot(take, block).astype(BF)
            send_ref[640 + y * 32 : 656 + y * 32, :] = plane[:, :128]
            send_ref[656 + y * 32 : 672 + y * 32, :] = plane[:, 128:]


def put_second(xs, y, z, block):
    for c, value in enumerate(shifts(block)):
        row = z * 96 + c * 32
        xs[row : row + 32, y * 128 : y * 128 + 128] = value


def put_first(x0s, y, start, block):
    for c, value in enumerate(shifts(block)):
        for a in range(3):
            if 0 <= y - a < 8:
                row = (a * 3 + c) * SPAN + start
                x0s[row : row + block.shape[0], (y - a) * 256 : (y - a + 1) * 256] = value


def prep(
    x1_ref, x0_ref, w1_ref, b1_ref, w2_ref, b2_ref,
    xs, x0s, wb2, wd, wb0, b1_out, b2_out, w1f,
):
    for y in range(4):
        for z in range(4):
            put_second(xs, y + 2, z + 2, x1_ref[y, z])
    for y in range(8):
        block = jnp.concatenate([x0_ref[i, y] for i in range(4)], axis=0)
        put_first(x0s, y + 1, 0, block)
    wb2[...] = jnp.zeros_like(wb2)
    wd[...] = jnp.zeros_like(wd)
    for a in range(3):
        w2t = jnp.transpose(w2_ref[a * 288 : a * 288 + 288, :].astype(F32)).astype(BF)
        for z in range(3):
            wb2[a, z * 64 : z * 64 + 64, z * 96 : z * 96 + 288] = w2t
        for b in range(3):
            for c in range(3):
                k = (2 - a) * 9 + (2 - b) * 3 + 2 - c
                value = w2_ref[k * 32 : k * 32 + 32]
                for z in range(4):
                    at = (z + b) * 192 + c * 64
                    wd[a, z * 32 : z * 32 + 32, at : at + 64] = value
    b2_out[...] = jnp.transpose(jnp.broadcast_to(b2_ref[...], (128, 64)))
    b1_out[...] = jnp.transpose(jnp.broadcast_to(b1_ref[...], (128, 32)))
    w1f[108:112, :] = jnp.zeros((4, 32), F32)
    for k in range(27):
        w1f[k * 4 : k * 4 + 4, :] = w1_ref[k].astype(F32)
    w1t = jnp.transpose(w1f[...]).astype(BF)
    block, chan, plane = place_of(lax.broadcasted_iota(jnp.int32, (112, 9 * SPAN), 1))
    row = lax.broadcasted_iota(jnp.int32, (112, 9 * SPAN), 0)
    third = lax.shift_right_logical(block * 11, 5)
    home = jnp.where(plane >= 0, third * 24 + block * 4 + chan, -100)
    spread = [dot(w1t, jnp.where(row == home + b * 12, 1.0, 0.0).astype(BF)) for b in range(3)]
    zrow = place_of(lax.broadcasted_iota(jnp.int32, (32, 9 * SPAN), 1))[2]
    for z in range(8):
        value = jnp.zeros((32, 9 * SPAN), F32)
        for b in range(3):
            value = jnp.where(zrow == z + b, spread[b], value)
        wb0[z * 32 : z * 32 + 32, :] = value.astype(BF)


def rims_in(xs_in, x0s_in, x1r_ref, x0r_ref, xs, x0s):
    for k, y in enumerate((0, 1, 6, 7)):
        for z in range(4):
            put_second(xs, y, z + 2, x1r_ref[k, z])
    for k, y in enumerate((0, 9)):
        put_first(x0s, y, 0, x0r_ref[k])


def rims_of(grid_z, got):
    even = z_parity(grid_z) == 0

    def rims(start, size):
        one = got[0][start : start + size]
        two = got[1][start : start + size] if len(got) == 2 else jnp.zeros_like(one)
        return jnp.where(even, two, one), jnp.where(even, one, two)

    return rims


def second_grads(grid_z, kinds, *refs):
    xs_in, wb2, b2_ref, g2y_ref = refs[:4]
    rims = rims_of(grid_z, refs[4 : 4 + kinds])
    xs, ds, keep_ref, send_ref, bias_ref, dz1 = refs[4 + kinds :]

    for y in range(8):
        for p in range(2):
            low, high = rims((y * 2 + p) * 32, 32)
            put_second(xs, y, p, low)
            put_second(xs, y, 6 + p, high)

    twice = doubler(64)
    coarse = []
    rim = [rims(512 + y * 64, 64) for y in range(2)]
    for z in range(4):
        plane = []
        for y in range(4):
            if z in (0, 3):
                plane.append(rim[y // 2][z // 3][:, (y % 2) * 64 : (y % 2) * 64 + 64])
            else:
                plane.append(g2y_ref[y, z - 1])
        coarse.append(dot(jnp.concatenate(plane, axis=0), twice))
    b2c = b2_ref[...]
    for part in range(3):
        for group in range(2):
            rows = slice(group * 288, group * 288 + 480)
            pre = dot(wb2[0], xs[rows, part * 256 : part * 256 + 256])
            pre += dot(wb2[1], xs[rows, part * 256 + 128 : part * 256 + 384])
            pre += dot(wb2[2], xs[rows, part * 256 + 256 : part * 256 + 512])
            for y in (2 * part, 2 * part + 1):
                at = (y + 1) // 2 * 64
                for k in range(3):
                    z = group * 3 + k
                    grad = coarse[(z + 1) // 2][at : at + 64]
                    here = pre[k * 64 : k * 64 + 64, (y % 2) * 128 : (y % 2) * 128 + 128] + b2c
                    delta = (grad * jnp.where(here > 0, 0.125, LOW)).astype(BF)
                    dz1[z * 64 : z * 64 + 64, y * 128 : y * 128 + 128] = delta
                    for c, value in enumerate(shifts(delta)):
                        row = z * 192 + c * 64
                        ds[row : row + 64, y * 128 : y * 128 + 128] = value

    own = dz1[64:320, 128:640]
    line = dot_nt(jnp.ones((8, 512), BF), own)
    bias_ref[...] = sum(line[:, z * 64 : z * 64 + 64] for z in range(4))
    parts = []
    for a in range(3):
        lanes = slice((a + 1) * 128, (a + 5) * 128)
        full = dot_nt(xs[96:480, lanes], own[:128])
        full += dot_nt(xs[288:672, lanes], own[128:])
        parts.append(full[:288, :64] + full[96:, 64:])
    even = z_parity(grid_z) == 0
    low = (parts[0][:216], jnp.concatenate([parts[0][216:], parts[1][:144]], axis=0))
    high = (jnp.concatenate([parts[1][144:], parts[2][:72]], axis=0), parts[2][72:])
    for k in range(2):
        keep_ref[:216, k * 64 : k * 64 + 64] = jnp.where(even, low[k], high[k])
        send_ref[:, k * 64 : k * 64 + 64] = jnp.where(even, high[k], low[k])


def first_grads(grid_z, kinds, *refs):
    x0s_in, ds, wd, wb0, b1_ref = refs[:5]
    rims = rims_of(grid_z, refs[5 : 5 + kinds])
    x0s, out_ref, line_ref, dz0, up = refs[5 + kinds :]

    back = dot(wd[0], ds[:, :512])
    back += dot(wd[1], ds[:, 128:640])
    back += dot(wd[2], ds[:, 256:768])
    back = back.astype(BF)
    stack = [back[:, y * 128 : y * 128 + 128] for y in range(4)]
    up[...] = dot(jnp.concatenate(stack, axis=0), doubler(128))

    ones = jnp.where(lax.broadcasted_iota(jnp.int32, (8, 256), 0) == 0, 1.0, 0.0)
    for y in range(10):
        halves = [rims(640 + y * 32 + h * 16, 16) for h in range(2)]
        low, high = (jnp.concatenate([h[k] for h in halves], axis=1) for k in range(2))
        pair = jnp.concatenate([low[:4].astype(F32), high[:4].astype(F32)], axis=0)
        put_first(x0s, y, 32, jnp.concatenate([pair, ones], axis=0).astype(BF))

    b1w = jnp.concatenate([b1_ref[...], b1_ref[...]], axis=1)
    for y in range(8):
        lanes = slice(y * 256, y * 256 + 256)
        pre = dot(wb0[...], x0s[:, lanes])
        for z in range(8):
            at = (y // 2) * 128 + (z // 2) * 32
            here = pre[z * 32 : z * 32 + 32] + b1w
            delta = up[at : at + 32, :] * jnp.where(here > 0, 0.125, LOW)
            dz0[z * 32 : z * 32 + 32, lanes] = delta.astype(BF)

    full = dot_nt(x0s[...], dz0[...])
    row = lax.broadcasted_iota(jnp.int32, (8, 256), 0)
    lane = lax.shift_right_logical(lax.broadcasted_iota(jnp.int32, (8, 256), 1), 5)
    band = (lane >= row - 1) & (lane <= row + 1)
    ends = jnp.where(row < 4, 0, 7) == lane
    odd = (row[:, :128] & 1) == 1
    upper = (row[:, :128] & 2) == 2
    out_ref[36:, :] = jnp.zeros((4, 128), F32)
    for block in range(9):
        edge = jnp.where(ends, full[block * SPAN + 32 : block * SPAN + 40], 0.0)
        edge = edge[:, :128] + edge[:, 128:]
        edge = pltpu.roll(edge[:4], 32, 1) + edge[4:]
        for i in range(4):
            part = jnp.where(band, full[block * SPAN + i * 8 : block * SPAN + i * 8 + 8], 0.0)
            part = part[:, :128] + part[:, 128:]
            part = jnp.where(odd, pltpu.roll(part, 96, 1), part)
            part = jnp.where(upper, pltpu.roll(part, 64, 1), part)
            part = jnp.sum(part, axis=0, keepdims=True) + edge[i : i + 1]
            out_ref[block * 4 + i : block * 4 + i + 1, :] = part
    line = full[4 * SPAN + 40 : 4 * SPAN + 48]
    line_ref[...] = sum(line[:, z * 32 : z * 32 + 32] for z in range(8))


def pack_grads(count, deep, keep_ref, got_ref, bias_two_ref, part_ref, bias_one_ref, out_ref, flat):
    flat[...] = jnp.zeros_like(flat)
    flat[:216, :] = keep_ref[...] + got_ref[...]
    at = (deep - 1) * count
    for b, lane in enumerate((32, 0, 96)):
        flat[at : at + 27, b * 32 : b * 32 + 32] = part_ref[:27, lane : lane + 32]
        flat[at + b * 9 : at + b * 9 + 9, 96:] = part_ref[27:36, lane : lane + 32]
    flat[at + 27 : at + 28, :64] = bias_two_ref[:1, :]
    flat[at + 27 : at + 28, 64:96] = bias_one_ref[:1, :]
    for k in range(deep):
        out_ref[:, k, :] = flat[k * count : (k + 1) * count, :]


def sum_parts(count, deep, parts_ref, out_ref):
    sums = [parts_ref[0], parts_ref[1]]
    for k in range(1, count // 2):
        sums[0] += parts_ref[2 * k]
        sums[1] += parts_ref[2 * k + 1]
    row = lax.broadcasted_iota(jnp.int32, (deep, 128), 0)
    sums[0] += jnp.where(row == deep - 1, sums[1], 0.0)
    for k in range(count):
        out_ref[k, 0] = sums[0].astype(BF)
        out_ref[k, 1] = sums[1].astype(BF)


def unpack(count, deep, sum_ref, g1_ref, b1_ref, g2_ref, b2_ref, flat):
    for half in range(2):
        for k in range(deep - 1):
            flat[k * count : (k + 1) * count, :] = sum_ref[:, half, k, :].astype(F32)
        g2_ref[half * 432 : half * 432 + 216, :] = flat[:216, :64]
        g2_ref[half * 432 + 216 : half * 432 + 432, :] = flat[:216, 64:]
    flat[:count, :] = sum_ref[:, 0, deep - 1, :].astype(F32)
    for a in range(3):
        for b in range(3):
            for c in range(3):
                row = (a * 3 + c) * 4
                for i in range(4):
                    r = row + i
                    if r < 27:
                        value = flat[r : r + 1, b * 32 : b * 32 + 32]
                    else:
                        value = flat[b * 9 + r - 27 : b * 9 + r - 26, 96:]
                    g1_ref[a * 9 + b * 3 + c, i : i + 1] = value
    b2_ref[...] = flat[27:28, :64]
    b1_ref[...] = flat[27:28, 64:96]


def call(kernel, out, inputs, scratch=(), name=None, room=8, specs=None, alias=None):
    return pl.pallas_call(
        kernel,
        out_shape=out,
        in_specs=specs or [VMEM] * len(inputs),
        out_specs=jax.tree.map(lambda _: VMEM, out),
        scratch_shapes=list(scratch),
        input_output_aliases=alias or {},
        name=name,
        compiler_params=pltpu.CompilerParams(vmem_limit_bytes=room << 20),
    )(*inputs)


def shaped(*shape, dtype=BF):
    return jax.ShapeDtypeStruct(shape, dtype)


def on_device(grid_z, x0, x1, g2, kernel_one, bias_one, kernel_two, bias_two):
    size = lax.axis_size("space")
    w1 = jnp.transpose(kernel_one, (2, 3, 4, 1, 0)).reshape(27, 4, 32)
    w2 = jnp.transpose(kernel_two, (2, 3, 4, 1, 0)).reshape(864, 64)
    inputs = (x0, x1, g2, w1, bias_one[None], w2, bias_two[None])
    x0, x1, g2, w1, b1, w2, b2 = call(
        fetch,
        (
            shaped(4, 8, 8, 256),
            shaped(32, 4, 4, 128),
            shaped(64, 2, 2, 64),
            shaped(27, 4, 32),
            shaped(1, 32, dtype=F32),
            shaped(864, 64),
            shaped(1, 64, dtype=F32),
        ),
        tuple(pltpu.with_memory_space_constraint(v, pltpu.HBM) for v in inputs),
        scratch=(pltpu.SemaphoreType.DMA((7,)),),
        specs=[pl.BlockSpec(memory_space=pltpu.HBM)] * 7,
        name="fetch",
    )
    x1 = jnp.transpose(x1, (1, 2, 0, 3))
    g2 = jnp.transpose(g2, (1, 2, 0, 3))

    send = call(
        functools.partial(y_pack, grid_z), (shaped(384, 128),) * 2, (x1, g2, x0), name="y_pack"
    )
    got = [lax.ppermute(v, "space", pairs_of((size, GY), grid_z, k)) for k, v in enumerate(send)]
    xs, x0s, wb2, wd, wb0, b1, b2 = call(
        prep,
        (
            shaped(768, 1024),
            shaped(9 * SPAN, 2048),
            shaped(3, 192, 480),
            shaped(3, 128, 1152),
            shaped(256, 9 * SPAN),
            shaped(32, 128, dtype=F32),
            shaped(64, 128, dtype=F32),
        ),
        (x1, x0, w1, b1, w2, b2),
        scratch=(pltpu.VMEM((112, 32), F32),),
        name="prep",
    )
    kinds = 1 if grid_z == 2 else 2
    sends = (shaped(960, 128),) * kinds
    wide = call(
        functools.partial(z_pack, grid_z),
        (shaped(4, 4, 32, 128), shaped(4, 2, 64, 64), shaped(2, 32, 256)) + sends,
        (b1, x1, g2, x0, *got),
        name="z_pack",
    )
    rims = [
        lax.ppermute(v, "space", pairs_of((size, grid_z), 1, k))
        for k, v in enumerate(wide[3:])
    ]
    xs, x0s = call(
        rims_in,
        (shaped(768, 1024), shaped(9 * SPAN, 2048)),
        (xs, x0s, wide[0], wide[2]),
        alias={0: 0, 1: 1},
        name="rims_in",
    )
    xs, ds, keep, swap, line_two = call(
        functools.partial(second_grads, grid_z, kinds),
        (
            shaped(768, 1024),
            shaped(1152, 768),
            shaped(216, 128, dtype=F32),
            shaped(216, 128, dtype=F32),
            shaped(8, 64, dtype=F32),
        ),
        (xs, wb2, b2, wide[1], *rims),
        scratch=(pltpu.VMEM((384, 768), BF),),
        alias={0: 0},
        name="second_grads",
    )
    swap = lax.ppermute(swap, "space", [(k, k ^ 1) for k in range(size)])
    x0s, part_one, line_one = call(
        functools.partial(first_grads, grid_z, kinds),
        (shaped(9 * SPAN, 2048), shaped(40, 128, dtype=F32), shaped(8, 32, dtype=F32)),
        (x0s, ds, wd, wb0, b1, *rims),
        scratch=(pltpu.VMEM((256, 2048), BF), pltpu.VMEM((512, 256), F32)),
        alias={0: 0},
        name="first_grads",
    )
    axes = ("section", "space")
    count = lax.axis_size(axes)
    deep = -(-216 // count) + 1
    shape = shaped(count, deep, 128, dtype=F32)
    lines = (pltpu.VMEM((deep * count, 128), F32),)
    packed = call(
        functools.partial(pack_grads, count, deep),
        shape,
        (keep, swap, line_two, part_one, line_one),
        scratch=lines,
        name="pack_grads",
    )
    parts = lax.all_to_all(packed, axes, 0, 0, tiled=True)
    mine = call(
        functools.partial(sum_parts, count, deep),
        shaped(count, 2, deep, 128),
        (parts,),
        name="sum_parts",
    )
    total = lax.all_to_all(mine, axes, 0, 0, tiled=True)
    g1, b1, g2, b2 = call(
        functools.partial(unpack, count, deep),
        (
            shaped(27, 4, 32, dtype=F32),
            shaped(1, 32, dtype=F32),
            shaped(864, 64, dtype=F32),
            shaped(1, 64, dtype=F32),
        ),
        (total,),
        scratch=lines,
        name="unpack",
    )
    g1 = jnp.transpose(g1.reshape(3, 3, 3, 4, 32), (4, 3, 0, 1, 2))
    g2 = jnp.transpose(g2.reshape(3, 3, 3, 32, 64), (4, 3, 0, 1, 2))
    return g1, b1[0], g2, b2[0]


def solution(mesh):
    grid_z = mesh.shape["space"] // GY
    placed = (P("space"),) * 3 + (P(),) * 4

    return jax.shard_map(
        functools.partial(on_device, grid_z),
        mesh=mesh,
        in_specs=placed,
        out_specs=(P(),) * 4,
        check_vma=False,
    )
```

```python
import functools

import jax
import jax.numpy as jnp
import numpy as np
from jax import lax
from jax.experimental import pallas as pl
from jax.experimental.pallas import tpu as pltpu
from jax.sharding import PartitionSpec as P

GY = 8
BF = jnp.bfloat16
F32 = jnp.float32
LOW = np.float32(0.3) * np.float32(0.125)
SPAN = 48
VMEM = pl.BlockSpec(memory_space=pltpu.VMEM)


def pairs_of(count, stride, kind):
    size, cells = count
    out = []
    for i in range(size):
        p = (i // stride) % cells
        q = p ^ 1 if kind == 0 else (p + 1 if p % 2 else p - 1)
        if 0 <= q < cells:
            out.append((i, i + (q - p) * stride))
    return out


def place_of(flat):
    block = lax.shift_right_logical(flat * 1366, 16)
    r = flat - block * SPAN
    chan = jnp.where(r < 32, lax.shift_right_logical(r, 3), r & 3)
    plane = jnp.where(r < 32, (r & 7) + 1, jnp.where(r < 36, 0, jnp.where(r < 40, 9, -100)))
    return block, chan, plane


def shifts(block):
    wide = block.astype(F32)
    size = wide.shape[1]
    lane = lax.broadcasted_iota(jnp.int32, wide.shape, 1)
    before = jnp.where(lane == 0, 0.0, pltpu.roll(wide, 1, 1)).astype(BF)
    after = jnp.where(lane == size - 1, 0.0, pltpu.roll(wide, size - 1, 1)).astype(BF)
    return before, block, after


def doubler(size):
    row = lax.broadcasted_iota(jnp.int32, (size, 2 * size), 0)
    col = lax.broadcasted_iota(jnp.int32, (size, 2 * size), 1)
    return jnp.where(lax.shift_right_logical(col, 1) == row, 1.0, 0.0).astype(BF)


def dot(a, b):
    return jnp.dot(a, b, preferred_element_type=F32)


def dot_nt(a, b):
    return lax.dot_general(a, b, (((1,), (1,)), ((), ())), preferred_element_type=F32)


def y_parity(grid_z):
    return lax.rem(lax.div(lax.axis_index("space"), grid_z), 2)


def z_parity(grid_z):
    return lax.rem(lax.rem(lax.axis_index("space"), grid_z), 2)


def y_pack(grid_z, x1_ref, g2_ref, x0_ref, a_ref, b_ref):
    par = y_parity(grid_z)
    for ref, up in ((a_ref, 1 - par), (b_ref, par)):
        for p in range(2):
            for z in range(4):
                ref[(p * 4 + z) * 32 : (p * 4 + z + 1) * 32, :] = x1_ref[up * 2 + p, z]
        ref[256:320, :] = jnp.concatenate([g2_ref[up, 0], g2_ref[up, 1]], axis=1)
        for i in range(4):
            plane = x0_ref[i, up * 7]
            ref[320 + i * 8 : 328 + i * 8, :] = plane[:, :128]
            ref[352 + i * 8 : 360 + i * 8, :] = plane[:, 128:]


def fetch(*refs):
    mb = lax.axis_index("section")
    sources, targets, sems = refs[:7], refs[7:14], refs[14]
    copies = [
        pltpu.make_async_copy(source.at[0, mb] if k < 3 else source, target, sems.at[k])
        for k, (source, target) in enumerate(zip(sources, targets))
    ]
    for copy in copies:
        copy.start()
    for copy in copies:
        copy.wait()


def z_pack(grid_z, x1_ref, g2_ref, x0_ref, ra_ref, rb_ref, x1r_ref, g2y_ref, x0r_ref, *sends):
    par = y_parity(grid_z)
    even = par == 0
    line = lax.div(lax.axis_index("space"), grid_z)
    inner = (line > 0) & (line < GY - 1)
    ra = ra_ref[...]
    rb = rb_ref[pl.ds(pl.multiple_of(par * 384, 384), 384), :]
    rb = jnp.where(inner, rb, jnp.zeros_like(rb))
    low = jnp.where(even, rb, ra)
    high = jnp.where(even, ra, rb)
    for side, rim in ((0, low), (1, high)):
        for p in range(2):
            for z in range(4):
                x1r_ref[side * 2 + p, z] = rim[(p * 4 + z) * 32 : (p * 4 + z + 1) * 32]
        for z in range(2):
            g2y_ref[side * 3, z] = rim[256:320, z * 64 : z * 64 + 64]
        x0r_ref[side, :, :128] = rim[320:352]
        x0r_ref[side, :, 128:] = rim[352:384]
    g2y_ref[1:3] = g2_ref[...]
    zpar = z_parity(grid_z)
    for k, send_ref in enumerate(sends):
        up = 1 - zpar if k == 0 else zpar
        for y in range(8):
            for p in range(2):
                if 2 <= y < 6:
                    plane = x1_ref[y - 2, up * 2 + p]
                else:
                    plane = x1r_ref[y if y < 2 else y - 4, up * 2 + p]
                send_ref[(y * 2 + p) * 32 : (y * 2 + p + 1) * 32, :] = plane
        for y in range(0, 4, 2):
            pair = jnp.concatenate([g2y_ref[y, up], g2y_ref[y + 1, up]], axis=1)
            send_ref[512 + y * 32 : 576 + y * 32, :] = pair
        row = lax.broadcasted_iota(jnp.int32, (16, 32), 0)
        col = lax.broadcasted_iota(jnp.int32, (16, 32), 1)
        take = jnp.where((col == row * 8 + up * 7) & (row < 4), 1.0, 0.0).astype(BF)
        for y in range(10):
            if 1 <= y < 9:
                block = jnp.concatenate([x0_ref[i, y - 1] for i in range(4)], axis=0)
            else:
                block = x0r_ref[0 if y == 0 else 1]
            plane = dot(take, block).astype(BF)
            send_ref[640 + y * 32 : 656 + y * 32, :] = plane[:, :128]
            send_ref[656 + y * 32 : 672 + y * 32, :] = plane[:, 128:]


def put_second(xs, y, z, block):
    for c, value in enumerate(shifts(block)):
        row = z * 96 + c * 32
        xs[row : row + 32, y * 128 : y * 128 + 128] = value


def put_first(x0s, y, start, block):
    for c, value in enumerate(shifts(block)):
        for a in range(3):
            if 0 <= y - a < 8:
                row = (a * 3 + c) * SPAN + start
                x0s[row : row + block.shape[0], (y - a) * 256 : (y - a + 1) * 256] = value


def prep(
    x1_ref, x0_ref, x1r_ref, x0r_ref, w1_ref, b1_ref, w2_ref, b2_ref,
    xs, x0s, wb2, wd, wb0, b1_out, b2_out, w1f,
):
    for y in range(4):
        for z in range(4):
            put_second(xs, y + 2, z + 2, x1_ref[y, z])
    for y in range(8):
        block = jnp.concatenate([x0_ref[i, y] for i in range(4)], axis=0)
        put_first(x0s, y + 1, 0, block)
    for k, y in enumerate((0, 1, 6, 7)):
        for z in range(4):
            put_second(xs, y, z + 2, x1r_ref[k, z])
    for k, y in enumerate((0, 9)):
        put_first(x0s, y, 0, x0r_ref[k])
    wb2[...] = jnp.zeros_like(wb2)
    wd[...] = jnp.zeros_like(wd)
    for a in range(3):
        w2t = jnp.transpose(w2_ref[a * 288 : a * 288 + 288, :].astype(F32)).astype(BF)
        for z in range(3):
            wb2[a, z * 64 : z * 64 + 64, z * 96 : z * 96 + 288] = w2t
        for b in range(3):
            for c in range(3):
                k = (2 - a) * 9 + (2 - b) * 3 + 2 - c
                value = w2_ref[k * 32 : k * 32 + 32]
                for z in range(4):
                    at = (z + b) * 192 + c * 64
                    wd[a, z * 32 : z * 32 + 32, at : at + 64] = value
    b2_out[...] = jnp.transpose(jnp.broadcast_to(b2_ref[...], (128, 64)))
    b1_out[...] = jnp.transpose(jnp.broadcast_to(b1_ref[...], (128, 32)))
    w1f[108:112, :] = jnp.zeros((4, 32), F32)
    for k in range(27):
        w1f[k * 4 : k * 4 + 4, :] = w1_ref[k].astype(F32)
    w1t = jnp.transpose(w1f[...]).astype(BF)
    block, chan, plane = place_of(lax.broadcasted_iota(jnp.int32, (112, 9 * SPAN), 1))
    row = lax.broadcasted_iota(jnp.int32, (112, 9 * SPAN), 0)
    third = lax.shift_right_logical(block * 11, 5)
    home = jnp.where(plane >= 0, third * 24 + block * 4 + chan, -100)
    spread = [dot(w1t, jnp.where(row == home + b * 12, 1.0, 0.0).astype(BF)) for b in range(3)]
    zrow = place_of(lax.broadcasted_iota(jnp.int32, (32, 9 * SPAN), 1))[2]
    for z in range(8):
        value = jnp.zeros((32, 9 * SPAN), F32)
        for b in range(3):
            value = jnp.where(zrow == z + b, spread[b], value)
        wb0[z * 32 : z * 32 + 32, :] = value.astype(BF)


def rims_of(grid_z, got):
    even = z_parity(grid_z) == 0

    def rims(start, size):
        one = got[0][start : start + size]
        two = got[1][start : start + size] if len(got) == 2 else jnp.zeros_like(one)
        return jnp.where(even, two, one), jnp.where(even, one, two)

    return rims


def second_grads(grid_z, kinds, *refs):
    xs_in, wb2, b2_ref, g2y_ref = refs[:4]
    rims = rims_of(grid_z, refs[4 : 4 + kinds])
    xs, ds, keep_ref, send_ref, bias_ref, dz1 = refs[4 + kinds :]

    for y in range(8):
        for p in range(2):
            low, high = rims((y * 2 + p) * 32, 32)
            put_second(xs, y, p, low)
            put_second(xs, y, 6 + p, high)

    twice = doubler(64)
    coarse = []
    rim = [rims(512 + y * 64, 64) for y in range(2)]
    for z in range(4):
        plane = []
        for y in range(4):
            if z in (0, 3):
                plane.append(rim[y // 2][z // 3][:, (y % 2) * 64 : (y % 2) * 64 + 64])
            else:
                plane.append(g2y_ref[y, z - 1])
        coarse.append(dot(jnp.concatenate(plane, axis=0), twice))
    b2c = b2_ref[...]
    for part in range(3):
        for group in range(2):
            rows = slice(group * 288, group * 288 + 480)
            pre = dot(wb2[0], xs[rows, part * 256 : part * 256 + 256])
            pre += dot(wb2[1], xs[rows, part * 256 + 128 : part * 256 + 384])
            pre += dot(wb2[2], xs[rows, part * 256 + 256 : part * 256 + 512])
            for y in (2 * part, 2 * part + 1):
                at = (y + 1) // 2 * 64
                for k in range(3):
                    z = group * 3 + k
                    grad = coarse[(z + 1) // 2][at : at + 64]
                    here = pre[k * 64 : k * 64 + 64, (y % 2) * 128 : (y % 2) * 128 + 128] + b2c
                    delta = (grad * jnp.where(here > 0, 0.125, LOW)).astype(BF)
                    dz1[z * 64 : z * 64 + 64, y * 128 : y * 128 + 128] = delta
                    for c, value in enumerate(shifts(delta)):
                        row = z * 192 + c * 64
                        ds[row : row + 64, y * 128 : y * 128 + 128] = value

    own = dz1[64:320, 128:640]
    line = dot_nt(jnp.ones((8, 512), BF), own)
    bias_ref[...] = sum(line[:, z * 64 : z * 64 + 64] for z in range(4))
    parts = []
    for a in range(3):
        lanes = slice((a + 1) * 128, (a + 5) * 128)
        full = dot_nt(xs[96:480, lanes], own[:128])
        full += dot_nt(xs[288:672, lanes], own[128:])
        parts.append(full[:288, :64] + full[96:, 64:])
    even = z_parity(grid_z) == 0
    low = (parts[0][:216], jnp.concatenate([parts[0][216:], parts[1][:144]], axis=0))
    high = (jnp.concatenate([parts[1][144:], parts[2][:72]], axis=0), parts[2][72:])
    for k in range(2):
        keep_ref[:216, k * 64 : k * 64 + 64] = jnp.where(even, low[k], high[k])
        send_ref[:, k * 64 : k * 64 + 64] = jnp.where(even, high[k], low[k])


def first_grads(grid_z, kinds, *refs):
    x0s_in, ds, wd, wb0, b1_ref = refs[:5]
    rims = rims_of(grid_z, refs[5 : 5 + kinds])
    x0s, out_ref, line_ref, dz0, up = refs[5 + kinds :]

    back = dot(wd[0], ds[:, :512])
    back += dot(wd[1], ds[:, 128:640])
    back += dot(wd[2], ds[:, 256:768])
    back = back.astype(BF)
    stack = [back[:, y * 128 : y * 128 + 128] for y in range(4)]
    up[...] = dot(jnp.concatenate(stack, axis=0), doubler(128))

    ones = jnp.where(lax.broadcasted_iota(jnp.int32, (8, 256), 0) == 0, 1.0, 0.0)
    for y in range(10):
        halves = [rims(640 + y * 32 + h * 16, 16) for h in range(2)]
        low, high = (jnp.concatenate([h[k] for h in halves], axis=1) for k in range(2))
        pair = jnp.concatenate([low[:4].astype(F32), high[:4].astype(F32)], axis=0)
        put_first(x0s, y, 32, jnp.concatenate([pair, ones], axis=0).astype(BF))

    b1w = jnp.concatenate([b1_ref[...], b1_ref[...]], axis=1)
    for y in range(8):
        lanes = slice(y * 256, y * 256 + 256)
        pre = dot(wb0[...], x0s[:, lanes])
        for z in range(8):
            at = (y // 2) * 128 + (z // 2) * 32
            here = pre[z * 32 : z * 32 + 32] + b1w
            delta = up[at : at + 32, :] * jnp.where(here > 0, 0.125, LOW)
            dz0[z * 32 : z * 32 + 32, lanes] = delta.astype(BF)

    full = dot_nt(x0s[...], dz0[...])
    row = lax.broadcasted_iota(jnp.int32, (8, 256), 0)
    lane = lax.shift_right_logical(lax.broadcasted_iota(jnp.int32, (8, 256), 1), 5)
    band = (lane >= row - 1) & (lane <= row + 1)
    ends = jnp.where(row < 4, 0, 7) == lane
    odd = (row[:, :128] & 1) == 1
    upper = (row[:, :128] & 2) == 2
    out_ref[36:, :] = jnp.zeros((4, 128), F32)
    for block in range(9):
        edge = jnp.where(ends, full[block * SPAN + 32 : block * SPAN + 40], 0.0)
        edge = edge[:, :128] + edge[:, 128:]
        edge = pltpu.roll(edge[:4], 32, 1) + edge[4:]
        for i in range(4):
            part = jnp.where(band, full[block * SPAN + i * 8 : block * SPAN + i * 8 + 8], 0.0)
            part = part[:, :128] + part[:, 128:]
            part = jnp.where(odd, pltpu.roll(part, 96, 1), part)
            part = jnp.where(upper, pltpu.roll(part, 64, 1), part)
            part = jnp.sum(part, axis=0, keepdims=True) + edge[i : i + 1]
            out_ref[block * 4 + i : block * 4 + i + 1, :] = part
    line = full[4 * SPAN + 40 : 4 * SPAN + 48]
    line_ref[...] = sum(line[:, z * 32 : z * 32 + 32] for z in range(8))


def pack_grads(count, deep, keep_ref, got_ref, bias_two_ref, part_ref, bias_one_ref, out_ref, flat):
    flat[...] = jnp.zeros_like(flat)
    flat[:216, :] = keep_ref[...] + got_ref[...]
    at = (deep - 1) * count
    for b, lane in enumerate((32, 0, 96)):
        flat[at : at + 27, b * 32 : b * 32 + 32] = part_ref[:27, lane : lane + 32]
        flat[at + b * 9 : at + b * 9 + 9, 96:] = part_ref[27:36, lane : lane + 32]
    flat[at + 27 : at + 28, :64] = bias_two_ref[:1, :]
    flat[at + 27 : at + 28, 64:96] = bias_one_ref[:1, :]
    for k in range(deep):
        out_ref[:, k, :] = flat[k * count : (k + 1) * count, :]


def sum_parts(count, deep, parts_ref, out_ref):
    sums = [parts_ref[0], parts_ref[1]]
    for k in range(1, count // 2):
        sums[0] += parts_ref[2 * k]
        sums[1] += parts_ref[2 * k + 1]
    row = lax.broadcasted_iota(jnp.int32, (deep, 128), 0)
    sums[0] += jnp.where(row == deep - 1, sums[1], 0.0)
    for k in range(count):
        out_ref[k, 0] = sums[0].astype(BF)
        out_ref[k, 1] = sums[1].astype(BF)


def unpack(count, deep, sum_ref, g1_ref, b1_ref, g2_ref, b2_ref, flat):
    for half in range(2):
        for k in range(deep - 1):
            flat[k * count : (k + 1) * count, :] = sum_ref[:, half, k, :].astype(F32)
        g2_ref[half * 432 : half * 432 + 216, :] = flat[:216, :64]
        g2_ref[half * 432 + 216 : half * 432 + 432, :] = flat[:216, 64:]
    flat[:count, :] = sum_ref[:, 0, deep - 1, :].astype(F32)
    for a in range(3):
        for b in range(3):
            for c in range(3):
                row = (a * 3 + c) * 4
                for i in range(4):
                    r = row + i
                    if r < 27:
                        value = flat[r : r + 1, b * 32 : b * 32 + 32]
                    else:
                        value = flat[b * 9 + r - 27 : b * 9 + r - 26, 96:]
                    g1_ref[a * 9 + b * 3 + c, i : i + 1] = value
    b2_ref[...] = flat[27:28, :64]
    b1_ref[...] = flat[27:28, 64:96]


def call(kernel, out, inputs, scratch=(), name=None, room=8, specs=None, alias=None):
    return pl.pallas_call(
        kernel,
        out_shape=out,
        in_specs=specs or [VMEM] * len(inputs),
        out_specs=jax.tree.map(lambda _: VMEM, out),
        scratch_shapes=list(scratch),
        input_output_aliases=alias or {},
        name=name,
        compiler_params=pltpu.CompilerParams(vmem_limit_bytes=room << 20),
    )(*inputs)


def shaped(*shape, dtype=BF):
    return jax.ShapeDtypeStruct(shape, dtype)


def on_device(grid_z, x0, x1, g2, kernel_one, bias_one, kernel_two, bias_two):
    size = lax.axis_size("space")
    w1 = jnp.transpose(kernel_one, (2, 3, 4, 1, 0)).reshape(27, 4, 32)
    w2 = jnp.transpose(kernel_two, (2, 3, 4, 1, 0)).reshape(864, 64)
    inputs = (x0, x1, g2, w1, bias_one[None], w2, bias_two[None])
    x0, x1, g2, w1, b1, w2, b2 = call(
        fetch,
        (
            shaped(4, 8, 8, 256),
            shaped(32, 4, 4, 128),
            shaped(64, 2, 2, 64),
            shaped(27, 4, 32),
            shaped(1, 32, dtype=F32),
            shaped(864, 64),
            shaped(1, 64, dtype=F32),
        ),
        tuple(pltpu.with_memory_space_constraint(v, pltpu.HBM) for v in inputs),
        scratch=(pltpu.SemaphoreType.DMA((7,)),),
        specs=[pl.BlockSpec(memory_space=pltpu.HBM)] * 7,
        name="fetch",
    )
    x1 = jnp.transpose(x1, (1, 2, 0, 3))
    g2 = jnp.transpose(g2, (1, 2, 0, 3))

    send = call(
        functools.partial(y_pack, grid_z), (shaped(384, 128),) * 2, (x1, g2, x0), name="y_pack"
    )
    inner = [
        [y * grid_z + z, (y + 1) * grid_z + z] for y in range(1, GY - 2, 2) for z in range(grid_z)
    ]
    ends = [[y * grid_z + z, y * grid_z + z + 1] for y in (0, GY - 1) for z in range(0, grid_z, 2)]
    got = [
        lax.ppermute(send[0], "space", pairs_of((size, GY), grid_z, 0)),
        lax.all_gather(send[1], "space", axis_index_groups=inner + ends, tiled=True),
    ]
    kinds = 1 if grid_z == 2 else 2
    sends = (shaped(960, 128),) * kinds
    wide = call(
        functools.partial(z_pack, grid_z),
        (shaped(4, 4, 32, 128), shaped(4, 2, 64, 64), shaped(2, 32, 256)) + sends,
        (x1, g2, x0, *got),
        name="z_pack",
    )
    rims = [
        lax.ppermute(v, "space", pairs_of((size, grid_z), 1, k))
        for k, v in enumerate(wide[3:])
    ]
    xs, x0s, wb2, wd, wb0, b1, b2 = call(
        prep,
        (
            shaped(768, 1024),
            shaped(9 * SPAN, 2048),
            shaped(3, 192, 480),
            shaped(3, 128, 1152),
            shaped(256, 9 * SPAN),
            shaped(32, 128, dtype=F32),
            shaped(64, 128, dtype=F32),
        ),
        (x1, x0, wide[0], wide[2], w1, b1, w2, b2),
        scratch=(pltpu.VMEM((112, 32), F32),),
        name="prep",
    )
    xs, ds, keep, swap, line_two = call(
        functools.partial(second_grads, grid_z, kinds),
        (
            shaped(768, 1024),
            shaped(1152, 768),
            shaped(216, 128, dtype=F32),
            shaped(216, 128, dtype=F32),
            shaped(8, 64, dtype=F32),
        ),
        (xs, wb2, b2, wide[1], *rims),
        scratch=(pltpu.VMEM((384, 768), BF),),
        alias={0: 0},
        name="second_grads",
    )
    swap = lax.ppermute(swap, "space", [(k, k ^ 1) for k in range(size)])
    x0s, part_one, line_one = call(
        functools.partial(first_grads, grid_z, kinds),
        (shaped(9 * SPAN, 2048), shaped(40, 128, dtype=F32), shaped(8, 32, dtype=F32)),
        (x0s, ds, wd, wb0, b1, *rims),
        scratch=(pltpu.VMEM((256, 2048), BF), pltpu.VMEM((512, 256), F32)),
        alias={0: 0},
        name="first_grads",
    )
    axes = ("section", "space")
    count = lax.axis_size(axes)
    deep = -(-216 // count) + 1
    shape = shaped(count, deep, 128, dtype=F32)
    lines = (pltpu.VMEM((deep * count, 128), F32),)
    packed = call(
        functools.partial(pack_grads, count, deep),
        shape,
        (keep, swap, line_two, part_one, line_one),
        scratch=lines,
        name="pack_grads",
    )
    parts = lax.all_to_all(packed, axes, 0, 0, tiled=True)
    mine = call(
        functools.partial(sum_parts, count, deep),
        shaped(count, 2, deep, 128),
        (parts,),
        name="sum_parts",
    )
    total = lax.all_to_all(mine, axes, 0, 0, tiled=True)
    g1, b1, g2, b2 = call(
        functools.partial(unpack, count, deep),
        (
            shaped(27, 4, 32, dtype=F32),
            shaped(1, 32, dtype=F32),
            shaped(864, 64, dtype=F32),
            shaped(1, 64, dtype=F32),
        ),
        (total,),
        scratch=lines,
        name="unpack",
    )
    g1 = jnp.transpose(g1.reshape(3, 3, 3, 4, 32), (4, 3, 0, 1, 2))
    g2 = jnp.transpose(g2.reshape(3, 3, 3, 32, 64), (4, 3, 0, 1, 2))
    return g1, b1[0], g2, b2[0]


def solution(mesh):
    grid_z = mesh.shape["space"] // GY
    placed = (P("space"),) * 3 + (P(),) * 4

    return jax.shard_map(
        functools.partial(on_device, grid_z),
        mesh=mesh,
        in_specs=placed,
        out_specs=(P(),) * 4,
        check_vma=False,
    )
```

```python
import functools

import jax
import jax.numpy as jnp
import numpy as np
from jax import lax
from jax.experimental import pallas as pl
from jax.experimental.pallas import tpu as pltpu
from jax.sharding import PartitionSpec as P

GY = 8
BF = jnp.bfloat16
F32 = jnp.float32
LOW = np.float32(0.3) * np.float32(0.125)
PATCH = 432
VMEM = pl.BlockSpec(memory_space=pltpu.VMEM)


def pairs_of(count, stride, kind):
    size, cells = count
    out = []
    for i in range(size):
        p = (i // stride) % cells
        q = p ^ 1 if kind == 0 else (p + 1 if p % 2 else p - 1)
        if 0 <= q < cells:
            out.append((i, i + (q - p) * stride))
    return out


def place_of(flat):
    own = flat < 288
    block = jnp.where(
        own, lax.shift_right_logical(flat, 5), lax.shift_right_logical(flat - 288, 4)
    )
    r = flat & 31
    h = flat & 15
    chan = jnp.where(own, lax.shift_right_logical(r, 3), h & 3)
    rim = jnp.where(h < 4, 0, jnp.where(h < 8, 9, -100))
    return block, chan, jnp.where(own, (r & 7) + 1, rim)


def shifts(block):
    wide = block.astype(F32)
    size = wide.shape[1]
    lane = lax.broadcasted_iota(jnp.int32, wide.shape, 1)
    before = jnp.where(lane == 0, 0.0, pltpu.roll(wide, 1, 1)).astype(BF)
    after = jnp.where(lane == size - 1, 0.0, pltpu.roll(wide, size - 1, 1)).astype(BF)
    return before, block, after


def doubler(size):
    row = lax.broadcasted_iota(jnp.int32, (size, 2 * size), 0)
    col = lax.broadcasted_iota(jnp.int32, (size, 2 * size), 1)
    return jnp.where(lax.shift_right_logical(col, 1) == row, 1.0, 0.0).astype(BF)


def dot(a, b):
    return jnp.dot(a, b, preferred_element_type=F32)


def dot_nt(a, b):
    return lax.dot_general(a, b, (((1,), (1,)), ((), ())), preferred_element_type=F32)


def y_parity(grid_z):
    return lax.rem(lax.div(lax.axis_index("space"), grid_z), 2)


def z_parity(grid_z):
    return lax.rem(lax.rem(lax.axis_index("space"), grid_z), 2)


def y_pack(grid_z, x1_ref, g2_ref, x0_ref, a_ref, b_ref):
    par = y_parity(grid_z)
    for ref, up in ((a_ref, 1 - par), (b_ref, par)):
        for p in range(2):
            for z in range(4):
                ref[(p * 4 + z) * 32 : (p * 4 + z + 1) * 32, :] = x1_ref[up * 2 + p, z]
        ref[256:320, :] = jnp.concatenate([g2_ref[up, 0], g2_ref[up, 1]], axis=1)
        for i in range(4):
            plane = x0_ref[i, up * 7]
            ref[320 + i * 8 : 328 + i * 8, :] = plane[:, :128]
            ref[352 + i * 8 : 360 + i * 8, :] = plane[:, 128:]


def fetch(*refs):
    mb = lax.axis_index("section")
    sources, targets, sems = refs[:7], refs[7:14], refs[14]
    copies = [
        pltpu.make_async_copy(source.at[0, mb] if k < 3 else source, target, sems.at[k])
        for k, (source, target) in enumerate(zip(sources, targets))
    ]
    for copy in copies:
        copy.start()
    for copy in copies:
        copy.wait()


def z_pack(grid_z, x1_ref, g2_ref, x0_ref, ra_ref, rb_ref, x1r_ref, g2y_ref, x0r_ref, *sends):
    par = y_parity(grid_z)
    even = par == 0
    line = lax.div(lax.axis_index("space"), grid_z)
    inner = (line > 0) & (line < GY - 1)
    ra = ra_ref[...]
    rb = rb_ref[pl.ds(pl.multiple_of(par * 384, 384), 384), :]
    rb = jnp.where(inner, rb, jnp.zeros_like(rb))
    low = jnp.where(even, rb, ra)
    high = jnp.where(even, ra, rb)
    for side, rim in ((0, low), (1, high)):
        for p in range(2):
            for z in range(4):
                x1r_ref[side * 2 + p, z] = rim[(p * 4 + z) * 32 : (p * 4 + z + 1) * 32]
        for z in range(2):
            g2y_ref[side * 3, z] = rim[256:320, z * 64 : z * 64 + 64]
        x0r_ref[side, :, :128] = rim[320:352]
        x0r_ref[side, :, 128:] = rim[352:384]
    g2y_ref[1:3] = g2_ref[...]
    zpar = z_parity(grid_z)
    for k, send_ref in enumerate(sends):
        up = 1 - zpar if k == 0 else zpar
        for y in range(8):
            for p in range(2):
                if 2 <= y < 6:
                    plane = x1_ref[y - 2, up * 2 + p]
                else:
                    plane = x1r_ref[y if y < 2 else y - 4, up * 2 + p]
                send_ref[(y * 2 + p) * 32 : (y * 2 + p + 1) * 32, :] = plane
        for y in range(0, 4, 2):
            pair = jnp.concatenate([g2y_ref[y, up], g2y_ref[y + 1, up]], axis=1)
            send_ref[512 + y * 32 : 576 + y * 32, :] = pair
        row = lax.broadcasted_iota(jnp.int32, (16, 32), 0)
        col = lax.broadcasted_iota(jnp.int32, (16, 32), 1)
        take = jnp.where((col == row * 8 + up * 7) & (row < 4), 1.0, 0.0).astype(BF)
        for y in range(10):
            if 1 <= y < 9:
                block = jnp.concatenate([x0_ref[i, y - 1] for i in range(4)], axis=0)
            else:
                block = x0r_ref[0 if y == 0 else 1]
            plane = dot(take, block).astype(BF)
            send_ref[640 + y * 32 : 656 + y * 32, :] = plane[:, :128]
            send_ref[656 + y * 32 : 672 + y * 32, :] = plane[:, 128:]


def put_second(xs, y, z, block):
    for c, value in enumerate(shifts(block)):
        row = z * 96 + c * 32
        xs[row : row + 32, y * 128 : y * 128 + 128] = value


def put_first(x0s, y, rim, block):
    size = block.shape[0]
    for c, value in enumerate(shifts(block)):
        for a in range(3):
            if 0 <= y - a < 8:
                row = (288 if rim else 0) + (a * 3 + c) * size
                x0s[row : row + size, (y - a) * 256 : (y - a + 1) * 256] = value


def prep(
    x1_ref, x0_ref, x1r_ref, x0r_ref, w1_ref, b1_ref, w2_ref, b2_ref,
    xs, x0s, wb2, wd, wrim, pre_out, b2_out, wb0, w1f,
):
    for y in range(4):
        for z in range(4):
            put_second(xs, y + 2, z + 2, x1_ref[y, z])
    for y in range(8):
        block = jnp.concatenate([x0_ref[i, y] for i in range(4)], axis=0)
        put_first(x0s, y + 1, False, block)
    for k, y in enumerate((0, 1, 6, 7)):
        for z in range(4):
            put_second(xs, y, z + 2, x1r_ref[k, z])
    for k, y in enumerate((0, 9)):
        put_first(x0s, y, False, x0r_ref[k])
    wb2[...] = jnp.zeros_like(wb2)
    wd[...] = jnp.zeros_like(wd)
    for a in range(3):
        w2t = jnp.transpose(w2_ref[a * 288 : a * 288 + 288, :].astype(F32)).astype(BF)
        for z in range(3):
            wb2[a, z * 64 : z * 64 + 64, z * 96 : z * 96 + 288] = w2t
        for b in range(3):
            for c in range(3):
                k = (2 - a) * 9 + (2 - b) * 3 + 2 - c
                value = w2_ref[k * 32 : k * 32 + 32]
                for z in range(4):
                    at = (z + b) * 192 + c * 64
                    wd[a, z * 32 : z * 32 + 32, at : at + 64] = value
    b2_out[...] = jnp.transpose(jnp.broadcast_to(b2_ref[...], (128, 64)))
    b1c = jnp.transpose(jnp.broadcast_to(b1_ref[...], (128, 32)))
    w1f[108:112, :] = jnp.zeros((4, 32), F32)
    for k in range(27):
        w1f[k * 4 : k * 4 + 4, :] = w1_ref[k].astype(F32)
    w1t = jnp.transpose(w1f[...]).astype(BF)
    block, chan, plane = place_of(lax.broadcasted_iota(jnp.int32, (112, PATCH), 1))
    row = lax.broadcasted_iota(jnp.int32, (112, PATCH), 0)
    third = lax.shift_right_logical(block * 11, 5)
    home = jnp.where(plane >= 0, third * 24 + block * 4 + chan, -100)
    spread = [dot(w1t, jnp.where(row == home + b * 12, 1.0, 0.0).astype(BF)) for b in range(3)]
    zrow = place_of(lax.broadcasted_iota(jnp.int32, (32, PATCH), 1))[2]
    for z in range(8):
        value = jnp.zeros((32, PATCH), F32)
        for b in range(3):
            value = jnp.where(zrow == z + b, spread[b], value)
        wb0[z * 32 : z * 32 + 32, :] = value[:, :288].astype(BF)
        if z in (0, 7):
            wrim[z // 7 * 32 : z // 7 * 32 + 32, :] = value[:, 288:].astype(BF)
    b1w = jnp.concatenate([jnp.concatenate([b1c, b1c], axis=1)] * 8, axis=0)
    for y in range(8):
        lanes = slice(y * 256, y * 256 + 256)
        pre_out[:, lanes] = dot(wb0[...], x0s[:288, lanes]) + b1w


def rims_of(grid_z, got):
    even = z_parity(grid_z) == 0

    def rims(start, size):
        one = got[0][start : start + size]
        two = got[1][start : start + size] if len(got) == 2 else jnp.zeros_like(one)
        return jnp.where(even, two, one), jnp.where(even, one, two)

    return rims


def second_grads(grid_z, kinds, *refs):
    xs_in, wb2, wd, b2_ref, g2y_ref = refs[:5]
    rims = rims_of(grid_z, refs[5 : 5 + kinds])
    xs, up, keep_ref, send_ref, bias_ref, dz1, ds = refs[5 + kinds :]

    for y in range(8):
        for p in range(2):
            low, high = rims((y * 2 + p) * 32, 32)
            put_second(xs, y, p, low)
            put_second(xs, y, 6 + p, high)

    twice = doubler(64)
    coarse = []
    rim = [rims(512 + y * 64, 64) for y in range(2)]
    for z in range(4):
        plane = []
        for y in range(4):
            if z in (0, 3):
                plane.append(rim[y // 2][z // 3][:, (y % 2) * 64 : (y % 2) * 64 + 64])
            else:
                plane.append(g2y_ref[y, z - 1])
        coarse.append(dot(jnp.concatenate(plane, axis=0), twice))
    b2c = b2_ref[...]
    for part in range(3):
        for group in range(2):
            rows = slice(group * 288, group * 288 + 480)
            pre = dot(wb2[0], xs[rows, part * 256 : part * 256 + 256])
            pre += dot(wb2[1], xs[rows, part * 256 + 128 : part * 256 + 384])
            pre += dot(wb2[2], xs[rows, part * 256 + 256 : part * 256 + 512])
            for y in (2 * part, 2 * part + 1):
                at = (y + 1) // 2 * 64
                for k in range(3):
                    z = group * 3 + k
                    grad = coarse[(z + 1) // 2][at : at + 64]
                    here = pre[k * 64 : k * 64 + 64, (y % 2) * 128 : (y % 2) * 128 + 128] + b2c
                    delta = (grad * jnp.where(here > 0, 0.125, LOW)).astype(BF)
                    dz1[z * 64 : z * 64 + 64, y * 128 : y * 128 + 128] = delta
                    for c, value in enumerate(shifts(delta)):
                        row = z * 192 + c * 64
                        ds[row : row + 64, y * 128 : y * 128 + 128] = value

    own = dz1[64:320, 128:640]
    line = dot_nt(jnp.ones((8, 512), BF), own)
    bias_ref[...] = sum(line[:, z * 64 : z * 64 + 64] for z in range(4))
    parts = []
    first = lax.broadcasted_iota(jnp.int32, (288, 128), 1) < 64
    for a in range(3):
        lanes = slice((a + 1) * 128, (a + 5) * 128)
        full = dot_nt(xs[96:480, lanes], own[:128])
        full += dot_nt(xs[288:672, lanes], own[128:])
        flip = pltpu.roll(full, 64, 1)
        parts.append(jnp.where(first, full[:288] + flip[96:], flip[:288] + full[96:]))
    even = z_parity(grid_z) == 0
    first = first[:216]
    low = jnp.where(
        first, parts[0][:216], jnp.concatenate([parts[0][216:], parts[1][:144]], axis=0)
    )
    high = jnp.where(
        first, jnp.concatenate([parts[1][144:], parts[2][:72]], axis=0), parts[2][72:]
    )
    keep_ref[...] = jnp.where(even, low, high)
    send_ref[...] = jnp.where(even, high, low)

    back = dot(wd[0], ds[:, :512])
    back += dot(wd[1], ds[:, 128:640])
    back += dot(wd[2], ds[:, 256:768])
    back = back.astype(BF)
    stack = [back[:, y * 128 : y * 128 + 128] for y in range(4)]
    up[...] = dot(jnp.concatenate(stack, axis=0), doubler(128))


def first_grads(grid_z, kinds, *refs):
    x0s_in, up, wrim, pre_ref = refs[:4]
    rims = rims_of(grid_z, refs[4 : 4 + kinds])
    x0s, out_ref, line_ref, dz0 = refs[4 + kinds :]

    ones = jnp.where(lax.broadcasted_iota(jnp.int32, (8, 256), 0) == 0, 1.0, 0.0)
    for y in range(10):
        halves = [rims(640 + y * 32 + h * 16, 16) for h in range(2)]
        low, high = (jnp.concatenate([h[k] for h in halves], axis=1) for k in range(2))
        pair = jnp.concatenate([low[:4].astype(F32), high[:4].astype(F32)], axis=0)
        put_first(x0s, y, True, jnp.concatenate([pair, ones], axis=0).astype(BF))

    for y in range(8):
        lanes = slice(y * 256, y * 256 + 256)
        more = dot(wrim[...], x0s[288:, lanes])
        for z in range(8):
            at = (y // 2) * 128 + (z // 2) * 32
            here = pre_ref[z * 32 : z * 32 + 32, lanes]
            if z in (0, 7):
                here += more[z // 7 * 32 : z // 7 * 32 + 32]
            delta = up[at : at + 32, :] * jnp.where(here > 0, 0.125, LOW)
            dz0[z * 32 : z * 32 + 32, lanes] = delta.astype(BF)

    full = dot_nt(x0s[...], dz0[...])
    row = lax.broadcasted_iota(jnp.int32, (8, 256), 0)
    lane = lax.shift_right_logical(lax.broadcasted_iota(jnp.int32, (8, 256), 1), 5)
    band = (lane >= row - 1) & (lane <= row + 1)
    ends = jnp.where(row < 4, 0, 7) == lane
    odd = (row[:, :128] & 1) == 1
    upper = (row[:, :128] & 2) == 2
    out_ref[36:, :] = jnp.zeros((4, 128), F32)
    for block in range(9):
        edge = jnp.where(ends, full[288 + block * 16 : 296 + block * 16], 0.0)
        edge = edge[:, :128] + edge[:, 128:]
        edge = pltpu.roll(edge[:4], 32, 1) + edge[4:]
        for i in range(4):
            part = jnp.where(band, full[block * 32 + i * 8 : block * 32 + i * 8 + 8], 0.0)
            part = part[:, :128] + part[:, 128:]
            part = jnp.where(odd, pltpu.roll(part, 96, 1), part)
            part = jnp.where(upper, pltpu.roll(part, 64, 1), part)
            part = jnp.sum(part, axis=0, keepdims=True) + edge[i : i + 1]
            out_ref[block * 4 + i : block * 4 + i + 1, :] = part
    line = full[360:368]
    line_ref[...] = sum(line[:, z * 32 : z * 32 + 32] for z in range(8))


def pack_grads(count, deep, keep_ref, got_ref, bias_two_ref, part_ref, bias_one_ref, out_ref, flat):
    flat[...] = jnp.zeros_like(flat)
    flat[:216, :] = keep_ref[...] + got_ref[...]
    at = (deep - 1) * count
    for b, lane in enumerate((32, 0, 96)):
        flat[at : at + 27, b * 32 : b * 32 + 32] = part_ref[:27, lane : lane + 32]
        flat[at + b * 9 : at + b * 9 + 9, 96:] = part_ref[27:36, lane : lane + 32]
    flat[at + 27 : at + 28, :64] = bias_two_ref[:1, :]
    flat[at + 27 : at + 28, 64:96] = bias_one_ref[:1, :]
    for k in range(deep):
        out_ref[:, k, :] = flat[k * count : (k + 1) * count, :]


def sum_parts(count, deep, parts_ref, out_ref):
    sums = [parts_ref[0], parts_ref[1]]
    for k in range(1, count // 2):
        sums[0] += parts_ref[2 * k]
        sums[1] += parts_ref[2 * k + 1]
    row = lax.broadcasted_iota(jnp.int32, (deep, 128), 0)
    sums[0] += jnp.where(row == deep - 1, sums[1], 0.0)
    for k in range(count):
        out_ref[k, 0] = sums[0].astype(BF)
        out_ref[k, 1] = sums[1].astype(BF)


def unpack(count, deep, sum_ref, *refs):
    outs, (g1_ref, b1_ref, g2_ref, b2_ref, flat, sems) = refs[:4], refs[4:]
    flat[:count, :] = sum_ref[:, 0, deep - 1, :].astype(F32)
    for a in range(3):
        for b in range(3):
            for c in range(3):
                row = (a * 3 + c) * 4
                for i in range(4):
                    r = row + i
                    if r < 27:
                        value = flat[r : r + 1, b * 32 : b * 32 + 32]
                    else:
                        value = flat[b * 9 + r - 27 : b * 9 + r - 26, 96:]
                    g1_ref[a * 9 + b * 3 + c, i : i + 1] = value
    b2_ref[...] = flat[27:28, :64]
    b1_ref[...] = flat[27:28, 64:96]
    copies = [
        pltpu.make_async_copy(g1_ref, outs[0], sems.at[0]),
        pltpu.make_async_copy(b1_ref, outs[1], sems.at[1]),
        pltpu.make_async_copy(b2_ref, outs[3], sems.at[2]),
    ]
    for copy in copies:
        copy.start()
    for half in range(2):
        for k in range(deep - 1):
            at = (half * deep + k) * count
            flat[at : at + count, :] = sum_ref[:, half, k, :].astype(F32)
        at = half * deep * count
        g2_ref[half * 432 : half * 432 + 216, :] = flat[at : at + 216, :64]
        g2_ref[half * 432 + 216 : half * 432 + 432, :] = flat[at : at + 216, 64:]
        rows = slice(half * 432, half * 432 + 432)
        copies.append(pltpu.make_async_copy(g2_ref.at[rows], outs[2].at[rows], sems.at[3 + half]))
        copies[-1].start()
    for copy in copies:
        copy.wait()


def call(kernel, out, inputs, scratch=(), name=None, room=8, specs=None, outs=None, alias=None):
    return pl.pallas_call(
        kernel,
        out_shape=out,
        in_specs=specs or [VMEM] * len(inputs),
        out_specs=outs or jax.tree.map(lambda _: VMEM, out),
        scratch_shapes=list(scratch),
        input_output_aliases=alias or {},
        name=name,
        compiler_params=pltpu.CompilerParams(vmem_limit_bytes=room << 20),
    )(*inputs)


def shaped(*shape, dtype=BF):
    return jax.ShapeDtypeStruct(shape, dtype)


def on_device(grid_z, x0, x1, g2, kernel_one, bias_one, kernel_two, bias_two):
    size = lax.axis_size("space")
    w1 = jnp.transpose(kernel_one, (2, 3, 4, 1, 0)).reshape(27, 4, 32)
    w2 = jnp.transpose(kernel_two, (2, 3, 4, 1, 0)).reshape(864, 64)
    inputs = (x0, x1, g2, w1, bias_one[None], w2, bias_two[None])
    x0, x1, g2, w1, b1, w2, b2 = call(
        fetch,
        (
            shaped(4, 8, 8, 256),
            shaped(32, 4, 4, 128),
            shaped(64, 2, 2, 64),
            shaped(27, 4, 32),
            shaped(1, 32, dtype=F32),
            shaped(864, 64),
            shaped(1, 64, dtype=F32),
        ),
        tuple(pltpu.with_memory_space_constraint(v, pltpu.HBM) for v in inputs),
        scratch=(pltpu.SemaphoreType.DMA((7,)),),
        specs=[pl.BlockSpec(memory_space=pltpu.HBM)] * 7,
        name="fetch",
    )
    x1 = jnp.transpose(x1, (1, 2, 0, 3))
    g2 = jnp.transpose(g2, (1, 2, 0, 3))

    send = call(
        functools.partial(y_pack, grid_z), (shaped(384, 128),) * 2, (x1, g2, x0), name="y_pack"
    )
    inner = [
        [y * grid_z + z, (y + 1) * grid_z + z] for y in range(1, GY - 2, 2) for z in range(grid_z)
    ]
    ends = [[y * grid_z + z, y * grid_z + z + 1] for y in (0, GY - 1) for z in range(0, grid_z, 2)]
    got = [
        lax.ppermute(send[0], "space", pairs_of((size, GY), grid_z, 0)),
        lax.all_gather(send[1], "space", axis_index_groups=inner + ends, tiled=True),
    ]
    kinds = 1 if grid_z == 2 else 2
    sends = (shaped(960, 128),) * kinds
    wide = call(
        functools.partial(z_pack, grid_z),
        (shaped(4, 4, 32, 128), shaped(4, 2, 64, 64), shaped(2, 32, 256)) + sends,
        (x1, g2, x0, *got),
        name="z_pack",
    )
    rims = [
        lax.ppermute(v, "space", pairs_of((size, grid_z), 1, k))
        for k, v in enumerate(wide[3:])
    ]
    xs, x0s, wb2, wd, wrim, pre, b2 = call(
        prep,
        (
            shaped(768, 1024),
            shaped(PATCH, 2048),
            shaped(3, 192, 480),
            shaped(3, 128, 1152),
            shaped(64, 144),
            shaped(256, 2048, dtype=F32),
            shaped(64, 128, dtype=F32),
        ),
        (x1, x0, wide[0], wide[2], w1, b1, w2, b2),
        scratch=(pltpu.VMEM((256, 288), BF), pltpu.VMEM((112, 32), F32)),
        name="prep",
    )
    xs, up, keep, swap, line_two = call(
        functools.partial(second_grads, grid_z, kinds),
        (
            shaped(768, 1024),
            shaped(512, 256, dtype=F32),
            shaped(216, 128, dtype=F32),
            shaped(216, 128, dtype=F32),
            shaped(8, 64, dtype=F32),
        ),
        (xs, wb2, wd, b2, wide[1], *rims),
        scratch=(pltpu.VMEM((384, 768), BF), pltpu.VMEM((1152, 768), BF)),
        alias={0: 0},
        name="second_grads",
    )
    swap = lax.ppermute(swap, "space", [(k, k ^ 1) for k in range(size)])
    x0s, part_one, line_one = call(
        functools.partial(first_grads, grid_z, kinds),
        (shaped(PATCH, 2048), shaped(40, 128, dtype=F32), shaped(8, 32, dtype=F32)),
        (x0s, up, wrim, pre, *rims),
        scratch=(pltpu.VMEM((256, 2048), BF),),
        alias={0: 0},
        name="first_grads",
    )
    axes = ("section", "space")
    count = lax.axis_size(axes)
    deep = -(-216 // count) + 1
    shape = shaped(count, deep, 128, dtype=F32)
    lines = (pltpu.VMEM((deep * count, 128), F32),)
    packed = call(
        functools.partial(pack_grads, count, deep),
        shape,
        (keep, swap, line_two, part_one, line_one),
        scratch=lines,
        name="pack_grads",
    )
    parts = lax.all_to_all(packed, axes, 0, 0, tiled=True)
    mine = call(
        functools.partial(sum_parts, count, deep),
        shaped(count, 2, deep, 128),
        (parts,),
        name="sum_parts",
    )
    total = lax.all_to_all(mine, axes, 0, 0, tiled=True)
    g1, b1, g2, b2 = call(
        functools.partial(unpack, count, deep),
        (
            shaped(27, 4, 32, dtype=F32),
            shaped(1, 32, dtype=F32),
            shaped(864, 64, dtype=F32),
            shaped(1, 64, dtype=F32),
        ),
        (total,),
        scratch=(
            pltpu.VMEM((27, 4, 32), F32),
            pltpu.VMEM((1, 32), F32),
            pltpu.VMEM((864, 64), F32),
            pltpu.VMEM((1, 64), F32),
            pltpu.VMEM((2 * deep * count, 128), F32),
            pltpu.SemaphoreType.DMA((5,)),
        ),
        outs=(pl.BlockSpec(memory_space=pltpu.HBM),) * 4,
        name="unpack",
    )
    g1 = jnp.transpose(g1.reshape(3, 3, 3, 4, 32), (4, 3, 0, 1, 2))
    g2 = jnp.transpose(g2.reshape(3, 3, 3, 32, 64), (4, 3, 0, 1, 2))
    return g1, b1[0], g2, b2[0]


def solution(mesh):
    grid_z = mesh.shape["space"] // GY
    placed = (P("space"),) * 3 + (P(),) * 4

    return jax.shard_map(
        functools.partial(on_device, grid_z),
        mesh=mesh,
        in_specs=placed,
        out_specs=(P(),) * 4,
        check_vma=False,
    )
```

```python
import functools

import jax
import jax.numpy as jnp
import numpy as np
from jax import lax
from jax.experimental import pallas as pl
from jax.experimental.pallas import tpu as pltpu
from jax.sharding import PartitionSpec as P

GY = 8
BF = jnp.bfloat16
F32 = jnp.float32
LOW = np.float32(0.3) * np.float32(0.125)
PATCH = 432
VMEM = pl.BlockSpec(memory_space=pltpu.VMEM)


def pairs_of(count, stride, kind):
    size, cells = count
    out = []
    for i in range(size):
        p = (i // stride) % cells
        q = p ^ 1 if kind == 0 else (p + 1 if p % 2 else p - 1)
        if 0 <= q < cells:
            out.append((i, i + (q - p) * stride))
    return out


def place_of(flat):
    own = flat < 288
    block = jnp.where(
        own, lax.shift_right_logical(flat, 5), lax.shift_right_logical(flat - 288, 4)
    )
    r = flat & 31
    h = flat & 15
    chan = jnp.where(own, lax.shift_right_logical(r, 3), h & 3)
    rim = jnp.where(h < 4, 0, jnp.where(h < 8, 9, -100))
    return block, chan, jnp.where(own, (r & 7) + 1, rim)


def shifts(block):
    wide = block.astype(F32)
    size = wide.shape[1]
    lane = lax.broadcasted_iota(jnp.int32, wide.shape, 1)
    before = jnp.where(lane == 0, 0.0, pltpu.roll(wide, 1, 1)).astype(BF)
    after = jnp.where(lane == size - 1, 0.0, pltpu.roll(wide, size - 1, 1)).astype(BF)
    return before, block, after


def doubler(size):
    row = lax.broadcasted_iota(jnp.int32, (size, 2 * size), 0)
    col = lax.broadcasted_iota(jnp.int32, (size, 2 * size), 1)
    return jnp.where(lax.shift_right_logical(col, 1) == row, 1.0, 0.0).astype(BF)


def dot(a, b):
    return jnp.dot(a, b, preferred_element_type=F32)


def dot_nt(a, b):
    return lax.dot_general(a, b, (((1,), (1,)), ((), ())), preferred_element_type=F32)


def y_parity(grid_z):
    return lax.rem(lax.div(lax.axis_index("space"), grid_z), 2)


def z_parity(grid_z):
    return lax.rem(lax.rem(lax.axis_index("space"), grid_z), 2)


def y_pack(grid_z, x1_ref, g2_ref, x0_ref, a_ref, b_ref):
    par = y_parity(grid_z)
    for ref, up in ((a_ref, 1 - par), (b_ref, par)):
        for p in range(2):
            for z in range(4):
                ref[(p * 4 + z) * 32 : (p * 4 + z + 1) * 32, :] = x1_ref[up * 2 + p, z]
        ref[256:320, :] = jnp.concatenate([g2_ref[up, 0], g2_ref[up, 1]], axis=1)
        for i in range(4):
            plane = x0_ref[i, up * 7]
            ref[320 + i * 8 : 328 + i * 8, :] = plane[:, :128]
            ref[352 + i * 8 : 360 + i * 8, :] = plane[:, 128:]


def fetch(*refs):
    mb = lax.axis_index("section")
    sources, targets, sems = refs[:3], refs[3:6], refs[6]
    copies = [
        pltpu.make_async_copy(source.at[0, mb], target, sems.at[k])
        for k, (source, target) in enumerate(zip(sources, targets))
    ]
    for copy in copies:
        copy.start()
    for copy in copies:
        copy.wait()


def z_pack(grid_z, x1_ref, g2_ref, x0_ref, ra_ref, rb_ref, x1r_ref, g2y_ref, x0r_ref, *sends):
    par = y_parity(grid_z)
    even = par == 0
    line = lax.div(lax.axis_index("space"), grid_z)
    inner = (line > 0) & (line < GY - 1)
    ra = ra_ref[...]
    rb = rb_ref[pl.ds(pl.multiple_of(par * 384, 384), 384), :]
    rb = jnp.where(inner, rb, jnp.zeros_like(rb))
    low = jnp.where(even, rb, ra)
    high = jnp.where(even, ra, rb)
    for side, rim in ((0, low), (1, high)):
        for p in range(2):
            for z in range(4):
                x1r_ref[side * 2 + p, z] = rim[(p * 4 + z) * 32 : (p * 4 + z + 1) * 32]
        for z in range(2):
            g2y_ref[side * 3, z] = rim[256:320, z * 64 : z * 64 + 64]
        x0r_ref[side, :, :128] = rim[320:352]
        x0r_ref[side, :, 128:] = rim[352:384]
    g2y_ref[1:3] = g2_ref[...]
    zpar = z_parity(grid_z)
    for k, send_ref in enumerate(sends):
        up = 1 - zpar if k == 0 else zpar
        for y in range(8):
            for p in range(2):
                if 2 <= y < 6:
                    plane = x1_ref[y - 2, up * 2 + p]
                else:
                    plane = x1r_ref[y if y < 2 else y - 4, up * 2 + p]
                send_ref[(y * 2 + p) * 32 : (y * 2 + p + 1) * 32, :] = plane
        for y in range(0, 4, 2):
            pair = jnp.concatenate([g2y_ref[y, up], g2y_ref[y + 1, up]], axis=1)
            send_ref[512 + y * 32 : 576 + y * 32, :] = pair
        row = lax.broadcasted_iota(jnp.int32, (16, 32), 0)
        col = lax.broadcasted_iota(jnp.int32, (16, 32), 1)
        take = jnp.where((col == row * 8 + up * 7) & (row < 4), 1.0, 0.0).astype(BF)
        for y in range(10):
            if 1 <= y < 9:
                block = jnp.concatenate([x0_ref[i, y - 1] for i in range(4)], axis=0)
            else:
                block = x0r_ref[0 if y == 0 else 1]
            plane = dot(take, block).astype(BF)
            send_ref[640 + y * 32 : 656 + y * 32, :] = plane[:, :128]
            send_ref[656 + y * 32 : 672 + y * 32, :] = plane[:, 128:]


def put_second(xs, y, z, block):
    for c, value in enumerate(shifts(block)):
        row = z * 96 + c * 32
        xs[row : row + 32, y * 128 : y * 128 + 128] = value


def put_first(x0s, y, rim, block):
    size = block.shape[0]
    for c, value in enumerate(shifts(block)):
        for a in range(3):
            if 0 <= y - a < 8:
                row = (288 if rim else 0) + (a * 3 + c) * size
                x0s[row : row + size, (y - a) * 256 : (y - a + 1) * 256] = value


def prep(
    x1_ref, x0_ref, x1r_ref, x0r_ref, w1_ref, b1_ref, w2_ref, b2_ref,
    xs, x0s, wb2, wd, wrim, pre_out, b2_out, wb0, w1f,
):
    for y in range(4):
        for z in range(4):
            put_second(xs, y + 2, z + 2, x1_ref[y, z])
    for y in range(8):
        block = jnp.concatenate([x0_ref[i, y] for i in range(4)], axis=0)
        put_first(x0s, y + 1, False, block)
    for k, y in enumerate((0, 1, 6, 7)):
        for z in range(4):
            put_second(xs, y, z + 2, x1r_ref[k, z])
    for k, y in enumerate((0, 9)):
        put_first(x0s, y, False, x0r_ref[k])
    wb2[...] = jnp.zeros_like(wb2)
    wd[...] = jnp.zeros_like(wd)
    for a in range(3):
        w2t = jnp.transpose(w2_ref[a * 288 : a * 288 + 288, :].astype(F32)).astype(BF)
        for z in range(3):
            wb2[a, z * 64 : z * 64 + 64, z * 96 : z * 96 + 288] = w2t
        for b in range(3):
            for c in range(3):
                k = (2 - a) * 9 + (2 - b) * 3 + 2 - c
                value = w2_ref[k * 32 : k * 32 + 32]
                for z in range(4):
                    at = (z + b) * 192 + c * 64
                    wd[a, z * 32 : z * 32 + 32, at : at + 64] = value
    b2_out[...] = jnp.transpose(jnp.broadcast_to(b2_ref[...], (128, 64)))
    b1c = jnp.transpose(jnp.broadcast_to(b1_ref[...], (128, 32)))
    w1f[108:112, :] = jnp.zeros((4, 32), F32)
    for k in range(27):
        w1f[k * 4 : k * 4 + 4, :] = w1_ref[k].astype(F32)
    w1t = jnp.transpose(w1f[...]).astype(BF)
    block, chan, plane = place_of(lax.broadcasted_iota(jnp.int32, (112, PATCH), 1))
    row = lax.broadcasted_iota(jnp.int32, (112, PATCH), 0)
    third = lax.shift_right_logical(block * 11, 5)
    home = jnp.where(plane >= 0, third * 24 + block * 4 + chan, -100)
    spread = [dot(w1t, jnp.where(row == home + b * 12, 1.0, 0.0).astype(BF)) for b in range(3)]
    zrow = place_of(lax.broadcasted_iota(jnp.int32, (32, PATCH), 1))[2]
    for z in range(8):
        value = jnp.zeros((32, PATCH), F32)
        for b in range(3):
            value = jnp.where(zrow == z + b, spread[b], value)
        wb0[z * 32 : z * 32 + 32, :] = value[:, :288].astype(BF)
        if z in (0, 7):
            wrim[z // 7 * 32 : z // 7 * 32 + 32, :] = value[:, 288:].astype(BF)
    b1w = jnp.concatenate([jnp.concatenate([b1c, b1c], axis=1)] * 8, axis=0)
    for y in range(8):
        lanes = slice(y * 256, y * 256 + 256)
        pre_out[:, lanes] = dot(wb0[...], x0s[:288, lanes]) + b1w


def rims_of(grid_z, got):
    even = z_parity(grid_z) == 0

    def rims(start, size):
        one = got[0][start : start + size]
        two = got[1][start : start + size] if len(got) == 2 else jnp.zeros_like(one)
        return jnp.where(even, two, one), jnp.where(even, one, two)

    return rims


def second_grads(grid_z, kinds, *refs):
    xs_in, wb2, wd, b2_ref, g2y_ref = refs[:5]
    rims = rims_of(grid_z, refs[5 : 5 + kinds])
    xs, up, keep_ref, send_ref, bias_ref, dz1, ds = refs[5 + kinds :]

    for y in range(8):
        for p in range(2):
            low, high = rims((y * 2 + p) * 32, 32)
            put_second(xs, y, p, low)
            put_second(xs, y, 6 + p, high)

    twice = doubler(64)
    coarse = []
    rim = [rims(512 + y * 64, 64) for y in range(2)]
    for z in range(4):
        plane = []
        for y in range(4):
            if z in (0, 3):
                plane.append(rim[y // 2][z // 3][:, (y % 2) * 64 : (y % 2) * 64 + 64])
            else:
                plane.append(g2y_ref[y, z - 1])
        coarse.append(dot(jnp.concatenate(plane, axis=0), twice))
    b2c = b2_ref[...]
    for part in range(3):
        for group in range(2):
            rows = slice(group * 288, group * 288 + 480)
            pre = dot(wb2[0], xs[rows, part * 256 : part * 256 + 256])
            pre += dot(wb2[1], xs[rows, part * 256 + 128 : part * 256 + 384])
            pre += dot(wb2[2], xs[rows, part * 256 + 256 : part * 256 + 512])
            for y in (2 * part, 2 * part + 1):
                at = (y + 1) // 2 * 64
                for k in range(3):
                    z = group * 3 + k
                    grad = coarse[(z + 1) // 2][at : at + 64]
                    here = pre[k * 64 : k * 64 + 64, (y % 2) * 128 : (y % 2) * 128 + 128] + b2c
                    delta = (grad * jnp.where(here > 0, 0.125, LOW)).astype(BF)
                    dz1[z * 64 : z * 64 + 64, y * 128 : y * 128 + 128] = delta
                    for c, value in enumerate(shifts(delta)):
                        row = z * 192 + c * 64
                        ds[row : row + 64, y * 128 : y * 128 + 128] = value

    own = dz1[64:320, 128:640]
    line = dot_nt(jnp.ones((8, 512), BF), own)
    bias_ref[...] = sum(line[:, z * 64 : z * 64 + 64] for z in range(4))
    parts = []
    first = lax.broadcasted_iota(jnp.int32, (288, 128), 1) < 64
    for a in range(3):
        lanes = slice((a + 1) * 128, (a + 5) * 128)
        full = dot_nt(xs[96:480, lanes], own[:128])
        full += dot_nt(xs[288:672, lanes], own[128:])
        flip = pltpu.roll(full, 64, 1)
        parts.append(jnp.where(first, full[:288] + flip[96:], flip[:288] + full[96:]))
    even = z_parity(grid_z) == 0
    first = first[:216]
    low = jnp.where(
        first, parts[0][:216], jnp.concatenate([parts[0][216:], parts[1][:144]], axis=0)
    )
    high = jnp.where(
        first, jnp.concatenate([parts[1][144:], parts[2][:72]], axis=0), parts[2][72:]
    )
    keep_ref[...] = jnp.where(even, low, high)
    send_ref[...] = jnp.where(even, high, low)

    back = dot(wd[0], ds[:, :512])
    back += dot(wd[1], ds[:, 128:640])
    back += dot(wd[2], ds[:, 256:768])
    back = back.astype(BF)
    stack = [back[:, y * 128 : y * 128 + 128] for y in range(4)]
    up[...] = dot(jnp.concatenate(stack, axis=0), doubler(128))


def first_grads(grid_z, kinds, *refs):
    x0s_in, up, wrim, pre_ref = refs[:4]
    rims = rims_of(grid_z, refs[4 : 4 + kinds])
    x0s, out_ref, line_ref, dz0 = refs[4 + kinds :]

    ones = jnp.where(lax.broadcasted_iota(jnp.int32, (8, 256), 0) == 0, 1.0, 0.0)
    for y in range(10):
        halves = [rims(640 + y * 32 + h * 16, 16) for h in range(2)]
        low, high = (jnp.concatenate([h[k] for h in halves], axis=1) for k in range(2))
        pair = jnp.concatenate([low[:4].astype(F32), high[:4].astype(F32)], axis=0)
        put_first(x0s, y, True, jnp.concatenate([pair, ones], axis=0).astype(BF))

    for y in range(8):
        lanes = slice(y * 256, y * 256 + 256)
        more = dot(wrim[...], x0s[288:, lanes])
        for z in range(8):
            at = (y // 2) * 128 + (z // 2) * 32
            here = pre_ref[z * 32 : z * 32 + 32, lanes]
            if z in (0, 7):
                here += more[z // 7 * 32 : z // 7 * 32 + 32]
            delta = up[at : at + 32, :] * jnp.where(here > 0, 0.125, LOW)
            dz0[z * 32 : z * 32 + 32, lanes] = delta.astype(BF)

    full = dot_nt(x0s[...], dz0[...])
    row = lax.broadcasted_iota(jnp.int32, (8, 256), 0)
    lane = lax.shift_right_logical(lax.broadcasted_iota(jnp.int32, (8, 256), 1), 5)
    band = (lane >= row - 1) & (lane <= row + 1)
    ends = jnp.where(row < 4, 0, 7) == lane
    odd = (row[:, :128] & 1) == 1
    upper = (row[:, :128] & 2) == 2
    out_ref[36:, :] = jnp.zeros((4, 128), F32)
    for block in range(9):
        edge = jnp.where(ends, full[288 + block * 16 : 296 + block * 16], 0.0)
        edge = edge[:, :128] + edge[:, 128:]
        edge = pltpu.roll(edge[:4], 32, 1) + edge[4:]
        for i in range(4):
            part = jnp.where(band, full[block * 32 + i * 8 : block * 32 + i * 8 + 8], 0.0)
            part = part[:, :128] + part[:, 128:]
            part = jnp.where(odd, pltpu.roll(part, 96, 1), part)
            part = jnp.where(upper, pltpu.roll(part, 64, 1), part)
            part = jnp.sum(part, axis=0, keepdims=True) + edge[i : i + 1]
            out_ref[block * 4 + i : block * 4 + i + 1, :] = part
    line = full[360:368]
    line_ref[...] = sum(line[:, z * 32 : z * 32 + 32] for z in range(8))


def pack_grads(count, deep, keep_ref, got_ref, bias_two_ref, part_ref, bias_one_ref, out_ref, flat):
    flat[...] = jnp.zeros_like(flat)
    flat[:216, :] = keep_ref[...] + got_ref[...]
    at = (deep - 1) * count
    for b, lane in enumerate((32, 0, 96)):
        flat[at : at + 27, b * 32 : b * 32 + 32] = part_ref[:27, lane : lane + 32]
        flat[at + b * 9 : at + b * 9 + 9, 96:] = part_ref[27:36, lane : lane + 32]
    flat[at + 27 : at + 28, :64] = bias_two_ref[:1, :]
    flat[at + 27 : at + 28, 64:96] = bias_one_ref[:1, :]
    for k in range(deep):
        out_ref[:, k, :] = flat[k * count : (k + 1) * count, :]


def sum_parts(count, deep, parts_ref, out_ref):
    sums = [parts_ref[0], parts_ref[1]]
    for k in range(1, count // 2):
        sums[0] += parts_ref[2 * k]
        sums[1] += parts_ref[2 * k + 1]
    row = lax.broadcasted_iota(jnp.int32, (deep, 128), 0)
    sums[0] += jnp.where(row == deep - 1, sums[1], 0.0)
    for k in range(count):
        out_ref[k, 0] = sums[0].astype(BF)
        out_ref[k, 1] = sums[1].astype(BF)


def unpack(count, deep, sum_ref, *refs):
    outs, (g1_ref, b1_ref, g2_ref, b2_ref, flat, sems) = refs[:4], refs[4:]
    flat[:count, :] = sum_ref[:, 0, deep - 1, :].astype(F32)
    for a in range(3):
        for b in range(3):
            for c in range(3):
                row = (a * 3 + c) * 4
                for i in range(4):
                    r = row + i
                    if r < 27:
                        value = flat[r : r + 1, b * 32 : b * 32 + 32]
                    else:
                        value = flat[b * 9 + r - 27 : b * 9 + r - 26, 96:]
                    g1_ref[a * 9 + b * 3 + c, i : i + 1] = value
    b2_ref[...] = flat[27:28, :64]
    b1_ref[...] = flat[27:28, 64:96]
    copies = [
        pltpu.make_async_copy(g1_ref, outs[0], sems.at[0]),
        pltpu.make_async_copy(b1_ref, outs[1], sems.at[1]),
        pltpu.make_async_copy(b2_ref, outs[3], sems.at[2]),
    ]
    for copy in copies:
        copy.start()
    for half in range(2):
        for k in range(deep - 1):
            at = (half * deep + k) * count
            flat[at : at + count, :] = sum_ref[:, half, k, :].astype(F32)
        at = half * deep * count
        g2_ref[half * 432 : half * 432 + 216, :] = flat[at : at + 216, :64]
        g2_ref[half * 432 + 216 : half * 432 + 432, :] = flat[at : at + 216, 64:]
        rows = slice(half * 432, half * 432 + 432)
        copies.append(pltpu.make_async_copy(g2_ref.at[rows], outs[2].at[rows], sems.at[3 + half]))
        copies[-1].start()
    for copy in copies:
        copy.wait()


def call(kernel, out, inputs, scratch=(), name=None, room=8, specs=None, outs=None, alias=None, flags=None):
    return pl.pallas_call(
        kernel,
        out_shape=out,
        in_specs=specs or [VMEM] * len(inputs),
        out_specs=outs or jax.tree.map(lambda _: VMEM, out),
        scratch_shapes=list(scratch),
        input_output_aliases=alias or {},
        name=name,
        compiler_params=pltpu.CompilerParams(vmem_limit_bytes=room << 20, flags=flags),
    )(*inputs)


def shaped(*shape, dtype=BF):
    return jax.ShapeDtypeStruct(shape, dtype)


def on_device(grid_z, x0, x1, g2, kernel_one, bias_one, kernel_two, bias_two):
    size = lax.axis_size("space")
    w1 = jnp.transpose(kernel_one, (2, 3, 4, 1, 0)).reshape(27, 4, 32)
    w2 = jnp.transpose(kernel_two, (2, 3, 4, 1, 0)).reshape(864, 64)
    x0, x1, g2 = call(
        fetch,
        (shaped(4, 8, 8, 256), shaped(32, 4, 4, 128), shaped(64, 2, 2, 64)),
        tuple(pltpu.with_memory_space_constraint(v, pltpu.HBM) for v in (x0, x1, g2)),
        scratch=(pltpu.SemaphoreType.DMA((3,)),),
        specs=[pl.BlockSpec(memory_space=pltpu.HBM)] * 3,
        name="fetch",
    )
    x1 = jnp.transpose(x1, (1, 2, 0, 3))
    g2 = jnp.transpose(g2, (1, 2, 0, 3))

    send = call(
        functools.partial(y_pack, grid_z), (shaped(384, 128),) * 2, (x1, g2, x0), name="y_pack"
    )
    inner = [
        [y * grid_z + z, (y + 1) * grid_z + z] for y in range(1, GY - 2, 2) for z in range(grid_z)
    ]
    ends = [[y * grid_z + z, y * grid_z + z + 1] for y in (0, GY - 1) for z in range(0, grid_z, 2)]
    got = [
        lax.ppermute(send[0], "space", pairs_of((size, GY), grid_z, 0)),
        lax.all_gather(send[1], "space", axis_index_groups=inner + ends, tiled=True),
    ]
    kinds = 1 if grid_z == 2 else 2
    sends = (shaped(960, 128),) * kinds
    wide = call(
        functools.partial(z_pack, grid_z),
        (shaped(4, 4, 32, 128), shaped(4, 2, 64, 64), shaped(2, 32, 256)) + sends,
        (x1, g2, x0, *got),
        name="z_pack",
    )
    rims = [
        lax.ppermute(v, "space", pairs_of((size, grid_z), 1, k))
        for k, v in enumerate(wide[3:])
    ]
    xs, x0s, wb2, wd, wrim, pre, b2 = call(
        prep,
        (
            shaped(768, 1024),
            shaped(PATCH, 2048),
            shaped(3, 192, 480),
            shaped(3, 128, 1152),
            shaped(64, 144),
            shaped(256, 2048, dtype=F32),
            shaped(64, 128, dtype=F32),
        ),
        (x1, x0, wide[0], wide[2], w1, bias_one[None], w2, bias_two[None]),
        scratch=(pltpu.VMEM((256, 288), BF), pltpu.VMEM((112, 32), F32)),
        name="prep",
    )
    xs, up, keep, swap, line_two = call(
        functools.partial(second_grads, grid_z, kinds),
        (
            shaped(768, 1024),
            shaped(512, 256, dtype=F32),
            shaped(216, 128, dtype=F32),
            shaped(216, 128, dtype=F32),
            shaped(8, 64, dtype=F32),
        ),
        (xs, wb2, wd, b2, wide[1], *rims),
        scratch=(pltpu.VMEM((384, 768), BF), pltpu.VMEM((1152, 768), BF)),
        alias={0: 0},
        name="second_grads",
    )
    swap = lax.ppermute(swap, "space", [(k, k ^ 1) for k in range(size)])
    x0s, part_one, line_one = call(
        functools.partial(first_grads, grid_z, kinds),
        (shaped(PATCH, 2048), shaped(40, 128, dtype=F32), shaped(8, 32, dtype=F32)),
        (x0s, up, wrim, pre, *rims),
        scratch=(pltpu.VMEM((256, 2048), BF),),
        alias={0: 0},
        name="first_grads",
    )
    axes = ("section", "space")
    count = lax.axis_size(axes)
    deep = -(-216 // count) + 1
    shape = shaped(count, deep, 128, dtype=F32)
    lines = (pltpu.VMEM((deep * count, 128), F32),)
    packed = call(
        functools.partial(pack_grads, count, deep),
        shape,
        (keep, swap, line_two, part_one, line_one),
        scratch=lines,
        name="pack_grads",
    )
    parts = lax.all_to_all(packed, axes, 0, 0, tiled=True)
    mine = call(
        functools.partial(sum_parts, count, deep),
        shaped(count, 2, deep, 128),
        (parts,),
        name="sum_parts",
    )
    total = lax.all_to_all(mine, axes, 0, 0, tiled=True)
    g1, b1, g2, b2 = call(
        functools.partial(unpack, count, deep),
        (
            shaped(27, 4, 32, dtype=F32),
            shaped(1, 32, dtype=F32),
            shaped(864, 64, dtype=F32),
            shaped(1, 64, dtype=F32),
        ),
        (total,),
        scratch=(
            pltpu.VMEM((27, 4, 32), F32),
            pltpu.VMEM((1, 32), F32),
            pltpu.VMEM((864, 64), F32),
            pltpu.VMEM((1, 64), F32),
            pltpu.VMEM((2 * deep * count, 128), F32),
            pltpu.SemaphoreType.DMA((5,)),
        ),
        outs=(pl.BlockSpec(memory_space=pltpu.HBM),) * 4,
        name="unpack",
    )
    g1 = jnp.transpose(g1.reshape(3, 3, 3, 4, 32), (4, 3, 0, 1, 2))
    g2 = jnp.transpose(g2.reshape(3, 3, 3, 32, 64), (4, 3, 0, 1, 2))
    return g1, b1[0], g2, b2[0]


def solution(mesh):
    grid_z = mesh.shape["space"] // GY
    placed = (P("space"),) * 3 + (P(),) * 4

    return jax.shard_map(
        functools.partial(on_device, grid_z),
        mesh=mesh,
        in_specs=placed,
        out_specs=(P(),) * 4,
        check_vma=False,
    )
```

```python
import functools

import jax
import jax.numpy as jnp
import numpy as np
from jax import lax
from jax.experimental import pallas as pl
from jax.experimental.pallas import tpu as pltpu
from jax.sharding import PartitionSpec as P

GY = 8
BF = jnp.bfloat16
F32 = jnp.float32
LOW = np.float32(0.3) * np.float32(0.125)
PATCH = 432
VMEM = pl.BlockSpec(memory_space=pltpu.VMEM)


def pairs_of(count, stride, kind):
    size, cells = count
    out = []
    for i in range(size):
        p = (i // stride) % cells
        q = p ^ 1 if kind == 0 else (p + 1 if p % 2 else p - 1)
        if 0 <= q < cells:
            out.append((i, i + (q - p) * stride))
    return out


def place_of(flat):
    own = flat < 288
    block = jnp.where(
        own, lax.shift_right_logical(flat, 5), lax.shift_right_logical(flat - 288, 4)
    )
    r = flat & 31
    h = flat & 15
    chan = jnp.where(own, lax.shift_right_logical(r, 3), h & 3)
    rim = jnp.where(h < 4, 0, jnp.where(h < 8, 9, -100))
    return block, chan, jnp.where(own, (r & 7) + 1, rim)


def shifts(block):
    wide = block.astype(F32)
    size = wide.shape[1]
    lane = lax.broadcasted_iota(jnp.int32, wide.shape, 1)
    before = jnp.where(lane == 0, 0.0, pltpu.roll(wide, 1, 1)).astype(BF)
    after = jnp.where(lane == size - 1, 0.0, pltpu.roll(wide, size - 1, 1)).astype(BF)
    return before, block, after


def doubler(size):
    row = lax.broadcasted_iota(jnp.int32, (size, 2 * size), 0)
    col = lax.broadcasted_iota(jnp.int32, (size, 2 * size), 1)
    return jnp.where(lax.shift_right_logical(col, 1) == row, 1.0, 0.0).astype(BF)


def dot(a, b):
    return jnp.dot(a, b, preferred_element_type=F32)


def dot_nt(a, b):
    return lax.dot_general(a, b, (((1,), (1,)), ((), ())), preferred_element_type=F32)


def y_parity(grid_z):
    return lax.rem(lax.div(lax.axis_index("space"), grid_z), 2)


def z_parity(grid_z):
    return lax.rem(lax.rem(lax.axis_index("space"), grid_z), 2)


def y_pack(grid_z, x1_ref, g2_ref, x0_ref, a_ref, b_ref):
    par = y_parity(grid_z)
    for ref, up in ((a_ref, 1 - par), (b_ref, par)):
        for p in range(2):
            for z in range(4):
                ref[(p * 4 + z) * 32 : (p * 4 + z + 1) * 32, :] = x1_ref[up * 2 + p, z]
        ref[256:320, :] = jnp.concatenate([g2_ref[up, 0], g2_ref[up, 1]], axis=1)
        for i in range(4):
            plane = x0_ref[i, up * 7]
            ref[320 + i * 8 : 328 + i * 8, :] = plane[:, :128]
            ref[352 + i * 8 : 360 + i * 8, :] = plane[:, 128:]


def fetch(*refs):
    mb = lax.axis_index("section")
    sources, targets, sems = refs[:3], refs[3:6], refs[6]
    copies = [
        pltpu.make_async_copy(source.at[0, mb], target, sems.at[k])
        for k, (source, target) in enumerate(zip(sources, targets))
    ]
    for copy in copies:
        copy.start()
    for copy in copies:
        copy.wait()


def z_pack(grid_z, x1_ref, g2_ref, x0_ref, ra_ref, rb_ref, x1r_ref, g2y_ref, x0r_ref, *sends):
    par = y_parity(grid_z)
    even = par == 0
    line = lax.div(lax.axis_index("space"), grid_z)
    inner = (line > 0) & (line < GY - 1)
    ra = ra_ref[...]
    rb = rb_ref[pl.ds(pl.multiple_of(par * 384, 384), 384), :]
    rb = jnp.where(inner, rb, jnp.zeros_like(rb))
    low = jnp.where(even, rb, ra)
    high = jnp.where(even, ra, rb)
    for side, rim in ((0, low), (1, high)):
        for p in range(2):
            for z in range(4):
                x1r_ref[side * 2 + p, z] = rim[(p * 4 + z) * 32 : (p * 4 + z + 1) * 32]
        for z in range(2):
            g2y_ref[side * 3, z] = rim[256:320, z * 64 : z * 64 + 64]
        x0r_ref[side, :, :128] = rim[320:352]
        x0r_ref[side, :, 128:] = rim[352:384]
    g2y_ref[1:3] = g2_ref[...]
    zpar = z_parity(grid_z)
    for k, send_ref in enumerate(sends):
        up = 1 - zpar if k == 0 else zpar
        for y in range(8):
            for p in range(2):
                if 2 <= y < 6:
                    plane = x1_ref[y - 2, up * 2 + p]
                else:
                    plane = x1r_ref[y if y < 2 else y - 4, up * 2 + p]
                send_ref[(y * 2 + p) * 32 : (y * 2 + p + 1) * 32, :] = plane
        for y in range(0, 4, 2):
            pair = jnp.concatenate([g2y_ref[y, up], g2y_ref[y + 1, up]], axis=1)
            send_ref[512 + y * 32 : 576 + y * 32, :] = pair
        row = lax.broadcasted_iota(jnp.int32, (16, 32), 0)
        col = lax.broadcasted_iota(jnp.int32, (16, 32), 1)
        take = jnp.where((col == row * 8 + up * 7) & (row < 4), 1.0, 0.0).astype(BF)
        for y in range(10):
            if 1 <= y < 9:
                block = jnp.concatenate([x0_ref[i, y - 1] for i in range(4)], axis=0)
            else:
                block = x0r_ref[0 if y == 0 else 1]
            plane = dot(take, block).astype(BF)
            send_ref[640 + y * 32 : 656 + y * 32, :] = plane[:, :128]
            send_ref[656 + y * 32 : 672 + y * 32, :] = plane[:, 128:]


def put_second(xs, y, z, block):
    for c, value in enumerate(shifts(block)):
        row = z * 96 + c * 32
        xs[row : row + 32, y * 128 : y * 128 + 128] = value


def put_first(x0s, y, rim, block):
    size = block.shape[0]
    for c, value in enumerate(shifts(block)):
        for a in range(3):
            if 0 <= y - a < 8:
                row = (288 if rim else 0) + (a * 3 + c) * size
                x0s[row : row + size, (y - a) * 256 : (y - a + 1) * 256] = value


def prep(
    x1_ref, x0_ref, x1r_ref, x0r_ref, w1_ref, b1_ref, w2_ref, b2_ref,
    xs, x0s, wb2, wd, wrim, pre_out, b2_out, wb0, w1f,
):
    for y in range(4):
        for z in range(4):
            put_second(xs, y + 2, z + 2, x1_ref[y, z])
    for y in range(8):
        block = jnp.concatenate([x0_ref[i, y] for i in range(4)], axis=0)
        put_first(x0s, y + 1, False, block)
    for k, y in enumerate((0, 1, 6, 7)):
        for z in range(4):
            put_second(xs, y, z + 2, x1r_ref[k, z])
    for k, y in enumerate((0, 9)):
        put_first(x0s, y, False, x0r_ref[k])
    wb2[...] = jnp.zeros_like(wb2)
    wd[...] = jnp.zeros_like(wd)
    for a in range(3):
        w2t = jnp.transpose(w2_ref[a * 288 : a * 288 + 288, :].astype(F32)).astype(BF)
        for z in range(3):
            wb2[a, z * 64 : z * 64 + 64, z * 96 : z * 96 + 288] = w2t
        for b in range(3):
            for c in range(3):
                k = (2 - a) * 9 + (2 - b) * 3 + 2 - c
                value = w2_ref[k * 32 : k * 32 + 32]
                for z in range(4):
                    at = (z + b) * 192 + c * 64
                    wd[a, z * 32 : z * 32 + 32, at : at + 64] = value
    b2_out[...] = jnp.transpose(jnp.broadcast_to(b2_ref[...], (128, 64)))
    b1c = jnp.transpose(jnp.broadcast_to(b1_ref[...], (128, 32)))
    w1f[108:112, :] = jnp.zeros((4, 32), F32)
    for k in range(27):
        w1f[k * 4 : k * 4 + 4, :] = w1_ref[k].astype(F32)
    w1t = jnp.transpose(w1f[...]).astype(BF)
    block, chan, plane = place_of(lax.broadcasted_iota(jnp.int32, (112, PATCH), 1))
    row = lax.broadcasted_iota(jnp.int32, (112, PATCH), 0)
    third = lax.shift_right_logical(block * 11, 5)
    home = jnp.where(plane >= 0, third * 24 + block * 4 + chan, -100)
    spread = [dot(w1t, jnp.where(row == home + b * 12, 1.0, 0.0).astype(BF)) for b in range(3)]
    zrow = place_of(lax.broadcasted_iota(jnp.int32, (32, PATCH), 1))[2]
    for z in range(8):
        value = jnp.zeros((32, PATCH), F32)
        for b in range(3):
            value = jnp.where(zrow == z + b, spread[b], value)
        wb0[z * 32 : z * 32 + 32, :] = value[:, :288].astype(BF)
        if z in (0, 7):
            wrim[z // 7 * 32 : z // 7 * 32 + 32, :] = value[:, 288:].astype(BF)
    b1w = jnp.concatenate([jnp.concatenate([b1c, b1c], axis=1)] * 8, axis=0)
    for y in range(8):
        lanes = slice(y * 256, y * 256 + 256)
        pre_out[:, lanes] = dot(wb0[...], x0s[:288, lanes]) + b1w


def rims_of(grid_z, got):
    even = z_parity(grid_z) == 0

    def rims(start, size):
        one = got[0][start : start + size]
        two = got[1][start : start + size] if len(got) == 2 else jnp.zeros_like(one)
        return jnp.where(even, two, one), jnp.where(even, one, two)

    return rims


def second_grads(grid_z, kinds, *refs):
    xs_in, wb2, b2_ref, g2y_ref = refs[:4]
    rims = rims_of(grid_z, refs[4 : 4 + kinds])
    xs, ds, keep_ref, send_ref, bias_ref, dz1 = refs[4 + kinds :]

    for y in range(8):
        for p in range(2):
            low, high = rims((y * 2 + p) * 32, 32)
            put_second(xs, y, p, low)
            put_second(xs, y, 6 + p, high)

    twice = doubler(64)
    coarse = []
    rim = [rims(512 + y * 64, 64) for y in range(2)]
    for z in range(4):
        plane = []
        for y in range(4):
            if z in (0, 3):
                plane.append(rim[y // 2][z // 3][:, (y % 2) * 64 : (y % 2) * 64 + 64])
            else:
                plane.append(g2y_ref[y, z - 1])
        coarse.append(dot(jnp.concatenate(plane, axis=0), twice))
    b2c = b2_ref[...]
    for part in range(3):
        for group in range(2):
            rows = slice(group * 288, group * 288 + 480)
            pre = dot(wb2[0], xs[rows, part * 256 : part * 256 + 256])
            pre += dot(wb2[1], xs[rows, part * 256 + 128 : part * 256 + 384])
            pre += dot(wb2[2], xs[rows, part * 256 + 256 : part * 256 + 512])
            for y in (2 * part, 2 * part + 1):
                at = (y + 1) // 2 * 64
                for k in range(3):
                    z = group * 3 + k
                    grad = coarse[(z + 1) // 2][at : at + 64]
                    here = pre[k * 64 : k * 64 + 64, (y % 2) * 128 : (y % 2) * 128 + 128] + b2c
                    delta = (grad * jnp.where(here > 0, 0.125, LOW)).astype(BF)
                    dz1[z * 64 : z * 64 + 64, y * 128 : y * 128 + 128] = delta
                    for c, value in enumerate(shifts(delta)):
                        row = z * 192 + c * 64
                        ds[row : row + 64, y * 128 : y * 128 + 128] = value

    own = dz1[64:320, 128:640]
    line = dot_nt(jnp.ones((8, 512), BF), own)
    bias_ref[...] = sum(line[:, z * 64 : z * 64 + 64] for z in range(4))
    parts = []
    first = lax.broadcasted_iota(jnp.int32, (288, 128), 1) < 64
    for a in range(3):
        lanes = slice((a + 1) * 128, (a + 5) * 128)
        full = dot_nt(xs[96:480, lanes], own[:128])
        full += dot_nt(xs[288:672, lanes], own[128:])
        flip = pltpu.roll(full, 64, 1)
        parts.append(jnp.where(first, full[:288] + flip[96:], flip[:288] + full[96:]))
    even = z_parity(grid_z) == 0
    first = first[:216]
    low = jnp.where(
        first, parts[0][:216], jnp.concatenate([parts[0][216:], parts[1][:144]], axis=0)
    )
    high = jnp.where(
        first, jnp.concatenate([parts[1][144:], parts[2][:72]], axis=0), parts[2][72:]
    )
    keep_ref[...] = jnp.where(even, low, high)
    send_ref[...] = jnp.where(even, high, low)


def first_grads(grid_z, kinds, *refs):
    x0s_in, ds, wd, wrim, pre_ref = refs[:5]
    rims = rims_of(grid_z, refs[5 : 5 + kinds])
    x0s, out_ref, line_ref, dz0, up = refs[5 + kinds :]

    back = dot(wd[0], ds[:, :512])
    back += dot(wd[1], ds[:, 128:640])
    back += dot(wd[2], ds[:, 256:768])
    back = back.astype(BF)
    stack = [back[:, y * 128 : y * 128 + 128] for y in range(4)]
    up[...] = dot(jnp.concatenate(stack, axis=0), doubler(128))

    ones = jnp.where(lax.broadcasted_iota(jnp.int32, (8, 256), 0) == 0, 1.0, 0.0)
    for y in range(10):
        halves = [rims(640 + y * 32 + h * 16, 16) for h in range(2)]
        low, high = (jnp.concatenate([h[k] for h in halves], axis=1) for k in range(2))
        pair = jnp.concatenate([low[:4].astype(F32), high[:4].astype(F32)], axis=0)
        put_first(x0s, y, True, jnp.concatenate([pair, ones], axis=0).astype(BF))

    for y in range(8):
        lanes = slice(y * 256, y * 256 + 256)
        more = dot(wrim[...], x0s[288:, lanes])
        for z in range(8):
            at = (y // 2) * 128 + (z // 2) * 32
            here = pre_ref[z * 32 : z * 32 + 32, lanes]
            if z in (0, 7):
                here += more[z // 7 * 32 : z // 7 * 32 + 32]
            delta = up[at : at + 32, :] * jnp.where(here > 0, 0.125, LOW)
            dz0[z * 32 : z * 32 + 32, lanes] = delta.astype(BF)

    full = dot_nt(x0s[...], dz0[...])
    row = lax.broadcasted_iota(jnp.int32, (8, 256), 0)
    lane = lax.shift_right_logical(lax.broadcasted_iota(jnp.int32, (8, 256), 1), 5)
    band = (lane >= row - 1) & (lane <= row + 1)
    ends = jnp.where(row < 4, 0, 7) == lane
    odd = (row[:, :128] & 1) == 1
    upper = (row[:, :128] & 2) == 2
    out_ref[36:, :] = jnp.zeros((4, 128), F32)
    for block in range(9):
        edge = jnp.where(ends, full[288 + block * 16 : 296 + block * 16], 0.0)
        edge = edge[:, :128] + edge[:, 128:]
        edge = pltpu.roll(edge[:4], 32, 1) + edge[4:]
        for i in range(4):
            part = jnp.where(band, full[block * 32 + i * 8 : block * 32 + i * 8 + 8], 0.0)
            part = part[:, :128] + part[:, 128:]
            part = jnp.where(odd, pltpu.roll(part, 96, 1), part)
            part = jnp.where(upper, pltpu.roll(part, 64, 1), part)
            part = jnp.sum(part, axis=0, keepdims=True) + edge[i : i + 1]
            out_ref[block * 4 + i : block * 4 + i + 1, :] = part
    line = full[360:368]
    line_ref[...] = sum(line[:, z * 32 : z * 32 + 32] for z in range(8))


def pack_grads(count, deep, keep_ref, got_ref, bias_two_ref, part_ref, bias_one_ref, out_ref, flat):
    flat[...] = jnp.zeros_like(flat)
    flat[:216, :] = keep_ref[...] + got_ref[...]
    at = (deep - 1) * count
    for b, lane in enumerate((32, 0, 96)):
        flat[at : at + 27, b * 32 : b * 32 + 32] = part_ref[:27, lane : lane + 32]
        flat[at + b * 9 : at + b * 9 + 9, 96:] = part_ref[27:36, lane : lane + 32]
    flat[at + 27 : at + 28, :64] = bias_two_ref[:1, :]
    flat[at + 27 : at + 28, 64:96] = bias_one_ref[:1, :]
    for k in range(deep):
        out_ref[:, k, :] = flat[k * count : (k + 1) * count, :]


def sum_parts(count, deep, parts_ref, out_ref):
    sums = [parts_ref[0], parts_ref[1]]
    for k in range(1, count // 2):
        sums[0] += parts_ref[2 * k]
        sums[1] += parts_ref[2 * k + 1]
    row = lax.broadcasted_iota(jnp.int32, (deep, 128), 0)
    sums[0] += jnp.where(row == deep - 1, sums[1], 0.0)
    for k in range(count):
        out_ref[k, 0] = sums[0].astype(BF)
        out_ref[k, 1] = sums[1].astype(BF)


def unpack(count, deep, sum_ref, *refs):
    outs, (g1_ref, b1_ref, g2_ref, b2_ref, flat, sems) = refs[:4], refs[4:]
    flat[:count, :] = sum_ref[:, 0, deep - 1, :].astype(F32)
    for a in range(3):
        for b in range(3):
            for c in range(3):
                row = (a * 3 + c) * 4
                for i in range(4):
                    r = row + i
                    if r < 27:
                        value = flat[r : r + 1, b * 32 : b * 32 + 32]
                    else:
                        value = flat[b * 9 + r - 27 : b * 9 + r - 26, 96:]
                    g1_ref[a * 9 + b * 3 + c, i : i + 1] = value
    b2_ref[...] = flat[27:28, :64]
    b1_ref[...] = flat[27:28, 64:96]
    copies = [
        pltpu.make_async_copy(g1_ref, outs[0], sems.at[0]),
        pltpu.make_async_copy(b1_ref, outs[1], sems.at[1]),
        pltpu.make_async_copy(b2_ref, outs[3], sems.at[2]),
    ]
    for copy in copies:
        copy.start()
    for half in range(2):
        for k in range(deep - 1):
            at = (half * deep + k) * count
            flat[at : at + count, :] = sum_ref[:, half, k, :].astype(F32)
        at = half * deep * count
        g2_ref[half * 432 : half * 432 + 216, :] = flat[at : at + 216, :64]
        g2_ref[half * 432 + 216 : half * 432 + 432, :] = flat[at : at + 216, 64:]
        rows = slice(half * 432, half * 432 + 432)
        copies.append(pltpu.make_async_copy(g2_ref.at[rows], outs[2].at[rows], sems.at[3 + half]))
        copies[-1].start()
    for copy in copies:
        copy.wait()


def call(kernel, out, inputs, scratch=(), name=None, room=8, specs=None, outs=None, alias=None, flags=None):
    return pl.pallas_call(
        kernel,
        out_shape=out,
        in_specs=specs or [VMEM] * len(inputs),
        out_specs=outs or jax.tree.map(lambda _: VMEM, out),
        scratch_shapes=list(scratch),
        input_output_aliases=alias or {},
        name=name,
        compiler_params=pltpu.CompilerParams(vmem_limit_bytes=room << 20, flags=flags),
    )(*inputs)


def shaped(*shape, dtype=BF):
    return jax.ShapeDtypeStruct(shape, dtype)


def on_device(grid_z, x0, x1, g2, kernel_one, bias_one, kernel_two, bias_two):
    size = lax.axis_size("space")
    w1 = jnp.transpose(kernel_one, (2, 3, 4, 1, 0)).reshape(27, 4, 32)
    w2 = jnp.transpose(kernel_two, (2, 3, 4, 1, 0)).reshape(864, 64)
    x0, x1, g2 = call(
        fetch,
        (shaped(4, 8, 8, 256), shaped(32, 4, 4, 128), shaped(64, 2, 2, 64)),
        tuple(pltpu.with_memory_space_constraint(v, pltpu.HBM) for v in (x0, x1, g2)),
        scratch=(pltpu.SemaphoreType.DMA((3,)),),
        specs=[pl.BlockSpec(memory_space=pltpu.HBM)] * 3,
        name="fetch",
    )
    x1 = jnp.transpose(x1, (1, 2, 0, 3))
    g2 = jnp.transpose(g2, (1, 2, 0, 3))

    send = call(
        functools.partial(y_pack, grid_z), (shaped(384, 128),) * 2, (x1, g2, x0), name="y_pack"
    )
    inner = [
        [y * grid_z + z, (y + 1) * grid_z + z] for y in range(1, GY - 2, 2) for z in range(grid_z)
    ]
    ends = [[y * grid_z + z, y * grid_z + z + 1] for y in (0, GY - 1) for z in range(0, grid_z, 2)]
    got = [
        lax.ppermute(send[0], "space", pairs_of((size, GY), grid_z, 0)),
        lax.all_gather(send[1], "space", axis_index_groups=inner + ends, tiled=True),
    ]
    kinds = 1 if grid_z == 2 else 2
    sends = (shaped(960, 128),) * kinds
    wide = call(
        functools.partial(z_pack, grid_z),
        (shaped(4, 4, 32, 128), shaped(4, 2, 64, 64), shaped(2, 32, 256)) + sends,
        (x1, g2, x0, *got),
        name="z_pack",
    )
    rims = [
        lax.ppermute(v, "space", pairs_of((size, grid_z), 1, k))
        for k, v in enumerate(wide[3:])
    ]
    xs, x0s, wb2, wd, wrim, pre, b2 = call(
        prep,
        (
            shaped(768, 1024),
            shaped(PATCH, 2048),
            shaped(3, 192, 480),
            shaped(3, 128, 1152),
            shaped(64, 144),
            shaped(256, 2048, dtype=F32),
            shaped(64, 128, dtype=F32),
        ),
        (x1, x0, wide[0], wide[2], w1, bias_one[None], w2, bias_two[None]),
        scratch=(pltpu.VMEM((256, 288), BF), pltpu.VMEM((112, 32), F32)),
        name="prep",
    )
    xs, ds, keep, swap, line_two = call(
        functools.partial(second_grads, grid_z, kinds),
        (
            shaped(768, 1024),
            shaped(1152, 768),
            shaped(216, 128, dtype=F32),
            shaped(216, 128, dtype=F32),
            shaped(8, 64, dtype=F32),
        ),
        (xs, wb2, b2, wide[1], *rims),
        scratch=(pltpu.VMEM((384, 768), BF),),
        alias={0: 0},
        name="second_grads",
    )
    swap = lax.ppermute(swap, "space", [(k, k ^ 1) for k in range(size)])
    x0s, part_one, line_one = call(
        functools.partial(first_grads, grid_z, kinds),
        (shaped(PATCH, 2048), shaped(40, 128, dtype=F32), shaped(8, 32, dtype=F32)),
        (x0s, ds, wd, wrim, pre, *rims),
        scratch=(pltpu.VMEM((256, 2048), BF), pltpu.VMEM((512, 256), F32)),
        alias={0: 0},
        name="first_grads",
    )
    axes = ("section", "space")
    count = lax.axis_size(axes)
    deep = -(-216 // count) + 1
    shape = shaped(count, deep, 128, dtype=F32)
    lines = (pltpu.VMEM((deep * count, 128), F32),)
    packed = call(
        functools.partial(pack_grads, count, deep),
        shape,
        (keep, swap, line_two, part_one, line_one),
        scratch=lines,
        name="pack_grads",
    )
    parts = lax.all_to_all(packed, axes, 0, 0, tiled=True)
    mine = call(
        functools.partial(sum_parts, count, deep),
        shaped(count, 2, deep, 128),
        (parts,),
        name="sum_parts",
    )
    total = lax.all_to_all(mine, axes, 0, 0, tiled=True)
    g1, b1, g2, b2 = call(
        functools.partial(unpack, count, deep),
        (
            shaped(27, 4, 32, dtype=F32),
            shaped(1, 32, dtype=F32),
            shaped(864, 64, dtype=F32),
            shaped(1, 64, dtype=F32),
        ),
        (total,),
        scratch=(
            pltpu.VMEM((27, 4, 32), F32),
            pltpu.VMEM((1, 32), F32),
            pltpu.VMEM((864, 64), F32),
            pltpu.VMEM((1, 64), F32),
            pltpu.VMEM((2 * deep * count, 128), F32),
            pltpu.SemaphoreType.DMA((5,)),
        ),
        outs=(pl.BlockSpec(memory_space=pltpu.HBM),) * 4,
        name="unpack",
    )
    g1 = jnp.transpose(g1.reshape(3, 3, 3, 4, 32), (4, 3, 0, 1, 2))
    g2 = jnp.transpose(g2.reshape(3, 3, 3, 32, 64), (4, 3, 0, 1, 2))
    return g1, b1[0], g2, b2[0]


def solution(mesh):
    grid_z = mesh.shape["space"] // GY
    placed = (P("space"),) * 3 + (P(),) * 4

    return jax.shard_map(
        functools.partial(on_device, grid_z),
        mesh=mesh,
        in_specs=placed,
        out_specs=(P(),) * 4,
        check_vma=False,
    )
```

```python
import functools

import jax
import jax.numpy as jnp
import numpy as np
from jax import lax
from jax.experimental import pallas as pl
from jax.experimental.pallas import tpu as pltpu
from jax.sharding import PartitionSpec as P

GY = 8
BF = jnp.bfloat16
F32 = jnp.float32
LOW = np.float32(0.3) * np.float32(0.125)
PATCH = 432
VMEM = pl.BlockSpec(memory_space=pltpu.VMEM)


def pairs_of(count, stride, kind):
    size, cells = count
    out = []
    for i in range(size):
        p = (i // stride) % cells
        q = p ^ 1 if kind == 0 else (p + 1 if p % 2 else p - 1)
        if 0 <= q < cells:
            out.append((i, i + (q - p) * stride))
    return out


def place_of(flat):
    own = flat < 288
    block = jnp.where(
        own, lax.shift_right_logical(flat, 5), lax.shift_right_logical(flat - 288, 4)
    )
    r = flat & 31
    h = flat & 15
    chan = jnp.where(own, lax.shift_right_logical(r, 3), h & 3)
    rim = jnp.where(h < 4, 0, jnp.where(h < 8, 9, -100))
    return block, chan, jnp.where(own, (r & 7) + 1, rim)


def shifts(block):
    wide = block.astype(F32)
    size = wide.shape[1]
    lane = lax.broadcasted_iota(jnp.int32, wide.shape, 1)
    before = jnp.where(lane == 0, 0.0, pltpu.roll(wide, 1, 1)).astype(BF)
    after = jnp.where(lane == size - 1, 0.0, pltpu.roll(wide, size - 1, 1)).astype(BF)
    return before, block, after


def doubler(size):
    row = lax.broadcasted_iota(jnp.int32, (size, 2 * size), 0)
    col = lax.broadcasted_iota(jnp.int32, (size, 2 * size), 1)
    return jnp.where(lax.shift_right_logical(col, 1) == row, 1.0, 0.0).astype(BF)


def dot(a, b):
    return jnp.dot(a, b, preferred_element_type=F32)


def dot_nt(a, b):
    return lax.dot_general(a, b, (((1,), (1,)), ((), ())), preferred_element_type=F32)


def y_parity(grid_z):
    return lax.rem(lax.div(lax.axis_index("space"), grid_z), 2)


def z_parity(grid_z):
    return lax.rem(lax.rem(lax.axis_index("space"), grid_z), 2)


def y_pack(grid_z, x1_ref, g2_ref, x0_ref, a_ref, b_ref):
    par = y_parity(grid_z)
    for ref, up in ((a_ref, 1 - par), (b_ref, par)):
        for p in range(2):
            for z in range(4):
                ref[(p * 4 + z) * 32 : (p * 4 + z + 1) * 32, :] = x1_ref[up * 2 + p, z]
        ref[256:320, :] = jnp.concatenate([g2_ref[up, 0], g2_ref[up, 1]], axis=1)
        for i in range(4):
            plane = x0_ref[i, up * 7]
            ref[320 + i * 8 : 328 + i * 8, :] = plane[:, :128]
            ref[352 + i * 8 : 360 + i * 8, :] = plane[:, 128:]


def fetch(*refs):
    mb = lax.axis_index("section")
    sources, targets, sems = refs[:3], refs[3:6], refs[6]
    copies = [
        pltpu.make_async_copy(source.at[0, mb], target, sems.at[k])
        for k, (source, target) in enumerate(zip(sources, targets))
    ]
    for copy in copies:
        copy.start()
    for copy in copies:
        copy.wait()


def z_pack(grid_z, x1_ref, g2_ref, x0_ref, ra_ref, rb_ref, x1r_ref, g2y_ref, x0r_ref, *sends):
    par = y_parity(grid_z)
    even = par == 0
    line = lax.div(lax.axis_index("space"), grid_z)
    inner = (line > 0) & (line < GY - 1)
    ra = ra_ref[...]
    rb = rb_ref[pl.ds(pl.multiple_of(par * 384, 384), 384), :]
    rb = jnp.where(inner, rb, jnp.zeros_like(rb))
    low = jnp.where(even, rb, ra)
    high = jnp.where(even, ra, rb)
    for side, rim in ((0, low), (1, high)):
        for p in range(2):
            for z in range(4):
                x1r_ref[side * 2 + p, z] = rim[(p * 4 + z) * 32 : (p * 4 + z + 1) * 32]
        for z in range(2):
            g2y_ref[side * 3, z] = rim[256:320, z * 64 : z * 64 + 64]
        x0r_ref[side, :, :128] = rim[320:352]
        x0r_ref[side, :, 128:] = rim[352:384]
    g2y_ref[1:3] = g2_ref[...]
    zpar = z_parity(grid_z)
    for k, send_ref in enumerate(sends):
        up = 1 - zpar if k == 0 else zpar
        for y in range(8):
            for p in range(2):
                if 2 <= y < 6:
                    plane = x1_ref[y - 2, up * 2 + p]
                else:
                    plane = x1r_ref[y if y < 2 else y - 4, up * 2 + p]
                send_ref[(y * 2 + p) * 32 : (y * 2 + p + 1) * 32, :] = plane
        for y in range(0, 4, 2):
            pair = jnp.concatenate([g2y_ref[y, up], g2y_ref[y + 1, up]], axis=1)
            send_ref[512 + y * 32 : 576 + y * 32, :] = pair
        row = lax.broadcasted_iota(jnp.int32, (16, 32), 0)
        col = lax.broadcasted_iota(jnp.int32, (16, 32), 1)
        take = jnp.where((col == row * 8 + up * 7) & (row < 4), 1.0, 0.0).astype(BF)
        for y in range(10):
            if 1 <= y < 9:
                block = jnp.concatenate([x0_ref[i, y - 1] for i in range(4)], axis=0)
            else:
                block = x0r_ref[0 if y == 0 else 1]
            plane = dot(take, block).astype(BF)
            send_ref[640 + y * 32 : 656 + y * 32, :] = plane[:, :128]
            send_ref[656 + y * 32 : 672 + y * 32, :] = plane[:, 128:]


def put_second(xs, y, z, block):
    for c, value in enumerate(shifts(block)):
        row = z * 96 + c * 32
        xs[row : row + 32, y * 128 : y * 128 + 128] = value


def put_first(x0s, y, rim, block):
    size = block.shape[0]
    for c, value in enumerate(shifts(block)):
        for a in range(3):
            if 0 <= y - a < 8:
                row = (288 if rim else 0) + (a * 3 + c) * size
                x0s[row : row + size, (y - a) * 256 : (y - a + 1) * 256] = value


def prep(
    x1_ref, x0_ref, x1r_ref, x0r_ref, w1_ref, b1_ref, w2_ref, b2_ref,
    xs, x0s, wb2, wd, wrim, pre_out, b2_out, wb0, w1f,
):
    for y in range(4):
        for z in range(4):
            put_second(xs, y + 2, z + 2, x1_ref[y, z])
    for y in range(8):
        block = jnp.concatenate([x0_ref[i, y] for i in range(4)], axis=0)
        put_first(x0s, y + 1, False, block)
    for k, y in enumerate((0, 1, 6, 7)):
        for z in range(4):
            put_second(xs, y, z + 2, x1r_ref[k, z])
    for k, y in enumerate((0, 9)):
        put_first(x0s, y, False, x0r_ref[k])
    wb2[...] = jnp.zeros_like(wb2)
    wd[...] = jnp.zeros_like(wd)
    for a in range(3):
        w2t = jnp.transpose(w2_ref[a * 288 : a * 288 + 288, :].astype(F32)).astype(BF)
        for z in range(3):
            wb2[a, z * 64 : z * 64 + 64, z * 96 : z * 96 + 288] = w2t
        for b in range(3):
            for c in range(3):
                k = (2 - a) * 9 + (2 - b) * 3 + 2 - c
                value = w2_ref[k * 32 : k * 32 + 32]
                for z in range(4):
                    at = (z + b) * 192 + c * 64
                    wd[a, z * 32 : z * 32 + 32, at : at + 64] = value
    b2_out[...] = jnp.transpose(jnp.broadcast_to(b2_ref[...], (128, 64)))
    b1c = jnp.transpose(jnp.broadcast_to(b1_ref[...], (128, 32)))
    w1f[108:112, :] = jnp.zeros((4, 32), F32)
    for k in range(27):
        w1f[k * 4 : k * 4 + 4, :] = w1_ref[k].astype(F32)
    w1t = jnp.transpose(w1f[...]).astype(BF)
    block, chan, plane = place_of(lax.broadcasted_iota(jnp.int32, (112, PATCH), 1))
    row = lax.broadcasted_iota(jnp.int32, (112, PATCH), 0)
    third = lax.shift_right_logical(block * 11, 5)
    home = jnp.where(plane >= 0, third * 24 + block * 4 + chan, -100)
    spread = [dot(w1t, jnp.where(row == home + b * 12, 1.0, 0.0).astype(BF)) for b in range(3)]
    zrow = place_of(lax.broadcasted_iota(jnp.int32, (32, PATCH), 1))[2]
    for z in range(8):
        value = jnp.zeros((32, PATCH), F32)
        for b in range(3):
            value = jnp.where(zrow == z + b, spread[b], value)
        wb0[z * 32 : z * 32 + 32, :] = value[:, :288].astype(BF)
        if z in (0, 7):
            wrim[z // 7 * 32 : z // 7 * 32 + 32, :] = value[:, 288:].astype(BF)
    b1w = jnp.concatenate([jnp.concatenate([b1c, b1c], axis=1)] * 8, axis=0)
    for y in range(8):
        lanes = slice(y * 256, y * 256 + 256)
        pre_out[:, lanes] = dot(wb0[...], x0s[:288, lanes]) + b1w


def rims_of(grid_z, got):
    even = z_parity(grid_z) == 0

    def rims(start, size):
        one = got[0][start : start + size]
        two = got[1][start : start + size] if len(got) == 2 else jnp.zeros_like(one)
        return jnp.where(even, two, one), jnp.where(even, one, two)

    return rims


def second_grads(grid_z, kinds, *refs):
    xs_in, wb2, b2_ref, g2y_ref = refs[:4]
    rims = rims_of(grid_z, refs[4 : 4 + kinds])
    xs, ds, keep_ref, send_ref, bias_ref, dz1 = refs[4 + kinds :]

    for y in range(8):
        for p in range(2):
            low, high = rims((y * 2 + p) * 32, 32)
            put_second(xs, y, p, low)
            put_second(xs, y, 6 + p, high)

    twice = doubler(64)
    coarse = []
    rim = [rims(512 + y * 64, 64) for y in range(2)]
    for z in range(4):
        plane = []
        for y in range(4):
            if z in (0, 3):
                plane.append(rim[y // 2][z // 3][:, (y % 2) * 64 : (y % 2) * 64 + 64])
            else:
                plane.append(g2y_ref[y, z - 1])
        coarse.append(dot(jnp.concatenate(plane, axis=0), twice))
    b2c = b2_ref[...]
    for part in range(3):
        for group in range(2):
            rows = slice(group * 288, group * 288 + 480)
            pre = dot(wb2[0], xs[rows, part * 256 : part * 256 + 256])
            pre += dot(wb2[1], xs[rows, part * 256 + 128 : part * 256 + 384])
            pre += dot(wb2[2], xs[rows, part * 256 + 256 : part * 256 + 512])
            for y in (2 * part, 2 * part + 1):
                at = (y + 1) // 2 * 64
                for k in range(3):
                    z = group * 3 + k
                    grad = coarse[(z + 1) // 2][at : at + 64]
                    here = pre[k * 64 : k * 64 + 64, (y % 2) * 128 : (y % 2) * 128 + 128] + b2c
                    delta = (grad * jnp.where(here > 0, 0.125, LOW)).astype(BF)
                    dz1[z * 64 : z * 64 + 64, y * 128 : y * 128 + 128] = delta
                    for c, value in enumerate(shifts(delta)):
                        row = z * 192 + c * 64
                        ds[row : row + 64, y * 128 : y * 128 + 128] = value

    own = dz1[64:320, 128:640]
    line = dot_nt(jnp.ones((8, 512), BF), own)
    bias_ref[...] = sum(line[:, z * 64 : z * 64 + 64] for z in range(4))
    parts = []
    first = lax.broadcasted_iota(jnp.int32, (288, 128), 1) < 64
    for a in range(3):
        lanes = slice((a + 1) * 128, (a + 5) * 128)
        full = dot_nt(xs[96:480, lanes], own[:128])
        full += dot_nt(xs[288:672, lanes], own[128:])
        flip = pltpu.roll(full, 64, 1)
        parts.append(jnp.where(first, full[:288] + flip[96:], flip[:288] + full[96:]))
    even = z_parity(grid_z) == 0
    first = first[:216]
    low = jnp.where(
        first, parts[0][:216], jnp.concatenate([parts[0][216:], parts[1][:144]], axis=0)
    )
    high = jnp.where(
        first, jnp.concatenate([parts[1][144:], parts[2][:72]], axis=0), parts[2][72:]
    )
    keep_ref[...] = jnp.where(even, low, high)
    send_ref[...] = jnp.where(even, high, low)


def first_grads(grid_z, kinds, *refs):
    x0s_in, ds, wd, wrim, pre_ref = refs[:5]
    rims = rims_of(grid_z, refs[5 : 5 + kinds])
    x0s, out_ref, line_ref, dz0, up = refs[5 + kinds :]

    back = dot(wd[0], ds[:, :512])
    back += dot(wd[1], ds[:, 128:640])
    back += dot(wd[2], ds[:, 256:768])
    back = back.astype(BF)
    stack = [back[:, y * 128 : y * 128 + 128] for y in range(4)]
    up[...] = dot(jnp.concatenate(stack, axis=0), doubler(128))

    ones = jnp.where(lax.broadcasted_iota(jnp.int32, (8, 256), 0) == 0, 1.0, 0.0)
    for y in range(10):
        halves = [rims(640 + y * 32 + h * 16, 16) for h in range(2)]
        low, high = (jnp.concatenate([h[k] for h in halves], axis=1) for k in range(2))
        pair = jnp.concatenate([low[:4].astype(F32), high[:4].astype(F32)], axis=0)
        put_first(x0s, y, True, jnp.concatenate([pair, ones], axis=0).astype(BF))

    for y in range(8):
        lanes = slice(y * 256, y * 256 + 256)
        more = dot(wrim[...], x0s[288:, lanes])
        for z in range(8):
            at = (y // 2) * 128 + (z // 2) * 32
            here = pre_ref[z * 32 : z * 32 + 32, lanes]
            if z in (0, 7):
                here += more[z // 7 * 32 : z // 7 * 32 + 32]
            delta = up[at : at + 32, :] * jnp.where(here > 0, 0.125, LOW)
            dz0[z * 32 : z * 32 + 32, lanes] = delta.astype(BF)

    full = dot_nt(x0s[...], dz0[...])
    row = lax.broadcasted_iota(jnp.int32, (8, 256), 0)
    lane = lax.shift_right_logical(lax.broadcasted_iota(jnp.int32, (8, 256), 1), 5)
    band = (lane >= row - 1) & (lane <= row + 1)
    ends = jnp.where(row < 4, 0, 7) == lane
    odd = (row[:, :128] & 1) == 1
    upper = (row[:, :128] & 2) == 2
    out_ref[36:, :] = jnp.zeros((4, 128), F32)
    for block in range(9):
        edge = jnp.where(ends, full[288 + block * 16 : 296 + block * 16], 0.0)
        edge = edge[:, :128] + edge[:, 128:]
        edge = pltpu.roll(edge[:4], 32, 1) + edge[4:]
        for i in range(4):
            part = jnp.where(band, full[block * 32 + i * 8 : block * 32 + i * 8 + 8], 0.0)
            part = part[:, :128] + part[:, 128:]
            part = jnp.where(odd, pltpu.roll(part, 96, 1), part)
            part = jnp.where(upper, pltpu.roll(part, 64, 1), part)
            part = jnp.sum(part, axis=0, keepdims=True) + edge[i : i + 1]
            out_ref[block * 4 + i : block * 4 + i + 1, :] = part
    line = full[360:368]
    line_ref[...] = sum(line[:, z * 32 : z * 32 + 32] for z in range(8))


def pack_grads(count, deep, keep_ref, got_ref, bias_two_ref, part_ref, bias_one_ref, out_ref, flat):
    flat[...] = jnp.zeros_like(flat)
    flat[:216, :] = keep_ref[...] + got_ref[...]
    at = (deep - 1) * count
    for b, lane in enumerate((32, 0, 96)):
        flat[at : at + 27, b * 32 : b * 32 + 32] = part_ref[:27, lane : lane + 32]
        flat[at + b * 9 : at + b * 9 + 9, 96:] = part_ref[27:36, lane : lane + 32]
    flat[at + 27 : at + 28, :64] = bias_two_ref[:1, :]
    flat[at + 27 : at + 28, 64:96] = bias_one_ref[:1, :]
    for k in range(deep):
        out_ref[:, k, :] = flat[k * count : (k + 1) * count, :]


def sum_parts(count, deep, parts_ref, out_ref):
    sums = [parts_ref[0], parts_ref[1]]
    for k in range(1, count // 2):
        sums[0] += parts_ref[2 * k]
        sums[1] += parts_ref[2 * k + 1]
    row = lax.broadcasted_iota(jnp.int32, (deep, 128), 0)
    last = row == deep - 1
    sums[0] += jnp.where(last, sums[1], 0.0)
    high = sums[0].astype(BF)
    low = jnp.where(last, sums[0] - high.astype(F32), sums[1]).astype(BF)
    for k in range(count):
        out_ref[k, 0] = high
        out_ref[k, 1] = low


def unpack(count, deep, sum_ref, *refs):
    outs, (g1_ref, b1_ref, g2_ref, b2_ref, flat, sems) = refs[:4], refs[4:]
    flat[:count, :] = sum_ref[:, 0, deep - 1, :].astype(F32) + sum_ref[
        :, 1, deep - 1, :
    ].astype(F32)
    for a in range(3):
        for b in range(3):
            for c in range(3):
                row = (a * 3 + c) * 4
                for i in range(4):
                    r = row + i
                    if r < 27:
                        value = flat[r : r + 1, b * 32 : b * 32 + 32]
                    else:
                        value = flat[b * 9 + r - 27 : b * 9 + r - 26, 96:]
                    g1_ref[a * 9 + b * 3 + c, i : i + 1] = value
    b2_ref[...] = flat[27:28, :64]
    b1_ref[...] = flat[27:28, 64:96]
    copies = [
        pltpu.make_async_copy(g1_ref, outs[0], sems.at[0]),
        pltpu.make_async_copy(b1_ref, outs[1], sems.at[1]),
        pltpu.make_async_copy(b2_ref, outs[3], sems.at[2]),
    ]
    for copy in copies:
        copy.start()
    for half in range(2):
        for k in range(deep - 1):
            at = (half * deep + k) * count
            flat[at : at + count, :] = sum_ref[:, half, k, :].astype(F32)
        at = half * deep * count
        g2_ref[half * 432 : half * 432 + 216, :] = flat[at : at + 216, :64]
        g2_ref[half * 432 + 216 : half * 432 + 432, :] = flat[at : at + 216, 64:]
        rows = slice(half * 432, half * 432 + 432)
        copies.append(pltpu.make_async_copy(g2_ref.at[rows], outs[2].at[rows], sems.at[3 + half]))
        copies[-1].start()
    for copy in copies:
        copy.wait()


def call(kernel, out, inputs, scratch=(), name=None, room=8, specs=None, outs=None, alias=None, flags=None):
    return pl.pallas_call(
        kernel,
        out_shape=out,
        in_specs=specs or [VMEM] * len(inputs),
        out_specs=outs or jax.tree.map(lambda _: VMEM, out),
        scratch_shapes=list(scratch),
        input_output_aliases=alias or {},
        name=name,
        compiler_params=pltpu.CompilerParams(vmem_limit_bytes=room << 20, flags=flags),
    )(*inputs)


def shaped(*shape, dtype=BF):
    return jax.ShapeDtypeStruct(shape, dtype)


def on_device(grid_z, x0, x1, g2, kernel_one, bias_one, kernel_two, bias_two):
    size = lax.axis_size("space")
    w1 = jnp.transpose(kernel_one, (2, 3, 4, 1, 0)).reshape(27, 4, 32)
    w2 = jnp.transpose(kernel_two, (2, 3, 4, 1, 0)).reshape(864, 64)
    x0, x1, g2 = call(
        fetch,
        (shaped(4, 8, 8, 256), shaped(32, 4, 4, 128), shaped(64, 2, 2, 64)),
        tuple(pltpu.with_memory_space_constraint(v, pltpu.HBM) for v in (x0, x1, g2)),
        scratch=(pltpu.SemaphoreType.DMA((3,)),),
        specs=[pl.BlockSpec(memory_space=pltpu.HBM)] * 3,
        name="fetch",
    )
    x1 = jnp.transpose(x1, (1, 2, 0, 3))
    g2 = jnp.transpose(g2, (1, 2, 0, 3))

    send = call(
        functools.partial(y_pack, grid_z), (shaped(384, 128),) * 2, (x1, g2, x0), name="y_pack"
    )
    inner = [
        [y * grid_z + z, (y + 1) * grid_z + z] for y in range(1, GY - 2, 2) for z in range(grid_z)
    ]
    ends = [[y * grid_z + z, y * grid_z + z + 1] for y in (0, GY - 1) for z in range(0, grid_z, 2)]
    got = [
        lax.ppermute(send[0], "space", pairs_of((size, GY), grid_z, 0)),
        lax.all_gather(send[1], "space", axis_index_groups=inner + ends, tiled=True),
    ]
    kinds = 1 if grid_z == 2 else 2
    sends = (shaped(960, 128),) * kinds
    wide = call(
        functools.partial(z_pack, grid_z),
        (shaped(4, 4, 32, 128), shaped(4, 2, 64, 64), shaped(2, 32, 256)) + sends,
        (x1, g2, x0, *got),
        name="z_pack",
    )
    rims = [
        lax.ppermute(v, "space", pairs_of((size, grid_z), 1, k))
        for k, v in enumerate(wide[3:])
    ]
    xs, x0s, wb2, wd, wrim, pre, b2 = call(
        prep,
        (
            shaped(768, 1024),
            shaped(PATCH, 2048),
            shaped(3, 192, 480),
            shaped(3, 128, 1152),
            shaped(64, 144),
            shaped(256, 2048, dtype=F32),
            shaped(64, 128, dtype=F32),
        ),
        (x1, x0, wide[0], wide[2], w1, bias_one[None], w2, bias_two[None]),
        scratch=(pltpu.VMEM((256, 288), BF), pltpu.VMEM((112, 32), F32)),
        name="prep",
    )
    xs, ds, keep, swap, line_two = call(
        functools.partial(second_grads, grid_z, kinds),
        (
            shaped(768, 1024),
            shaped(1152, 768),
            shaped(216, 128, dtype=F32),
            shaped(216, 128, dtype=F32),
            shaped(8, 64, dtype=F32),
        ),
        (xs, wb2, b2, wide[1], *rims),
        scratch=(pltpu.VMEM((384, 768), BF),),
        alias={0: 0},
        name="second_grads",
    )
    swap = lax.ppermute(swap, "space", [(k, k ^ 1) for k in range(size)])
    x0s, part_one, line_one = call(
        functools.partial(first_grads, grid_z, kinds),
        (shaped(PATCH, 2048), shaped(40, 128, dtype=F32), shaped(8, 32, dtype=F32)),
        (x0s, ds, wd, wrim, pre, *rims),
        scratch=(pltpu.VMEM((256, 2048), BF), pltpu.VMEM((512, 256), F32)),
        alias={0: 0},
        name="first_grads",
    )
    axes = ("section", "space")
    count = lax.axis_size(axes)
    deep = -(-216 // count) + 1
    shape = shaped(count, deep, 128, dtype=F32)
    lines = (pltpu.VMEM((deep * count, 128), F32),)
    packed = call(
        functools.partial(pack_grads, count, deep),
        shape,
        (keep, swap, line_two, part_one, line_one),
        scratch=lines,
        name="pack_grads",
    )
    parts = lax.all_to_all(packed, axes, 0, 0, tiled=True)
    mine = call(
        functools.partial(sum_parts, count, deep),
        shaped(count, 2, deep, 128),
        (parts,),
        name="sum_parts",
    )
    total = lax.all_to_all(mine, axes, 0, 0, tiled=True)
    g1, b1, g2, b2 = call(
        functools.partial(unpack, count, deep),
        (
            shaped(27, 4, 32, dtype=F32),
            shaped(1, 32, dtype=F32),
            shaped(864, 64, dtype=F32),
            shaped(1, 64, dtype=F32),
        ),
        (total,),
        scratch=(
            pltpu.VMEM((27, 4, 32), F32),
            pltpu.VMEM((1, 32), F32),
            pltpu.VMEM((864, 64), F32),
            pltpu.VMEM((1, 64), F32),
            pltpu.VMEM((2 * deep * count, 128), F32),
            pltpu.SemaphoreType.DMA((5,)),
        ),
        outs=(pl.BlockSpec(memory_space=pltpu.HBM),) * 4,
        name="unpack",
    )
    g1 = jnp.transpose(g1.reshape(3, 3, 3, 4, 32), (4, 3, 0, 1, 2))
    g2 = jnp.transpose(g2.reshape(3, 3, 3, 32, 64), (4, 3, 0, 1, 2))
    return g1, b1[0], g2, b2[0]


def solution(mesh):
    grid_z = mesh.shape["space"] // GY
    placed = (P("space"),) * 3 + (P(),) * 4

    return jax.shard_map(
        functools.partial(on_device, grid_z),
        mesh=mesh,
        in_specs=placed,
        out_specs=(P(),) * 4,
        check_vma=False,
    )
```
